128 devices in a mesh: req: 32 (over x, y, core), mlp: 4 (over z).
Axes of the slice: x: 4, y: 4, z: 4, core: 2. Of those that a mesh axis runs over, the one named last changes fastest.
Arguments:
- new_qkv: bfloat16 [1024, 3, 3072], P('req', None, 'mlp'), may hold values from -8 to 8
- prompt_cache: bfloat16 [32, 4096, 2, 3072], P('req', None, None, 'mlp'), may hold values from -6 to 6
- tail_cache: bfloat16 [512, 256, 2, 3072], P('req', None, None, 'mlp'), may hold values from -6 to 6
- residual: bfloat16 [1024, 3072], P('req', 'mlp'), may hold values from -6 to 6
- w_out: bfloat16 [3072, 3072], P('mlp'), may hold values from -0.109375 to 0.109375
- mlp_gain: float32 [3072], replicated, may hold values from 0.5 to 1.5
- w_gate: bfloat16 [3072, 8192], P(None, ('req', 'mlp')), may hold values from -0.109375 to 0.109375
- w_up: bfloat16 [3072, 8192], P(None, ('req', 'mlp')), may hold values from -0.109375 to 0.109375
- w_down: bfloat16 [8192, 3072], P(('req', 'mlp')), may hold values from -0.25 to 0.25
- final_gain: float32 [3072], replicated, may hold values from 0.5 to 1.5
- score_weight: float32 [3072], replicated, may hold values from -0.109375 to 0.109375
- slot_part: int32 [32], replicated, may hold values from 0 to 31, each once
- prompt_len: int32 [16], replicated, may hold values from 1 to 8192, 65536 in all
- tail_len: int32 [512], replicated, may hold values from 1 to 256, 65536 in all
Outputs:
- hidden_out: bfloat16 [1024, 3072], P('req', 'mlp')
- score: float32 [1024], P('req')
The draws below stay inside these ranges and needn't reach their ends.
Inputs may be any that keep to these rules, and one draw needn't show every extreme that they name: Each value once; slot s holds half slot_part[s] % 2 of prompt slot_part[s] // 2. `prompt_len`: the largest is exactly 8192. `tail_len`: the largest is exactly 256.
All inputs are finite; a program needn't handle non-finite values.
Results may differ from the reference program's by a relative error of at most 0.015.
Values may be sent and summed in bfloat16 or wider, within the bound.
A program may use at most 192 MiB of HBM per device.

```python
import math
import jax
import jax.numpy as jnp
import numpy as np
from jax import lax

D = 3072
H = 32
HD = 96
FF = 8192
CONT = 32
HALF = 4096
TAIL = 256
PROMPTS = 16
SLOTS = 32
ROWS = 1024


def draw_new_qkv(key, part):
    base_key = jax.random.fold_in(key, 0)
    return jnp.clip(jax.random.normal(base_key, (ROWS, 3, D), jnp.float32), -6.0, 6.0).astype(jnp.bfloat16)


def strengthened(result, key, source, target, blocks, factor):
    owner, partner = [(jnp.arange(result.shape[axis_at]) // (result.shape[axis_at] // blocks)).reshape([-1 if axis == axis_at else 1 for axis in range(result.ndim)]) for axis_at in (source, target)]
    chosen = jax.random.permutation(key, blocks)[partner]
    strong = (owner == chosen) | (owner == (partner + blocks // 2) % blocks)
    return jnp.where(strong, factor * result, result)


def block_levels(own_key, shape, pieces, least, top_value):
    gain, own = 1.0, jax.random.fold_in(own_key, 6)
    for axis_at, blocks in pieces:
        steps = jnp.exp(jax.random.uniform(jax.random.fold_in(own, axis_at), (blocks,), jnp.float32, least / len(pieces), top_value / len(pieces)))
        gain = gain * jnp.repeat(steps, shape[axis_at] // blocks).reshape([-1 if axis == axis_at else 1 for axis in range(len(shape))])
    return gain


def profile(amount, total, reach, slope):
    portions = [(1 << 20) // math.isqrt(rank ** slope) + 1 for rank in range(2, amount + 1)]
    surplus, counts = total - reach - (amount - 1), [1] * (amount - 1)
    while surplus > 0:
        movable = [i for i in range(amount - 1) if counts[i] < reach]
        pool, remaining = sum([portions[i] for i in movable]), surplus
        for i in movable:
            more = min(reach - counts[i], max(1, remaining * portions[i] // pool), surplus)
            counts[i] = counts[i] + more
            surplus = surplus - more
    return np.array([reach] + counts)


def ragged(stream_key, number_of, total, limit, skew):
    if number_of == 2:
        one = jax.random.randint(stream_key, (), max(1, total - limit), min(limit, total - 1) + 1)
        return jnp.stack([one, total - one])
    sizes = jnp.asarray(profile(number_of, total, limit, skew), jnp.int32)
    couples = (number_of - 1) // 2
    giver, taker = sizes[1:1 + 2 * couples:2], sizes[2:2 + 2 * couples:2]
    slack = jnp.minimum(giver - 1, limit - taker)
    shifted = jax.random.randint(jax.random.fold_in(stream_key, 1), (couples,), 0, 1 << 20) % (slack + 1)
    sizes = sizes.at[1:1 + 2 * couples:2].set(giver - shifted).at[2:2 + 2 * couples:2].set(taker + shifted)
    return sizes[jax.random.permutation(jax.random.fold_in(stream_key, 2), number_of)]


def normal_values(own_key, shape, spread, bound, shards=(), held_as=jnp.bfloat16):
    gain = block_levels(own_key, shape, shards, -0.22, 0.18) if shards else 1.0
    result = jax.random.normal(own_key, shape, jnp.float32) * spread * gain
    return jnp.minimum(jnp.maximum(result, -bound), bound).astype(held_as)


def bell_draw_with(key, dims, spread, limit, shards, heavy, kind=jnp.bfloat16):
    drawn = spread * jax.random.normal(key, dims, jnp.float32)
    if shards:
        drawn = drawn * block_levels(key, dims, shards, -0.22, 0.18)
    return jnp.clip(strengthened(drawn, jax.random.fold_in(key, 3), *heavy), -limit, limit).astype(kind)


def setup_inputs(seed: int = 0) -> dict:
    streams_of = jax.random.split(jax.random.key(seed), 15)
    new_qkv = draw_new_qkv(jax.random.fold_in(streams_of[14], 71), 0)
    prompt_cache = normal_values(streams_of[1], (SLOTS, HALF, 2, D), 1.0, 6.0, ((0, 32), (3, 4)))
    tail_cache = normal_values(streams_of[2], (PROMPTS * CONT, TAIL, 2, D), 1.0, 6.0, ((0, 32), (3, 4)))
    residual = normal_values(streams_of[3], (ROWS, D), 1.0, 6.0, ((0, 32), (1, 4)))
    w_out = normal_values(streams_of[4], (D, D), D ** -0.5, 0.109375, ((0, 4),))
    mlp_gain = jnp.clip(1.0 + 0.1 * jax.random.normal(streams_of[5], (D,), jnp.float32), 0.5, 1.5)
    w_gate = normal_values(streams_of[6], (D, FF), D ** -0.5, 0.109375, ((1, 128),))
    w_up = normal_values(streams_of[7], (D, FF), D ** -0.5, 0.109375, ((1, 128),))
    w_down = bell_draw_with(streams_of[8], (FF, D), FF ** -0.5, 0.25, ((0, 128),), (0, 1, 128, 5.5))
    final_gain = jnp.clip(1.0 + 0.1 * jax.random.normal(streams_of[9], (D,), jnp.float32), 0.5, 1.5)
    score_weight = normal_values(streams_of[10], (D,), D ** -0.5, 0.109375, (), jnp.float32)
    slot_part = jax.random.permutation(streams_of[11], SLOTS).astype(jnp.int32)
    prompt_len = ragged(streams_of[12], PROMPTS, PROMPTS * HALF, 2 * HALF, 2).astype(jnp.int32)
    tail_len = ragged(streams_of[13], PROMPTS * CONT, PROMPTS * CONT * TAIL // 2, TAIL, 1).astype(jnp.int32)
    return dict(new_qkv=new_qkv, prompt_cache=prompt_cache, tail_cache=tail_cache, residual=residual, w_out=w_out, mlp_gain=mlp_gain, w_gate=w_gate, w_up=w_up, w_down=w_down, final_gain=final_gain, score_weight=score_weight, slot_part=slot_part, prompt_len=prompt_len, tail_len=tail_len)


norm_eps = 1e-05
masked_value = -1e+30

def rotary(values, position):
    half_dim = HD // 2
    freqs = 10000.0 ** (-(jnp.arange(half_dim, dtype=jnp.float32) * 2.0) / HD)
    angles = position.astype(jnp.float32)[..., None] * freqs
    cosine = jnp.cos(angles)[..., None, :]
    sine = jnp.sin(angles)[..., None, :]
    first = values[..., :half_dim]
    second = values[..., half_dim:]
    return jnp.concatenate([first * cosine - second * sine, second * cosine + first * sine], axis=-1)

def rounded(values):
    return lax.optimization_barrier(values.astype(jnp.bfloat16)).astype(jnp.float32)

def reference(new_qkv, prompt_cache, tail_cache, residual, w_out, mlp_gain, w_gate, w_up, w_down, final_gain, score_weight, slot_part, prompt_len, tail_len):
    score_scale = 1.0 / math.sqrt(HD)
    slot_ids = jnp.arange(SLOTS, dtype=jnp.int32)
    slot_of = lax.optimization_barrier(jnp.sum(jnp.where(slot_part[None, :] == slot_ids[:, None], slot_ids[None, :], 0), axis=1)).astype(jnp.int32)
    blocks = new_qkv.reshape(PROMPTS, CONT, 2, 3, H, HD)
    tails = tail_cache.reshape(PROMPTS, CONT, TAIL, 2, H, HD)
    tail_lens = tail_len.reshape(PROMPTS, CONT)

    def one_prompt(prompt):
        block = lax.dynamic_index_in_dim(blocks, prompt, 0, keepdims=False)
        tail = lax.dynamic_index_in_dim(tails, prompt, 0, keepdims=False)
        lens = lax.dynamic_index_in_dim(tail_lens, prompt, 0, keepdims=False)
        plen = lax.dynamic_index_in_dim(prompt_len, prompt, 0, keepdims=False)
        position = plen + lens[:, None] + jnp.arange(2, dtype=jnp.int32)[None, :]
        query = rotary(block[:, :, 0].astype(jnp.float32), position).astype(jnp.bfloat16).astype(jnp.float32)
        key_new = rotary(block[:, :, 1].astype(jnp.float32), position).astype(jnp.bfloat16).astype(jnp.float32)
        value_new = block[:, :, 2].astype(jnp.float32)
        slot_a = lax.dynamic_index_in_dim(slot_of, 2 * prompt, 0, keepdims=False)
        slot_b = lax.dynamic_index_in_dim(slot_of, 2 * prompt + 1, 0, keepdims=False)
        cache = jnp.concatenate([lax.dynamic_index_in_dim(prompt_cache, slot_a, 0, keepdims=False), lax.dynamic_index_in_dim(prompt_cache, slot_b, 0, keepdims=False)], axis=0)
        pkeys = cache[:, 0].reshape(2 * HALF, H, HD).astype(jnp.float32)
        pvalues = cache[:, 1].reshape(2 * HALF, H, HD).astype(jnp.float32)
        tkeys = tail[:, :, 0].astype(jnp.float32)
        tvalues = tail[:, :, 1].astype(jnp.float32)
        s_pre = jnp.einsum('cthd,khd->chtk', query, pkeys) * score_scale
        s_pre = jnp.where(jnp.arange(2 * HALF)[None, None, None, :] < plen, s_pre, masked_value)
        s_tail = jnp.einsum('cthd,cjhd->chtj', query, tkeys) * score_scale
        s_tail = jnp.where(jnp.arange(TAIL)[None, None, None, :] < lens[:, None, None, None], s_tail, masked_value)
        s_new = jnp.einsum('cthd,cuhd->chtu', query, key_new) * score_scale
        causal = jnp.arange(2)[None, :] <= jnp.arange(2)[:, None]
        s_new = jnp.where(causal[None, None, :, :], s_new, masked_value)
        top = jnp.maximum(jnp.maximum(lax.optimization_barrier(jnp.max(s_pre, -1)), lax.optimization_barrier(jnp.max(s_tail, -1))), lax.optimization_barrier(jnp.max(s_new, -1)))
        w_pre = jnp.exp(s_pre - top[..., None])
        w_tail = jnp.exp(s_tail - top[..., None])
        w_new = jnp.exp(s_new - top[..., None])
        total = lax.optimization_barrier(jnp.sum(w_pre, -1)) + lax.optimization_barrier(jnp.sum(w_tail, -1)) + lax.optimization_barrier(jnp.sum(w_new, -1))
        numer = jnp.einsum('chtk,khd->cthd', rounded(w_pre), pvalues)
        numer = numer + jnp.einsum('chtj,cjhd->cthd', rounded(w_tail), tvalues)
        numer = numer + jnp.einsum('chtu,cuhd->cthd', rounded(w_new), value_new)
        attn = numer / jnp.transpose(total, (0, 2, 1))[..., None]
        return attn.astype(jnp.bfloat16).reshape(CONT * 2, D)
    attn = lax.map(one_prompt, jnp.arange(PROMPTS, dtype=jnp.int32)).reshape(ROWS, D)
    hstate = residual.astype(jnp.float32) + jnp.dot(attn, w_out, preferred_element_type=jnp.float32)
    normed = (hstate * lax.rsqrt(lax.optimization_barrier(jnp.mean(hstate * hstate, axis=1, keepdims=True)) + norm_eps) * mlp_gain).astype(jnp.bfloat16)
    gate = jnp.dot(normed, w_gate, preferred_element_type=jnp.float32)
    upper = jnp.dot(normed, w_up, preferred_element_type=jnp.float32)
    hidden = (jax.nn.silu(gate) * upper).astype(jnp.bfloat16)
    final_state = hstate + jnp.dot(hidden, w_down, preferred_element_type=jnp.float32)
    scores = lax.optimization_barrier(jnp.sum(final_state * final_gain * score_weight, axis=1)) * lax.rsqrt(lax.optimization_barrier(jnp.mean(final_state * final_state, axis=1)) + norm_eps)
    return (final_state.astype(jnp.bfloat16), scores)
```

```python
import math

import jax
import jax.numpy as jnp
from jax import lax
from jax.sharding import PartitionSpec as P

HD = 96


norm_eps = 1e-05
masked_value = -1e30


def rotary(values, position):
    half_dim = HD // 2
    freqs = 10000.0 ** (-(jnp.arange(half_dim, dtype=jnp.float32) * 2.0) / HD)
    angles = position.astype(jnp.float32)[..., None] * freqs
    cosine = jnp.cos(angles)[..., None, :]
    sine = jnp.sin(angles)[..., None, :]
    first = values[..., :half_dim]
    second = values[..., half_dim:]
    return jnp.concatenate(
        [first * cosine - second * sine, second * cosine + first * sine], axis=-1
    )


def per_device(
    new_qkv,
    prompt_cache,
    tail_cache,
    residual,
    w_out,
    mlp_gain,
    w_gate,
    w_up,
    w_down,
    final_gain,
    score_weight,
    slot_part,
    prompt_len,
    tail_len,
):
    req_count = lax.axis_size("req")
    req_index = lax.axis_index("req")
    mlp_index = lax.axis_index("mlp")
    rows_here = new_qkv.shape[0]
    width_here = new_qkv.shape[2]
    heads_here = width_here // HD
    conts_here = rows_here // 2
    width = w_out.shape[1]
    score_scale = 1.0 / math.sqrt(HD)
    own_prompt = req_index // 2
    tail_here = lax.dynamic_slice_in_dim(tail_len, req_index * conts_here, conts_here)
    plen_here = lax.dynamic_index_in_dim(prompt_len, own_prompt, 0, keepdims=False)
    position = plen_here + tail_here[:, None] + jnp.arange(2, dtype=jnp.int32)[None, :]
    block = new_qkv.reshape(conts_here, 2, 3, heads_here, HD)
    query = rotary(block[:, :, 0].astype(jnp.float32), position).astype(jnp.bfloat16)
    key_new = rotary(block[:, :, 1].astype(jnp.float32), position).astype(jnp.bfloat16)
    value_new = block[:, :, 2]
    gathered = lax.all_gather(query.reshape(rows_here, width_here), "req", axis=0, tiled=True)
    slot_ids = jnp.arange(req_count, dtype=jnp.int32)
    slot_of = jnp.sum(
        jnp.where(slot_part[None, :] == slot_ids[:, None], slot_ids[None, :], 0), axis=1
    )
    held_part = lax.dynamic_index_in_dim(slot_part, req_index, 0, keepdims=False)
    owned_prompt = held_part // 2
    held_half = held_part % 2
    span = prompt_cache.shape[1]
    owned_rows = 2 * rows_here
    q_owned = lax.dynamic_slice_in_dim(gathered, owned_prompt * owned_rows, owned_rows, 0).reshape(
        owned_rows, heads_here, HD
    )
    owned_len = lax.dynamic_index_in_dim(prompt_len, owned_prompt, 0, keepdims=False)
    valid_count = jnp.clip(owned_len - held_half * span, 0, span)
    block_len = min(512, span)
    block_count = (valid_count + block_len - 1) // block_len
    cache_keys = prompt_cache[0, :, 0].reshape(span, heads_here, HD)
    cache_values = prompt_cache[0, :, 1].reshape(span, heads_here, HD)

    def score_block(number, buffer):
        key_block = lax.dynamic_slice_in_dim(cache_keys, number * block_len, block_len, 0)
        block_scores = (
            jnp.einsum("rhd,khd->hrk", q_owned, key_block, preferred_element_type=jnp.float32)
            * score_scale
        )
        places = number * block_len + jnp.arange(block_len, dtype=jnp.int32)
        block_scores = jnp.where(places[None, None, :] < valid_count, block_scores, masked_value)
        return lax.dynamic_update_slice_in_dim(buffer, block_scores, number * block_len, 2)

    empty_scores = jnp.full((heads_here, owned_rows, span), masked_value, jnp.float32)
    prefix_scores = lax.fori_loop(0, block_count, score_block, empty_scores)
    prefix_max = jnp.max(prefix_scores, axis=2)

    def value_block(number, carry):
        numer, totals = carry
        score_part = lax.dynamic_slice_in_dim(prefix_scores, number * block_len, block_len, 2)
        weights = jnp.exp(score_part - prefix_max[:, :, None])
        value_part = lax.dynamic_slice_in_dim(cache_values, number * block_len, block_len, 0)
        numer = numer + jnp.einsum(
            "hrk,khd->rhd",
            weights.astype(jnp.bfloat16),
            value_part,
            preferred_element_type=jnp.float32,
        )
        return (numer, totals + jnp.sum(weights, axis=2))

    start_carry = (
        jnp.zeros((owned_rows, heads_here, HD), jnp.float32),
        jnp.zeros((heads_here, owned_rows), jnp.float32),
    )
    owner_numer, owner_total = lax.fori_loop(0, block_count, value_block, start_carry)
    packed = jnp.concatenate(
        [
            owner_numer.reshape(owned_rows, width_here),
            jnp.transpose(owner_total),
            jnp.transpose(prefix_max),
        ],
        axis=1,
    )
    packed_all = lax.all_gather(packed[None], "req", axis=0, tiled=True)
    row_offset = req_index % 2 * rows_here
    slot_first = lax.dynamic_index_in_dim(slot_of, 2 * own_prompt, 0, keepdims=False)
    slot_second = lax.dynamic_index_in_dim(slot_of, 2 * own_prompt + 1, 0, keepdims=False)

    def part_of(slot):
        piece = lax.dynamic_slice_in_dim(
            lax.dynamic_index_in_dim(packed_all, slot, 0, keepdims=False), row_offset, rows_here, 0
        )
        numer = piece[:, :width_here].reshape(rows_here, heads_here, HD)
        total = piece[:, width_here : width_here + heads_here]
        top = piece[:, width_here + heads_here :]
        return numer, total, top

    numer_first, total_first, max_first = part_of(slot_first)
    numer_second, total_second, max_second = part_of(slot_second)

    tail_cap = tail_cache.shape[1]
    tail_keys = tail_cache[:, :, 0].reshape(conts_here, tail_cap, heads_here, HD)
    tail_values = tail_cache[:, :, 1].reshape(conts_here, tail_cap, heads_here, HD)
    s_tail = (
        jnp.einsum("cthd,cjhd->chtj", query, tail_keys, preferred_element_type=jnp.float32)
        * score_scale
    )
    s_tail = jnp.where(
        jnp.arange(tail_cap)[None, None, None, :] < tail_here[:, None, None, None],
        s_tail,
        masked_value,
    )
    s_new = (
        jnp.einsum("cthd,cuhd->chtu", query, key_new, preferred_element_type=jnp.float32)
        * score_scale
    )
    causal = jnp.arange(2)[None, :] <= jnp.arange(2)[:, None]
    s_new = jnp.where(causal[None, None, :, :], s_new, masked_value)
    tail_max = jnp.maximum(jnp.max(s_tail, -1), jnp.max(s_new, -1))
    w_tail = jnp.exp(s_tail - tail_max[..., None])
    w_new = jnp.exp(s_new - tail_max[..., None])
    numer_tail = jnp.einsum(
        "chtj,cjhd->cthd",
        w_tail.astype(jnp.bfloat16),
        tail_values,
        preferred_element_type=jnp.float32,
    )
    numer_tail = numer_tail + jnp.einsum(
        "chtu,cuhd->cthd", w_new.astype(jnp.bfloat16), value_new, preferred_element_type=jnp.float32
    )
    numer_tail = numer_tail.reshape(rows_here, heads_here, HD)
    total_tail = jnp.transpose(jnp.sum(w_tail, -1) + jnp.sum(w_new, -1), (0, 2, 1)).reshape(
        rows_here, heads_here
    )
    max_tail = jnp.transpose(tail_max, (0, 2, 1)).reshape(rows_here, heads_here)
    row_max = jnp.maximum(jnp.maximum(max_first, max_second), max_tail)
    scale_first = jnp.exp(max_first - row_max)
    scale_second = jnp.exp(max_second - row_max)
    scale_tail = jnp.exp(max_tail - row_max)
    row_total = total_first * scale_first + total_second * scale_second + total_tail * scale_tail
    row_numer = (
        numer_first * scale_first[..., None]
        + numer_second * scale_second[..., None]
        + numer_tail * scale_tail[..., None]
    )
    attn = (row_numer / row_total[:, :, None]).astype(jnp.bfloat16).reshape(rows_here, width_here)
    residual_full = lax.all_gather(residual, "mlp", axis=1, tiled=True)
    projected = lax.psum(jnp.dot(attn, w_out, preferred_element_type=jnp.float32), "mlp")
    state = residual_full.astype(jnp.float32) + projected
    mean_square = jnp.mean(state * state, axis=1, keepdims=True)
    normed = (state * lax.rsqrt(mean_square + norm_eps) * mlp_gain).astype(jnp.bfloat16)
    mlp_count = lax.axis_size("mlp")
    share = rows_here // mlp_count
    normed_share = lax.dynamic_slice_in_dim(normed, mlp_index * share, share, 0)
    piece = lax.all_gather(normed_share, "req", axis=0, tiled=True)
    gate_w = lax.all_gather(w_gate, "mlp", axis=1, tiled=True)
    up_w = lax.all_gather(w_up, "mlp", axis=1, tiled=True)
    down_w = lax.all_gather(w_down, "mlp", axis=0, tiled=True)
    gate = jnp.dot(piece, gate_w, preferred_element_type=jnp.float32)
    upper = jnp.dot(piece, up_w, preferred_element_type=jnp.float32)
    hidden_all = (jax.nn.silu(gate) * upper).astype(jnp.bfloat16)
    row_sums = lax.psum_scatter(
        jnp.dot(hidden_all, down_w, preferred_element_type=jnp.float32),
        "req",
        scatter_dimension=0,
        tiled=True,
    )
    state_share = lax.dynamic_slice_in_dim(state, mlp_index * share, share, 0)
    final_share = state_share + row_sums
    final_square = jnp.mean(final_share * final_share, axis=1)
    final_dot = jnp.sum(final_share * final_gain * score_weight, axis=1)
    score_share = final_dot * lax.rsqrt(final_square + norm_eps)
    scores = lax.all_gather(score_share, "mlp", axis=0, tiled=True)
    out_rows = lax.all_to_all(
        final_share.astype(jnp.bfloat16), "mlp", split_axis=1, concat_axis=0, tiled=True
    )
    return (out_rows, scores)


def solution(mesh):
    in_specs = (
        P("req", None, "mlp"),
        P("req", None, None, "mlp"),
        P("req", None, None, "mlp"),
        P("req", "mlp"),
        P("mlp", None),
        P(),
        P(None, ("req", "mlp")),
        P(None, ("req", "mlp")),
        P(("req", "mlp"), None),
        P(),
        P(),
        P(),
        P(),
        P(),
    )
    out_specs = (P("req", "mlp"), P("req"))
    return jax.shard_map(
        per_device, mesh=mesh, in_specs=in_specs, out_specs=out_specs, check_vma=False
    )
```

```python
import math

import jax
import jax.numpy as jnp
from jax import lax
from jax.sharding import PartitionSpec as P

HD = 96


norm_eps = 1e-05
masked_value = -1e30


def rotary(values, position):
    half_dim = HD // 2
    freqs = 10000.0 ** (-(jnp.arange(half_dim, dtype=jnp.float32) * 2.0) / HD)
    angles = position.astype(jnp.float32)[..., None] * freqs
    cosine = jnp.cos(angles)[..., None, :]
    sine = jnp.sin(angles)[..., None, :]
    first = values[..., :half_dim]
    second = values[..., half_dim:]
    return jnp.concatenate(
        [first * cosine - second * sine, second * cosine + first * sine], axis=-1
    )


def per_device(
    new_qkv,
    prompt_cache,
    tail_cache,
    residual,
    w_out,
    mlp_gain,
    w_gate,
    w_up,
    w_down,
    final_gain,
    score_weight,
    slot_part,
    prompt_len,
    tail_len,
):
    req_count = lax.axis_size("req")
    req_index = lax.axis_index("req")
    mlp_index = lax.axis_index("mlp")
    rows_here = new_qkv.shape[0]
    width_here = new_qkv.shape[2]
    heads_here = width_here // HD
    conts_here = rows_here // 2
    width = w_out.shape[1]
    score_scale = 1.0 / math.sqrt(HD)
    own_prompt = req_index // 2
    tail_here = lax.dynamic_slice_in_dim(tail_len, req_index * conts_here, conts_here)
    plen_here = lax.dynamic_index_in_dim(prompt_len, own_prompt, 0, keepdims=False)
    position = plen_here + tail_here[:, None] + jnp.arange(2, dtype=jnp.int32)[None, :]
    block = new_qkv.reshape(conts_here, 2, 3, heads_here, HD)
    query = rotary(block[:, :, 0].astype(jnp.float32), position).astype(jnp.bfloat16)
    key_new = rotary(block[:, :, 1].astype(jnp.float32), position).astype(jnp.bfloat16)
    value_new = block[:, :, 2]
    gathered = lax.all_gather(query.reshape(rows_here, width_here), "req", axis=0, tiled=True)
    weights_cat = jnp.concatenate([w_gate, w_up, jnp.transpose(w_down)], axis=1)
    weights_all = lax.all_gather(weights_cat, "mlp", axis=0, tiled=False)
    gathered, weights_all = lax.optimization_barrier((gathered, weights_all))
    slot_ids = jnp.arange(req_count, dtype=jnp.int32)
    slot_of = jnp.sum(
        jnp.where(slot_part[None, :] == slot_ids[:, None], slot_ids[None, :], 0), axis=1
    )
    held_part = lax.dynamic_index_in_dim(slot_part, req_index, 0, keepdims=False)
    owned_prompt = held_part // 2
    held_half = held_part % 2
    span = prompt_cache.shape[1]
    owned_rows = 2 * rows_here
    q_owned = lax.dynamic_slice_in_dim(gathered, owned_prompt * owned_rows, owned_rows, 0).reshape(
        owned_rows, heads_here, HD
    )
    owned_len = lax.dynamic_index_in_dim(prompt_len, owned_prompt, 0, keepdims=False)
    valid_count = jnp.clip(owned_len - held_half * span, 0, span)
    block_len = min(512, span)
    block_count = (valid_count + block_len - 1) // block_len
    cache_keys = prompt_cache[0, :, 0].reshape(span, heads_here, HD)
    cache_values = prompt_cache[0, :, 1].reshape(span, heads_here, HD)

    def score_block(number, buffer):
        key_block = lax.dynamic_slice_in_dim(cache_keys, number * block_len, block_len, 0)
        block_scores = (
            jnp.einsum("rhd,khd->hrk", q_owned, key_block, preferred_element_type=jnp.float32)
            * score_scale
        )
        places = number * block_len + jnp.arange(block_len, dtype=jnp.int32)
        block_scores = jnp.where(places[None, None, :] < valid_count, block_scores, masked_value)
        return lax.dynamic_update_slice_in_dim(buffer, block_scores, number * block_len, 2)

    empty_scores = jnp.full((heads_here, owned_rows, span), masked_value, jnp.float32)
    prefix_scores = lax.fori_loop(0, block_count, score_block, empty_scores)
    prefix_max = jnp.max(prefix_scores, axis=2)

    def value_block(number, carry):
        numer, totals = carry
        score_part = lax.dynamic_slice_in_dim(prefix_scores, number * block_len, block_len, 2)
        weights = jnp.exp(score_part - prefix_max[:, :, None])
        value_part = lax.dynamic_slice_in_dim(cache_values, number * block_len, block_len, 0)
        numer = numer + jnp.einsum(
            "hrk,khd->rhd",
            weights.astype(jnp.bfloat16),
            value_part,
            preferred_element_type=jnp.float32,
        )
        return (numer, totals + jnp.sum(weights, axis=2))

    start_carry = (
        jnp.zeros((owned_rows, heads_here, HD), jnp.float32),
        jnp.zeros((heads_here, owned_rows), jnp.float32),
    )
    owner_numer, owner_total = lax.fori_loop(0, block_count, value_block, start_carry)
    packed = jnp.concatenate(
        [
            owner_numer.reshape(owned_rows, width_here),
            jnp.transpose(owner_total),
            jnp.transpose(prefix_max),
        ],
        axis=1,
    )
    packed_all = lax.all_gather(packed[None], "req", axis=0, tiled=True)
    row_offset = req_index % 2 * rows_here
    slot_first = lax.dynamic_index_in_dim(slot_of, 2 * own_prompt, 0, keepdims=False)
    slot_second = lax.dynamic_index_in_dim(slot_of, 2 * own_prompt + 1, 0, keepdims=False)

    def part_of(slot):
        piece = lax.dynamic_slice_in_dim(
            lax.dynamic_index_in_dim(packed_all, slot, 0, keepdims=False), row_offset, rows_here, 0
        )
        numer = piece[:, :width_here].reshape(rows_here, heads_here, HD)
        total = piece[:, width_here : width_here + heads_here]
        top = piece[:, width_here + heads_here :]
        return numer, total, top

    numer_first, total_first, max_first = part_of(slot_first)
    numer_second, total_second, max_second = part_of(slot_second)

    tail_cap = tail_cache.shape[1]
    tail_keys = tail_cache[:, :, 0].reshape(conts_here, tail_cap, heads_here, HD)
    tail_values = tail_cache[:, :, 1].reshape(conts_here, tail_cap, heads_here, HD)
    s_tail = (
        jnp.einsum("cthd,cjhd->chtj", query, tail_keys, preferred_element_type=jnp.float32)
        * score_scale
    )
    s_tail = jnp.where(
        jnp.arange(tail_cap)[None, None, None, :] < tail_here[:, None, None, None],
        s_tail,
        masked_value,
    )
    s_new = (
        jnp.einsum("cthd,cuhd->chtu", query, key_new, preferred_element_type=jnp.float32)
        * score_scale
    )
    causal = jnp.arange(2)[None, :] <= jnp.arange(2)[:, None]
    s_new = jnp.where(causal[None, None, :, :], s_new, masked_value)
    tail_max = jnp.maximum(jnp.max(s_tail, -1), jnp.max(s_new, -1))
    w_tail = jnp.exp(s_tail - tail_max[..., None])
    w_new = jnp.exp(s_new - tail_max[..., None])
    numer_tail = jnp.einsum(
        "chtj,cjhd->cthd",
        w_tail.astype(jnp.bfloat16),
        tail_values,
        preferred_element_type=jnp.float32,
    )
    numer_tail = numer_tail + jnp.einsum(
        "chtu,cuhd->cthd", w_new.astype(jnp.bfloat16), value_new, preferred_element_type=jnp.float32
    )
    numer_tail = numer_tail.reshape(rows_here, heads_here, HD)
    total_tail = jnp.transpose(jnp.sum(w_tail, -1) + jnp.sum(w_new, -1), (0, 2, 1)).reshape(
        rows_here, heads_here
    )
    max_tail = jnp.transpose(tail_max, (0, 2, 1)).reshape(rows_here, heads_here)
    row_max = jnp.maximum(jnp.maximum(max_first, max_second), max_tail)
    scale_first = jnp.exp(max_first - row_max)
    scale_second = jnp.exp(max_second - row_max)
    scale_tail = jnp.exp(max_tail - row_max)
    row_total = total_first * scale_first + total_second * scale_second + total_tail * scale_tail
    row_numer = (
        numer_first * scale_first[..., None]
        + numer_second * scale_second[..., None]
        + numer_tail * scale_tail[..., None]
    )
    attn = (row_numer / row_total[:, :, None]).astype(jnp.bfloat16).reshape(rows_here, width_here)
    residual_full = lax.all_gather(residual, "mlp", axis=1, tiled=True)
    projected = lax.psum(jnp.dot(attn, w_out, preferred_element_type=jnp.float32), "mlp")
    state = residual_full.astype(jnp.float32) + projected
    mean_square = jnp.mean(state * state, axis=1, keepdims=True)
    normed = (state * lax.rsqrt(mean_square + norm_eps) * mlp_gain).astype(jnp.bfloat16)
    mlp_count = lax.axis_size("mlp")
    share = rows_here // mlp_count
    normed_share = lax.dynamic_slice_in_dim(normed, mlp_index * share, share, 0)
    piece = lax.all_gather(normed_share, "req", axis=0, tiled=True)
    hidden_here = w_gate.shape[1]
    gate_w = weights_all[:, :, :hidden_here]
    up_w = weights_all[:, :, hidden_here : 2 * hidden_here]
    down_w = weights_all[:, :, 2 * hidden_here :]
    gate = jnp.einsum("rk,mkj->rmj", piece, gate_w, preferred_element_type=jnp.float32)
    upper = jnp.einsum("rk,mkj->rmj", piece, up_w, preferred_element_type=jnp.float32)
    hidden_all = (jax.nn.silu(gate) * upper).astype(jnp.bfloat16)
    down_sum = jnp.einsum("rmj,mfj->rf", hidden_all, down_w, preferred_element_type=jnp.float32)
    row_sums = lax.psum_scatter(
        down_sum,
        "req",
        scatter_dimension=0,
        tiled=True,
    )
    state_share = lax.dynamic_slice_in_dim(state, mlp_index * share, share, 0)
    final_share = state_share + row_sums
    final_square = jnp.mean(final_share * final_share, axis=1)
    final_dot = jnp.sum(final_share * final_gain * score_weight, axis=1)
    score_share = final_dot * lax.rsqrt(final_square + norm_eps)
    scores = lax.all_gather(score_share, "mlp", axis=0, tiled=True)
    out_rows = lax.all_to_all(
        final_share.astype(jnp.bfloat16), "mlp", split_axis=1, concat_axis=0, tiled=True
    )
    return (out_rows, scores)


def solution(mesh):
    in_specs = (
        P("req", None, "mlp"),
        P("req", None, None, "mlp"),
        P("req", None, None, "mlp"),
        P("req", "mlp"),
        P("mlp", None),
        P(),
        P(None, ("req", "mlp")),
        P(None, ("req", "mlp")),
        P(("req", "mlp"), None),
        P(),
        P(),
        P(),
        P(),
        P(),
    )
    out_specs = (P("req", "mlp"), P("req"))
    return jax.shard_map(
        per_device, mesh=mesh, in_specs=in_specs, out_specs=out_specs, check_vma=False
    )
```

```python
import functools
import math

import jax
import jax.numpy as jnp
from jax import lax
from jax.experimental import pallas as pl
from jax.experimental.pallas import tpu as pltpu
from jax.sharding import PartitionSpec as P

HD = 96


norm_eps = 1e-05
masked_value = -1e30


def rotary(values, position):
    half_dim = HD // 2
    freqs = 10000.0 ** (-(jnp.arange(half_dim, dtype=jnp.float32) * 2.0) / HD)
    angles = position.astype(jnp.float32)[..., None] * freqs
    cosine = jnp.cos(angles)[..., None, :]
    sine = jnp.sin(angles)[..., None, :]
    first = values[..., :half_dim]
    second = values[..., half_dim:]
    return jnp.concatenate(
        [first * cosine - second * sine, second * cosine + first * sine], axis=-1
    )


def prompt_kernel(block_len, score_scale, valid_ref, q_ref, cache_ref, acc_ref, top_ref, sum_ref):
    number = pl.program_id(0)

    @pl.when(number == 0)
    def _():
        acc_ref[...] = jnp.zeros_like(acc_ref)
        top_ref[...] = jnp.full_like(top_ref, masked_value)
        sum_ref[...] = jnp.zeros_like(sum_ref)

    @pl.when(number * block_len < valid_ref[0])
    def _():
        keys = cache_ref[:, 0, :]
        values = cache_ref[:, 1, :]
        scores = (
            lax.dot_general(
                q_ref[...], keys, (((1,), (1,)), ((), ())), preferred_element_type=jnp.float32
            )
            * score_scale
        )
        places = number * block_len + lax.broadcasted_iota(jnp.int32, scores.shape, 1)
        scores = jnp.where(places < valid_ref[0], scores, masked_value)
        top_old = top_ref[...]
        top_new = jnp.maximum(top_old, jnp.max(scores, axis=1, keepdims=True))
        shrink = jnp.exp(top_old - top_new)
        weights = jnp.exp(scores - top_new)
        sum_ref[...] = shrink * sum_ref[...] + jnp.sum(weights, axis=1, keepdims=True)
        acc_ref[...] = shrink * acc_ref[...] + jnp.dot(
            weights.astype(jnp.bfloat16), values, preferred_element_type=jnp.float32
        )
        top_ref[...] = top_new


def prompt_attention(q_diag, cache, valid_count, score_scale):
    span = cache.shape[1]
    block_len = min(512, span)
    lanes = cache.shape[3]
    rows = q_diag.shape[0]

    def cache_block(number, valid):
        last = (valid[0] + block_len - 1) // block_len - 1
        return (0, jnp.maximum(jnp.minimum(number, last), 0), 0, 0)

    spec = pltpu.PrefetchScalarGridSpec(
        num_scalar_prefetch=1,
        grid=(span // block_len,),
        in_specs=[
            pl.BlockSpec((rows, lanes), lambda number, valid: (0, 0)),
            pl.BlockSpec((None, block_len, 2, lanes), cache_block),
        ],
        out_specs=[
            pl.BlockSpec((rows, lanes), lambda number, valid: (0, 0)),
            pl.BlockSpec((rows, 1), lambda number, valid: (0, 0)),
            pl.BlockSpec((rows, 1), lambda number, valid: (0, 0)),
        ],
    )
    return pl.pallas_call(
        functools.partial(prompt_kernel, block_len, score_scale),
        grid_spec=spec,
        out_shape=[
            jax.ShapeDtypeStruct((rows, lanes), jnp.float32),
            jax.ShapeDtypeStruct((rows, 1), jnp.float32),
            jax.ShapeDtypeStruct((rows, 1), jnp.float32),
        ],
    )(valid_count.reshape(1), q_diag, cache)


def tail_kernel(score_scale, lens_ref, q_ref, cache_ref, acc_ref, top_ref, sum_ref):
    number = pl.program_id(0)
    keys = cache_ref[:, 0, :]
    values = cache_ref[:, 1, :]
    scores = (
        lax.dot_general(q_ref[...], keys, (((1,), (1,)), ((), ())), preferred_element_type=jnp.float32)
        * score_scale
    )
    places = lax.broadcasted_iota(jnp.int32, scores.shape, 1)
    scores = jnp.where(places < lens_ref[number], scores, masked_value)
    top = jnp.max(scores, axis=1, keepdims=True)
    weights = jnp.exp(scores - top)
    top_ref[...] = top
    sum_ref[...] = jnp.sum(weights, axis=1, keepdims=True)
    acc_ref[...] = jnp.dot(weights.astype(jnp.bfloat16), values, preferred_element_type=jnp.float32)


def tail_attention(q_diag, cache, lens, score_scale):
    conts, rows, lanes = q_diag.shape
    cap = cache.shape[1]
    spec = pltpu.PrefetchScalarGridSpec(
        num_scalar_prefetch=1,
        grid=(conts,),
        in_specs=[
            pl.BlockSpec((None, rows, lanes), lambda number, lens: (number, 0, 0)),
            pl.BlockSpec((None, cap, 2, lanes), lambda number, lens: (number, 0, 0, 0)),
        ],
        out_specs=[
            pl.BlockSpec((None, rows, lanes), lambda number, lens: (number, 0, 0)),
            pl.BlockSpec((None, rows, 1), lambda number, lens: (number, 0, 0)),
            pl.BlockSpec((None, rows, 1), lambda number, lens: (number, 0, 0)),
        ],
    )
    return pl.pallas_call(
        functools.partial(tail_kernel, score_scale),
        grid_spec=spec,
        out_shape=[
            jax.ShapeDtypeStruct((conts, rows, lanes), jnp.float32),
            jax.ShapeDtypeStruct((conts, rows, 1), jnp.float32),
            jax.ShapeDtypeStruct((conts, rows, 1), jnp.float32),
        ],
    )(lens, q_diag, cache)


def per_device(
    new_qkv,
    prompt_cache,
    tail_cache,
    residual,
    w_out,
    mlp_gain,
    w_gate,
    w_up,
    w_down,
    final_gain,
    score_weight,
    slot_part,
    prompt_len,
    tail_len,
):
    req_count = lax.axis_size("req")
    req_index = lax.axis_index("req")
    mlp_index = lax.axis_index("mlp")
    rows_here = new_qkv.shape[0]
    width_here = new_qkv.shape[2]
    heads_here = width_here // HD
    conts_here = rows_here // 2
    width = w_out.shape[1]
    score_scale = 1.0 / math.sqrt(HD)
    own_prompt = req_index // 2
    tail_here = lax.dynamic_slice_in_dim(tail_len, req_index * conts_here, conts_here)
    plen_here = lax.dynamic_index_in_dim(prompt_len, own_prompt, 0, keepdims=False)
    position = plen_here + tail_here[:, None] + jnp.arange(2, dtype=jnp.int32)[None, :]
    block = new_qkv.reshape(conts_here, 2, 3, heads_here, HD)
    query = rotary(block[:, :, 0].astype(jnp.float32), position).astype(jnp.bfloat16)
    key_new = rotary(block[:, :, 1].astype(jnp.float32), position).astype(jnp.bfloat16)
    value_new = block[:, :, 2]
    gathered = lax.all_gather(query.reshape(rows_here, width_here), "req", axis=0, tiled=True)
    weights_cat = jnp.concatenate([w_gate, w_up, jnp.transpose(w_down)], axis=1)
    weights_all = lax.all_gather(weights_cat, "mlp", axis=0, tiled=False)
    gathered, weights_all = lax.optimization_barrier((gathered, weights_all))
    slot_ids = jnp.arange(req_count, dtype=jnp.int32)
    slot_of = jnp.sum(
        jnp.where(slot_part[None, :] == slot_ids[:, None], slot_ids[None, :], 0), axis=1
    )
    held_part = lax.dynamic_index_in_dim(slot_part, req_index, 0, keepdims=False)
    owned_prompt = held_part // 2
    held_half = held_part % 2
    span = prompt_cache.shape[1]
    owned_rows = 2 * rows_here
    q_owned = lax.dynamic_slice_in_dim(gathered, owned_prompt * owned_rows, owned_rows, 0).reshape(
        owned_rows, heads_here, HD
    )
    owned_len = lax.dynamic_index_in_dim(prompt_len, owned_prompt, 0, keepdims=False)
    valid_count = jnp.clip(owned_len - held_half * span, 0, span)
    eye = jnp.eye(heads_here, dtype=jnp.bfloat16)
    q_diag = jnp.einsum("rhd,hg->hrgd", q_owned, eye).reshape(heads_here * owned_rows, width_here)
    prompt_acc, prompt_top, prompt_sum = prompt_attention(q_diag, prompt_cache, valid_count, score_scale)
    prompt_acc = prompt_acc.reshape(heads_here, owned_rows, heads_here, HD)
    owner_numer = jnp.stack([prompt_acc[h, :, h, :] for h in range(heads_here)], axis=1)
    owner_total = prompt_sum.reshape(heads_here, owned_rows)
    prefix_max = prompt_top.reshape(heads_here, owned_rows)
    packed = jnp.concatenate(
        [
            owner_numer.reshape(owned_rows, width_here),
            jnp.transpose(owner_total),
            jnp.transpose(prefix_max),
        ],
        axis=1,
    )
    packed_all = lax.all_gather(packed[None], "req", axis=0, tiled=True)
    row_offset = req_index % 2 * rows_here
    slot_first = lax.dynamic_index_in_dim(slot_of, 2 * own_prompt, 0, keepdims=False)
    slot_second = lax.dynamic_index_in_dim(slot_of, 2 * own_prompt + 1, 0, keepdims=False)

    def part_of(slot):
        piece = lax.dynamic_slice_in_dim(
            lax.dynamic_index_in_dim(packed_all, slot, 0, keepdims=False), row_offset, rows_here, 0
        )
        numer = piece[:, :width_here].reshape(rows_here, heads_here, HD)
        total = piece[:, width_here : width_here + heads_here]
        top = piece[:, width_here + heads_here :]
        return numer, total, top

    numer_first, total_first, max_first = part_of(slot_first)
    numer_second, total_second, max_second = part_of(slot_second)

    tail_diag = jnp.einsum("cthd,hg->chtgd", query, eye).reshape(
        conts_here, heads_here * 2, width_here
    )
    tail_acc, tail_top, tail_sum = tail_attention(tail_diag, tail_cache, tail_here, score_scale)
    tail_acc = tail_acc.reshape(conts_here, heads_here, 2, heads_here, HD)
    cache_numer = jnp.stack([tail_acc[:, h, :, h, :] for h in range(heads_here)], axis=2)
    cache_top = tail_top.reshape(conts_here, heads_here, 2)
    cache_sum = tail_sum.reshape(conts_here, heads_here, 2)
    s_new = (
        jnp.einsum("cthd,cuhd->chtu", query, key_new, preferred_element_type=jnp.float32)
        * score_scale
    )
    causal = jnp.arange(2)[None, :] <= jnp.arange(2)[:, None]
    s_new = jnp.where(causal[None, None, :, :], s_new, masked_value)
    tail_max = jnp.maximum(cache_top, jnp.max(s_new, -1))
    cache_scale = jnp.exp(cache_top - tail_max)
    w_new = jnp.exp(s_new - tail_max[..., None])
    numer_tail = cache_numer * jnp.transpose(cache_scale, (0, 2, 1))[..., None]
    numer_tail = numer_tail + jnp.einsum(
        "chtu,cuhd->cthd", w_new.astype(jnp.bfloat16), value_new, preferred_element_type=jnp.float32
    )
    numer_tail = numer_tail.reshape(rows_here, heads_here, HD)
    total_tail = jnp.transpose(cache_sum * cache_scale + jnp.sum(w_new, -1), (0, 2, 1)).reshape(
        rows_here, heads_here
    )
    max_tail = jnp.transpose(tail_max, (0, 2, 1)).reshape(rows_here, heads_here)
    row_max = jnp.maximum(jnp.maximum(max_first, max_second), max_tail)
    scale_first = jnp.exp(max_first - row_max)
    scale_second = jnp.exp(max_second - row_max)
    scale_tail = jnp.exp(max_tail - row_max)
    row_total = total_first * scale_first + total_second * scale_second + total_tail * scale_tail
    row_numer = (
        numer_first * scale_first[..., None]
        + numer_second * scale_second[..., None]
        + numer_tail * scale_tail[..., None]
    )
    attn = (row_numer / row_total[:, :, None]).astype(jnp.bfloat16).reshape(rows_here, width_here)
    residual_full = lax.all_gather(residual, "mlp", axis=1, tiled=True)
    projected = lax.psum(jnp.dot(attn, w_out, preferred_element_type=jnp.float32), "mlp")
    state = residual_full.astype(jnp.float32) + projected
    mean_square = jnp.mean(state * state, axis=1, keepdims=True)
    normed = (state * lax.rsqrt(mean_square + norm_eps) * mlp_gain).astype(jnp.bfloat16)
    mlp_count = lax.axis_size("mlp")
    share = rows_here // mlp_count
    normed_share = lax.dynamic_slice_in_dim(normed, mlp_index * share, share, 0)
    piece = lax.all_gather(normed_share, "req", axis=0, tiled=True)
    hidden_here = w_gate.shape[1]
    gate_w = weights_all[:, :, :hidden_here]
    up_w = weights_all[:, :, hidden_here : 2 * hidden_here]
    down_w = weights_all[:, :, 2 * hidden_here :]
    gate = jnp.einsum("rk,mkj->rmj", piece, gate_w, preferred_element_type=jnp.float32)
    upper = jnp.einsum("rk,mkj->rmj", piece, up_w, preferred_element_type=jnp.float32)
    hidden_all = (jax.nn.silu(gate) * upper).astype(jnp.bfloat16)
    down_sum = jnp.einsum("rmj,mfj->rf", hidden_all, down_w, preferred_element_type=jnp.float32)
    row_sums = lax.psum_scatter(
        down_sum,
        "req",
        scatter_dimension=0,
        tiled=True,
    )
    state_share = lax.dynamic_slice_in_dim(state, mlp_index * share, share, 0)
    final_share = state_share + row_sums
    final_square = jnp.mean(final_share * final_share, axis=1)
    final_dot = jnp.sum(final_share * final_gain * score_weight, axis=1)
    score_share = final_dot * lax.rsqrt(final_square + norm_eps)
    scores = lax.all_gather(score_share, "mlp", axis=0, tiled=True)
    out_rows = lax.all_to_all(
        final_share.astype(jnp.bfloat16), "mlp", split_axis=1, concat_axis=0, tiled=True
    )
    return (out_rows, scores)


def solution(mesh):
    in_specs = (
        P("req", None, "mlp"),
        P("req", None, None, "mlp"),
        P("req", None, None, "mlp"),
        P("req", "mlp"),
        P("mlp", None),
        P(),
        P(None, ("req", "mlp")),
        P(None, ("req", "mlp")),
        P(("req", "mlp"), None),
        P(),
        P(),
        P(),
        P(),
        P(),
    )
    out_specs = (P("req", "mlp"), P("req"))
    return jax.shard_map(
        per_device, mesh=mesh, in_specs=in_specs, out_specs=out_specs, check_vma=False
    )
```

```python
import functools
import math

import jax
import jax.numpy as jnp
from jax import lax
from jax.experimental import pallas as pl
from jax.experimental.pallas import tpu as pltpu
from jax.sharding import PartitionSpec as P

HD = 96


norm_eps = 1e-05
masked_value = -1e30


def rotary(values, position):
    half_dim = HD // 2
    freqs = 10000.0 ** (-(jnp.arange(half_dim, dtype=jnp.float32) * 2.0) / HD)
    angles = position.astype(jnp.float32)[..., None] * freqs
    cosine = jnp.cos(angles)[..., None, :]
    sine = jnp.sin(angles)[..., None, :]
    first = values[..., :half_dim]
    second = values[..., half_dim:]
    return jnp.concatenate(
        [first * cosine - second * sine, second * cosine + first * sine], axis=-1
    )


def prompt_kernel(block_len, score_scale, valid_ref, q_ref, cache_ref, acc_ref, top_ref, sum_ref):
    number = pl.program_id(0)

    @pl.when(number == 0)
    def _():
        acc_ref[...] = jnp.zeros_like(acc_ref)
        top_ref[...] = jnp.full_like(top_ref, masked_value)
        sum_ref[...] = jnp.zeros_like(sum_ref)

    @pl.when(number * block_len < valid_ref[0])
    def _():
        keys = cache_ref[:, 0, :]
        values = cache_ref[:, 1, :]
        scores = (
            lax.dot_general(
                q_ref[...], keys, (((1,), (1,)), ((), ())), preferred_element_type=jnp.float32
            )
            * score_scale
        )
        places = number * block_len + lax.broadcasted_iota(jnp.int32, scores.shape, 1)
        scores = jnp.where(places < valid_ref[0], scores, masked_value)
        top_old = top_ref[...]
        top_new = jnp.maximum(top_old, jnp.max(scores, axis=1, keepdims=True))
        shrink = jnp.exp(top_old - top_new)
        weights = jnp.exp(scores - top_new)
        sum_ref[...] = shrink * sum_ref[...] + jnp.sum(weights, axis=1, keepdims=True)
        acc_ref[...] = shrink * acc_ref[...] + jnp.dot(
            weights.astype(jnp.bfloat16), values, preferred_element_type=jnp.float32
        )
        top_ref[...] = top_new


def prompt_attention(q_diag, cache, valid_count, score_scale):
    span = cache.shape[1]
    block_len = min(512, span)
    lanes = cache.shape[3]
    rows = q_diag.shape[0]

    def cache_block(number, valid):
        last = (valid[0] + block_len - 1) // block_len - 1
        return (0, jnp.maximum(jnp.minimum(number, last), 0), 0, 0)

    spec = pltpu.PrefetchScalarGridSpec(
        num_scalar_prefetch=1,
        grid=(span // block_len,),
        in_specs=[
            pl.BlockSpec((rows, lanes), lambda number, valid: (0, 0)),
            pl.BlockSpec((None, block_len, 2, lanes), cache_block),
        ],
        out_specs=[
            pl.BlockSpec((rows, lanes), lambda number, valid: (0, 0)),
            pl.BlockSpec((rows, 1), lambda number, valid: (0, 0)),
            pl.BlockSpec((rows, 1), lambda number, valid: (0, 0)),
        ],
    )
    return pl.pallas_call(
        functools.partial(prompt_kernel, block_len, score_scale),
        grid_spec=spec,
        out_shape=[
            jax.ShapeDtypeStruct((rows, lanes), jnp.float32),
            jax.ShapeDtypeStruct((rows, 1), jnp.float32),
            jax.ShapeDtypeStruct((rows, 1), jnp.float32),
        ],
    )(valid_count.reshape(1), q_diag, cache)


def tail_kernel(score_scale, lens_ref, q_ref, cache_ref, acc_ref, top_ref, sum_ref):
    number = pl.program_id(0)
    keys = cache_ref[:, 0, :]
    values = cache_ref[:, 1, :]
    scores = (
        lax.dot_general(q_ref[...], keys, (((1,), (1,)), ((), ())), preferred_element_type=jnp.float32)
        * score_scale
    )
    places = lax.broadcasted_iota(jnp.int32, scores.shape, 1)
    scores = jnp.where(places < lens_ref[number], scores, masked_value)
    top = jnp.max(scores, axis=1, keepdims=True)
    weights = jnp.exp(scores - top)
    top_ref[...] = top
    sum_ref[...] = jnp.sum(weights, axis=1, keepdims=True)
    acc_ref[...] = jnp.dot(weights.astype(jnp.bfloat16), values, preferred_element_type=jnp.float32)


def tail_attention(q_diag, cache, lens, score_scale):
    conts, rows, lanes = q_diag.shape
    cap = cache.shape[1]
    spec = pltpu.PrefetchScalarGridSpec(
        num_scalar_prefetch=1,
        grid=(conts,),
        in_specs=[
            pl.BlockSpec((None, rows, lanes), lambda number, lens: (number, 0, 0)),
            pl.BlockSpec((None, cap, 2, lanes), lambda number, lens: (number, 0, 0, 0)),
        ],
        out_specs=[
            pl.BlockSpec((None, rows, lanes), lambda number, lens: (number, 0, 0)),
            pl.BlockSpec((None, rows, 1), lambda number, lens: (number, 0, 0)),
            pl.BlockSpec((None, rows, 1), lambda number, lens: (number, 0, 0)),
        ],
    )
    return pl.pallas_call(
        functools.partial(tail_kernel, score_scale),
        grid_spec=spec,
        out_shape=[
            jax.ShapeDtypeStruct((conts, rows, lanes), jnp.float32),
            jax.ShapeDtypeStruct((conts, rows, 1), jnp.float32),
            jax.ShapeDtypeStruct((conts, rows, 1), jnp.float32),
        ],
    )(lens, q_diag, cache)


def per_device(
    new_qkv,
    prompt_cache,
    tail_cache,
    residual,
    w_out,
    mlp_gain,
    w_gate,
    w_up,
    w_down,
    final_gain,
    score_weight,
    slot_part,
    prompt_len,
    tail_len,
):
    req_count = lax.axis_size("req")
    req_index = lax.axis_index("req")
    mlp_index = lax.axis_index("mlp")
    rows_here = new_qkv.shape[0]
    width_here = new_qkv.shape[2]
    heads_here = width_here // HD
    conts_here = rows_here // 2
    width = w_out.shape[1]
    score_scale = 1.0 / math.sqrt(HD)
    own_prompt = req_index // 2
    tail_here = lax.dynamic_slice_in_dim(tail_len, req_index * conts_here, conts_here)
    plen_here = lax.dynamic_index_in_dim(prompt_len, own_prompt, 0, keepdims=False)
    position = plen_here + tail_here[:, None] + jnp.arange(2, dtype=jnp.int32)[None, :]
    block = new_qkv.reshape(conts_here, 2, 3, heads_here, HD)
    query = rotary(block[:, :, 0].astype(jnp.float32), position).astype(jnp.bfloat16)
    key_new = rotary(block[:, :, 1].astype(jnp.float32), position).astype(jnp.bfloat16)
    value_new = block[:, :, 2]
    gathered = lax.all_gather(query.reshape(rows_here, width_here), "req", axis=0, tiled=True)
    mlp_count = lax.axis_size("mlp")
    weights_cat = jnp.concatenate([w_gate, w_up, jnp.transpose(w_down)], axis=1)
    weights_all = jnp.stack(
        [weights_cat]
        + [
            lax.ppermute(
                weights_cat, "mlp", [(m, (m + shift) % mlp_count) for m in range(mlp_count)]
            )
            for shift in range(1, mlp_count)
        ]
    )
    slot_ids = jnp.arange(req_count, dtype=jnp.int32)
    slot_of = jnp.sum(
        jnp.where(slot_part[None, :] == slot_ids[:, None], slot_ids[None, :], 0), axis=1
    )
    held_part = lax.dynamic_index_in_dim(slot_part, req_index, 0, keepdims=False)
    owned_prompt = held_part // 2
    held_half = held_part % 2
    span = prompt_cache.shape[1]
    owned_rows = 2 * rows_here
    q_owned = lax.dynamic_slice_in_dim(gathered, owned_prompt * owned_rows, owned_rows, 0).reshape(
        owned_rows, heads_here, HD
    )
    owned_len = lax.dynamic_index_in_dim(prompt_len, owned_prompt, 0, keepdims=False)
    valid_count = jnp.clip(owned_len - held_half * span, 0, span)
    eye = jnp.eye(heads_here, dtype=jnp.bfloat16)
    q_diag = jnp.einsum("rhd,hg->hrgd", q_owned, eye).reshape(heads_here * owned_rows, width_here)
    prompt_acc, prompt_top, prompt_sum = prompt_attention(q_diag, prompt_cache, valid_count, score_scale)
    prompt_acc = prompt_acc.reshape(heads_here, owned_rows, heads_here, HD)
    owner_numer = jnp.stack([prompt_acc[h, :, h, :] for h in range(heads_here)], axis=1)
    owner_total = prompt_sum.reshape(heads_here, owned_rows)
    prefix_max = prompt_top.reshape(heads_here, owned_rows)
    packed = jnp.concatenate(
        [
            owner_numer.reshape(owned_rows, width_here),
            jnp.transpose(owner_total),
            jnp.transpose(prefix_max),
        ],
        axis=1,
    )
    packed, weights_all = lax.optimization_barrier((packed, weights_all))
    packed_all = lax.all_gather(packed[None], "req", axis=0, tiled=True)
    row_offset = req_index % 2 * rows_here
    slot_first = lax.dynamic_index_in_dim(slot_of, 2 * own_prompt, 0, keepdims=False)
    slot_second = lax.dynamic_index_in_dim(slot_of, 2 * own_prompt + 1, 0, keepdims=False)

    def part_of(slot):
        piece = lax.dynamic_slice_in_dim(
            lax.dynamic_index_in_dim(packed_all, slot, 0, keepdims=False), row_offset, rows_here, 0
        )
        numer = piece[:, :width_here].reshape(rows_here, heads_here, HD)
        total = piece[:, width_here : width_here + heads_here]
        top = piece[:, width_here + heads_here :]
        return numer, total, top

    numer_first, total_first, max_first = part_of(slot_first)
    numer_second, total_second, max_second = part_of(slot_second)

    tail_diag = jnp.einsum("cthd,hg->chtgd", query, eye).reshape(
        conts_here, heads_here * 2, width_here
    )
    tail_acc, tail_top, tail_sum = tail_attention(tail_diag, tail_cache, tail_here, score_scale)
    tail_acc = tail_acc.reshape(conts_here, heads_here, 2, heads_here, HD)
    cache_numer = jnp.stack([tail_acc[:, h, :, h, :] for h in range(heads_here)], axis=2)
    cache_top = tail_top.reshape(conts_here, heads_here, 2)
    cache_sum = tail_sum.reshape(conts_here, heads_here, 2)
    s_new = (
        jnp.einsum("cthd,cuhd->chtu", query, key_new, preferred_element_type=jnp.float32)
        * score_scale
    )
    causal = jnp.arange(2)[None, :] <= jnp.arange(2)[:, None]
    s_new = jnp.where(causal[None, None, :, :], s_new, masked_value)
    tail_max = jnp.maximum(cache_top, jnp.max(s_new, -1))
    cache_scale = jnp.exp(cache_top - tail_max)
    w_new = jnp.exp(s_new - tail_max[..., None])
    numer_tail = cache_numer * jnp.transpose(cache_scale, (0, 2, 1))[..., None]
    numer_tail = numer_tail + jnp.einsum(
        "chtu,cuhd->cthd", w_new.astype(jnp.bfloat16), value_new, preferred_element_type=jnp.float32
    )
    numer_tail = numer_tail.reshape(rows_here, heads_here, HD)
    total_tail = jnp.transpose(cache_sum * cache_scale + jnp.sum(w_new, -1), (0, 2, 1)).reshape(
        rows_here, heads_here
    )
    max_tail = jnp.transpose(tail_max, (0, 2, 1)).reshape(rows_here, heads_here)
    row_max = jnp.maximum(jnp.maximum(max_first, max_second), max_tail)
    scale_first = jnp.exp(max_first - row_max)
    scale_second = jnp.exp(max_second - row_max)
    scale_tail = jnp.exp(max_tail - row_max)
    row_total = total_first * scale_first + total_second * scale_second + total_tail * scale_tail
    row_numer = (
        numer_first * scale_first[..., None]
        + numer_second * scale_second[..., None]
        + numer_tail * scale_tail[..., None]
    )
    attn = (row_numer / row_total[:, :, None]).astype(jnp.bfloat16).reshape(rows_here, width_here)
    partial = jnp.dot(attn, w_out, preferred_element_type=jnp.float32)
    col_start = mlp_index * width_here
    own_cols = lax.dynamic_slice_in_dim(partial, col_start, width_here, 1)
    partial = lax.dynamic_update_slice_in_dim(
        partial, own_cols + residual.astype(jnp.float32), col_start, 1
    )
    state = lax.psum(partial, "mlp")
    mean_square = jnp.mean(state * state, axis=1, keepdims=True)
    normed = (state * lax.rsqrt(mean_square + norm_eps) * mlp_gain).astype(jnp.bfloat16)
    share = rows_here // mlp_count
    normed_share = lax.dynamic_slice_in_dim(normed, mlp_index * share, share, 0)
    piece = lax.all_gather(normed_share, "req", axis=0, tiled=True)
    hidden_here = w_gate.shape[1]
    gate_w = weights_all[:, :, :hidden_here]
    up_w = weights_all[:, :, hidden_here : 2 * hidden_here]
    down_w = weights_all[:, :, 2 * hidden_here :]
    gate = jnp.einsum("rk,mkj->rmj", piece, gate_w, preferred_element_type=jnp.float32)
    upper = jnp.einsum("rk,mkj->rmj", piece, up_w, preferred_element_type=jnp.float32)
    hidden_all = (jax.nn.silu(gate) * upper).astype(jnp.bfloat16)
    down_sum = jnp.einsum("rmj,mfj->rf", hidden_all, down_w, preferred_element_type=jnp.float32)
    row_sums = lax.psum_scatter(
        down_sum,
        "req",
        scatter_dimension=0,
        tiled=True,
    )
    state_share = lax.dynamic_slice_in_dim(state, mlp_index * share, share, 0)
    final_share = state_share + row_sums
    final_square = jnp.mean(final_share * final_share, axis=1)
    final_dot = jnp.sum(final_share * final_gain * score_weight, axis=1)
    score_share = final_dot * lax.rsqrt(final_square + norm_eps)
    payload = jnp.concatenate(
        [
            final_share.reshape(share, mlp_count, width_here),
            jnp.broadcast_to(score_share[:, None, None], (share, mlp_count, 1)),
        ],
        axis=2,
    )
    arrived = lax.all_to_all(payload, "mlp", split_axis=1, concat_axis=0, tiled=True)
    out_rows = arrived[:, 0, :width_here].astype(jnp.bfloat16)
    scores = arrived[:, 0, width_here]
    return (out_rows, scores)


def solution(mesh):
    in_specs = (
        P("req", None, "mlp"),
        P("req", None, None, "mlp"),
        P("req", None, None, "mlp"),
        P("req", "mlp"),
        P("mlp", None),
        P(),
        P(None, ("req", "mlp")),
        P(None, ("req", "mlp")),
        P(("req", "mlp"), None),
        P(),
        P(),
        P(),
        P(),
        P(),
    )
    out_specs = (P("req", "mlp"), P("req"))
    return jax.shard_map(
        per_device, mesh=mesh, in_specs=in_specs, out_specs=out_specs, check_vma=False
    )
```

```python
import functools
import math

import jax
import jax.numpy as jnp
from jax import lax
from jax.experimental import pallas as pl
from jax.experimental.pallas import tpu as pltpu
from jax.sharding import PartitionSpec as P

HD = 96


norm_eps = 1e-05
masked_value = -1e30


def rotary(values, position):
    half_dim = HD // 2
    freqs = 10000.0 ** (-(jnp.arange(half_dim, dtype=jnp.float32) * 2.0) / HD)
    angles = position.astype(jnp.float32)[..., None] * freqs
    cosine = jnp.cos(angles)[..., None, :]
    sine = jnp.sin(angles)[..., None, :]
    first = values[..., :half_dim]
    second = values[..., half_dim:]
    return jnp.concatenate(
        [first * cosine - second * sine, second * cosine + first * sine], axis=-1
    )


def prompt_kernel(block_len, score_scale, valid_ref, q_ref, cache_ref, acc_ref, top_ref, sum_ref):
    number = pl.program_id(0)

    @pl.when(number == 0)
    def _():
        acc_ref[...] = jnp.zeros_like(acc_ref)
        top_ref[...] = jnp.full_like(top_ref, masked_value)
        sum_ref[...] = jnp.zeros_like(sum_ref)

    @pl.when(number * block_len < valid_ref[0])
    def _():
        keys = cache_ref[:, 0, :]
        values = cache_ref[:, 1, :]
        scores = (
            lax.dot_general(
                q_ref[...], keys, (((1,), (1,)), ((), ())), preferred_element_type=jnp.float32
            )
            * score_scale
        )
        places = number * block_len + lax.broadcasted_iota(jnp.int32, scores.shape, 1)
        scores = jnp.where(places < valid_ref[0], scores, masked_value)
        top_old = top_ref[...]
        top_new = jnp.maximum(top_old, jnp.max(scores, axis=1, keepdims=True))
        shrink = jnp.exp(top_old - top_new)
        weights = jnp.exp(scores - top_new)
        sum_ref[...] = shrink * sum_ref[...] + jnp.sum(weights, axis=1, keepdims=True)
        acc_ref[...] = shrink * acc_ref[...] + jnp.dot(
            weights.astype(jnp.bfloat16), values, preferred_element_type=jnp.float32
        )
        top_ref[...] = top_new


def prompt_attention(q_diag, cache, valid_count, score_scale):
    span = cache.shape[1]
    block_len = min(512, span)
    lanes = cache.shape[3]
    rows = q_diag.shape[0]

    def cache_block(number, valid):
        last = (valid[0] + block_len - 1) // block_len - 1
        return (0, jnp.maximum(jnp.minimum(number, last), 0), 0, 0)

    spec = pltpu.PrefetchScalarGridSpec(
        num_scalar_prefetch=1,
        grid=(span // block_len,),
        in_specs=[
            pl.BlockSpec((rows, lanes), lambda number, valid: (0, 0)),
            pl.BlockSpec((None, block_len, 2, lanes), cache_block),
        ],
        out_specs=[
            pl.BlockSpec((rows, lanes), lambda number, valid: (0, 0)),
            pl.BlockSpec((rows, 1), lambda number, valid: (0, 0)),
            pl.BlockSpec((rows, 1), lambda number, valid: (0, 0)),
        ],
    )
    return pl.pallas_call(
        functools.partial(prompt_kernel, block_len, score_scale),
        grid_spec=spec,
        cost_estimate=pl.CostEstimate(
            flops=4 * rows * lanes * span,
            transcendentals=rows * span,
            bytes_accessed=cache.size * 2 + rows * lanes * 6,
        ),
        out_shape=[
            jax.ShapeDtypeStruct((rows, lanes), jnp.float32),
            jax.ShapeDtypeStruct((rows, 1), jnp.float32),
            jax.ShapeDtypeStruct((rows, 1), jnp.float32),
        ],
    )(valid_count.reshape(1), q_diag, cache)


def tail_kernel(score_scale, lens_ref, q_ref, cache_ref, acc_ref, top_ref, sum_ref):
    number = pl.program_id(0)
    keys = cache_ref[:, 0, :]
    values = cache_ref[:, 1, :]
    scores = (
        lax.dot_general(q_ref[...], keys, (((1,), (1,)), ((), ())), preferred_element_type=jnp.float32)
        * score_scale
    )
    places = lax.broadcasted_iota(jnp.int32, scores.shape, 1)
    scores = jnp.where(places < lens_ref[number], scores, masked_value)
    top = jnp.max(scores, axis=1, keepdims=True)
    weights = jnp.exp(scores - top)
    top_ref[...] = top
    sum_ref[...] = jnp.sum(weights, axis=1, keepdims=True)
    acc_ref[...] = jnp.dot(weights.astype(jnp.bfloat16), values, preferred_element_type=jnp.float32)


def tail_attention(q_diag, cache, lens, score_scale):
    conts, rows, lanes = q_diag.shape
    cap = cache.shape[1]
    spec = pltpu.PrefetchScalarGridSpec(
        num_scalar_prefetch=1,
        grid=(conts,),
        in_specs=[
            pl.BlockSpec((None, rows, lanes), lambda number, lens: (number, 0, 0)),
            pl.BlockSpec((None, cap, 2, lanes), lambda number, lens: (number, 0, 0, 0)),
        ],
        out_specs=[
            pl.BlockSpec((None, rows, lanes), lambda number, lens: (number, 0, 0)),
            pl.BlockSpec((None, rows, 1), lambda number, lens: (number, 0, 0)),
            pl.BlockSpec((None, rows, 1), lambda number, lens: (number, 0, 0)),
        ],
    )
    return pl.pallas_call(
        functools.partial(tail_kernel, score_scale),
        grid_spec=spec,
        cost_estimate=pl.CostEstimate(
            flops=4 * conts * rows * lanes * cap,
            transcendentals=conts * rows * cap,
            bytes_accessed=cache.size * 2 + conts * rows * lanes * 6,
        ),
        out_shape=[
            jax.ShapeDtypeStruct((conts, rows, lanes), jnp.float32),
            jax.ShapeDtypeStruct((conts, rows, 1), jnp.float32),
            jax.ShapeDtypeStruct((conts, rows, 1), jnp.float32),
        ],
    )(lens, q_diag, cache)


def per_device(
    new_qkv,
    prompt_cache,
    tail_cache,
    residual,
    w_out,
    mlp_gain,
    w_gate,
    w_up,
    w_down,
    final_gain,
    score_weight,
    slot_part,
    prompt_len,
    tail_len,
):
    req_count = lax.axis_size("req")
    req_index = lax.axis_index("req")
    mlp_index = lax.axis_index("mlp")
    rows_here = new_qkv.shape[0]
    width_here = new_qkv.shape[2]
    heads_here = width_here // HD
    conts_here = rows_here // 2
    width = w_out.shape[1]
    score_scale = 1.0 / math.sqrt(HD)
    own_prompt = req_index // 2
    tail_here = lax.dynamic_slice_in_dim(tail_len, req_index * conts_here, conts_here)
    plen_here = lax.dynamic_index_in_dim(prompt_len, own_prompt, 0, keepdims=False)
    position = plen_here + tail_here[:, None] + jnp.arange(2, dtype=jnp.int32)[None, :]
    block = new_qkv.reshape(conts_here, 2, 3, heads_here, HD)
    query = rotary(block[:, :, 0].astype(jnp.float32), position).astype(jnp.bfloat16)
    key_new = rotary(block[:, :, 1].astype(jnp.float32), position).astype(jnp.bfloat16)
    value_new = block[:, :, 2]
    gathered = lax.all_gather(query.reshape(rows_here, width_here), "req", axis=0, tiled=True)
    mlp_count = lax.axis_size("mlp")
    weights_cat = jnp.concatenate([w_gate, w_up, jnp.transpose(w_down)], axis=1)
    weights_all = jnp.stack(
        [weights_cat]
        + [
            lax.ppermute(
                weights_cat, "mlp", [(m, (m + shift) % mlp_count) for m in range(mlp_count)]
            )
            for shift in range(1, mlp_count)
        ]
    )
    slot_ids = jnp.arange(req_count, dtype=jnp.int32)
    slot_of = jnp.sum(
        jnp.where(slot_part[None, :] == slot_ids[:, None], slot_ids[None, :], 0), axis=1
    )
    held_part = lax.dynamic_index_in_dim(slot_part, req_index, 0, keepdims=False)
    owned_prompt = held_part // 2
    held_half = held_part % 2
    span = prompt_cache.shape[1]
    owned_rows = 2 * rows_here
    q_owned = lax.dynamic_slice_in_dim(gathered, owned_prompt * owned_rows, owned_rows, 0).reshape(
        owned_rows, heads_here, HD
    )
    owned_len = lax.dynamic_index_in_dim(prompt_len, owned_prompt, 0, keepdims=False)
    valid_count = jnp.clip(owned_len - held_half * span, 0, span)
    eye = jnp.eye(heads_here, dtype=jnp.bfloat16)
    q_diag = jnp.einsum("rhd,hg->hrgd", q_owned, eye).reshape(heads_here * owned_rows, width_here)
    prompt_acc, prompt_top, prompt_sum = prompt_attention(q_diag, prompt_cache, valid_count, score_scale)
    prompt_acc = prompt_acc.reshape(heads_here, owned_rows, heads_here, HD)
    owner_numer = jnp.stack([prompt_acc[h, :, h, :] for h in range(heads_here)], axis=1)
    owner_total = prompt_sum.reshape(heads_here, owned_rows)
    prefix_max = prompt_top.reshape(heads_here, owned_rows)
    packed = jnp.concatenate(
        [
            owner_numer.reshape(owned_rows, width_here),
            jnp.transpose(owner_total),
            jnp.transpose(prefix_max),
        ],
        axis=1,
    )
    packed_all = lax.all_gather(packed[None], "req", axis=0, tiled=True)
    row_offset = req_index % 2 * rows_here
    slot_first = lax.dynamic_index_in_dim(slot_of, 2 * own_prompt, 0, keepdims=False)
    slot_second = lax.dynamic_index_in_dim(slot_of, 2 * own_prompt + 1, 0, keepdims=False)

    def part_of(slot):
        piece = lax.dynamic_slice_in_dim(
            lax.dynamic_index_in_dim(packed_all, slot, 0, keepdims=False), row_offset, rows_here, 0
        )
        numer = piece[:, :width_here].reshape(rows_here, heads_here, HD)
        total = piece[:, width_here : width_here + heads_here]
        top = piece[:, width_here + heads_here :]
        return numer, total, top

    numer_first, total_first, max_first = part_of(slot_first)
    numer_second, total_second, max_second = part_of(slot_second)

    tail_diag = jnp.einsum("cthd,hg->chtgd", query, eye).reshape(
        conts_here, heads_here * 2, width_here
    )
    tail_acc, tail_top, tail_sum = tail_attention(tail_diag, tail_cache, tail_here, score_scale)
    tail_acc = tail_acc.reshape(conts_here, heads_here, 2, heads_here, HD)
    cache_numer = jnp.stack([tail_acc[:, h, :, h, :] for h in range(heads_here)], axis=2)
    cache_top = tail_top.reshape(conts_here, heads_here, 2)
    cache_sum = tail_sum.reshape(conts_here, heads_here, 2)
    s_new = (
        jnp.einsum("cthd,cuhd->chtu", query, key_new, preferred_element_type=jnp.float32)
        * score_scale
    )
    causal = jnp.arange(2)[None, :] <= jnp.arange(2)[:, None]
    s_new = jnp.where(causal[None, None, :, :], s_new, masked_value)
    tail_max = jnp.maximum(cache_top, jnp.max(s_new, -1))
    cache_scale = jnp.exp(cache_top - tail_max)
    w_new = jnp.exp(s_new - tail_max[..., None])
    numer_tail = cache_numer * jnp.transpose(cache_scale, (0, 2, 1))[..., None]
    numer_tail = numer_tail + jnp.einsum(
        "chtu,cuhd->cthd", w_new.astype(jnp.bfloat16), value_new, preferred_element_type=jnp.float32
    )
    numer_tail = numer_tail.reshape(rows_here, heads_here, HD)
    total_tail = jnp.transpose(cache_sum * cache_scale + jnp.sum(w_new, -1), (0, 2, 1)).reshape(
        rows_here, heads_here
    )
    max_tail = jnp.transpose(tail_max, (0, 2, 1)).reshape(rows_here, heads_here)
    row_max = jnp.maximum(jnp.maximum(max_first, max_second), max_tail)
    scale_first = jnp.exp(max_first - row_max)
    scale_second = jnp.exp(max_second - row_max)
    scale_tail = jnp.exp(max_tail - row_max)
    row_total = total_first * scale_first + total_second * scale_second + total_tail * scale_tail
    row_numer = (
        numer_first * scale_first[..., None]
        + numer_second * scale_second[..., None]
        + numer_tail * scale_tail[..., None]
    )
    attn = (row_numer / row_total[:, :, None]).astype(jnp.bfloat16).reshape(rows_here, width_here)
    attn, weights_all = lax.optimization_barrier((attn, weights_all))
    partial = jnp.dot(attn, w_out, preferred_element_type=jnp.float32)
    col_start = mlp_index * width_here
    own_cols = lax.dynamic_slice_in_dim(partial, col_start, width_here, 1)
    partial = lax.dynamic_update_slice_in_dim(
        partial, own_cols + residual.astype(jnp.float32), col_start, 1
    )
    share = rows_here // mlp_count
    state_share = lax.dynamic_slice_in_dim(partial, mlp_index * share, share, 0)
    for shift in range(1, mlp_count):
        target = (mlp_index + shift) % mlp_count
        state_share = state_share + lax.ppermute(
            lax.dynamic_slice_in_dim(partial, target * share, share, 0),
            "mlp",
            [(m, (m + shift) % mlp_count) for m in range(mlp_count)],
        )
    mean_square = jnp.mean(state_share * state_share, axis=1, keepdims=True)
    normed_share = (state_share * lax.rsqrt(mean_square + norm_eps) * mlp_gain).astype(jnp.bfloat16)
    piece = lax.all_gather(normed_share, "req", axis=0, tiled=True)
    hidden_here = w_gate.shape[1]
    gate_w = weights_all[:, :, :hidden_here]
    up_w = weights_all[:, :, hidden_here : 2 * hidden_here]
    down_w = weights_all[:, :, 2 * hidden_here :]
    gate = jnp.einsum("rk,mkj->rmj", piece, gate_w, preferred_element_type=jnp.float32)
    upper = jnp.einsum("rk,mkj->rmj", piece, up_w, preferred_element_type=jnp.float32)
    hidden_all = (jax.nn.silu(gate) * upper).astype(jnp.bfloat16)
    down_sum = jnp.einsum("rmj,mfj->rf", hidden_all, down_w, preferred_element_type=jnp.float32)
    row_sums = lax.psum_scatter(
        down_sum.astype(jnp.bfloat16),
        "req",
        scatter_dimension=0,
        tiled=True,
    )
    final_share = state_share + row_sums.astype(jnp.float32)
    final_square = jnp.mean(final_share * final_share, axis=1)
    final_dot = jnp.sum(final_share * final_gain * score_weight, axis=1)
    score_share = final_dot * lax.rsqrt(final_square + norm_eps)
    payload = jnp.concatenate(
        [
            final_share.reshape(share, mlp_count, width_here),
            jnp.broadcast_to(score_share[:, None, None], (share, mlp_count, 1)),
        ],
        axis=2,
    )
    arrived = lax.all_to_all(payload, "mlp", split_axis=1, concat_axis=0, tiled=True)
    out_rows = arrived[:, 0, :width_here].astype(jnp.bfloat16)
    scores = arrived[:, 0, width_here]
    return (out_rows, scores)


def solution(mesh):
    in_specs = (
        P("req", None, "mlp"),
        P("req", None, None, "mlp"),
        P("req", None, None, "mlp"),
        P("req", "mlp"),
        P("mlp", None),
        P(),
        P(None, ("req", "mlp")),
        P(None, ("req", "mlp")),
        P(("req", "mlp"), None),
        P(),
        P(),
        P(),
        P(),
        P(),
    )
    out_specs = (P("req", "mlp"), P("req"))
    return jax.shard_map(
        per_device, mesh=mesh, in_specs=in_specs, out_specs=out_specs, check_vma=False
    )
```

```python
import functools
import math

import jax
import jax.numpy as jnp
from jax import lax
from jax.experimental import pallas as pl
from jax.experimental.pallas import tpu as pltpu
from jax.sharding import PartitionSpec as P

HD = 96


norm_eps = 1e-05
masked_value = -1e30


def rotary(values, position):
    half_dim = HD // 2
    freqs = 10000.0 ** (-(jnp.arange(half_dim, dtype=jnp.float32) * 2.0) / HD)
    angles = position.astype(jnp.float32)[..., None] * freqs
    cosine = jnp.cos(angles)[..., None, :]
    sine = jnp.sin(angles)[..., None, :]
    first = values[..., :half_dim]
    second = values[..., half_dim:]
    return jnp.concatenate(
        [first * cosine - second * sine, second * cosine + first * sine], axis=-1
    )


def prompt_kernel(block_len, score_scale, valid_ref, q_ref, cache_ref, acc_ref, top_ref, sum_ref):
    number = pl.program_id(0)

    @pl.when(number == 0)
    def _():
        acc_ref[...] = jnp.zeros_like(acc_ref)
        top_ref[...] = jnp.full_like(top_ref, masked_value)
        sum_ref[...] = jnp.zeros_like(sum_ref)

    @pl.when(number * block_len < valid_ref[0])
    def _():
        keys = cache_ref[:, 0, :]
        values = cache_ref[:, 1, :]
        scores = (
            lax.dot_general(
                q_ref[...], keys, (((1,), (1,)), ((), ())), preferred_element_type=jnp.float32
            )
            * score_scale
        )
        places = number * block_len + lax.broadcasted_iota(jnp.int32, scores.shape, 1)
        scores = jnp.where(places < valid_ref[0], scores, masked_value)
        top_old = top_ref[...]
        top_new = jnp.maximum(top_old, jnp.max(scores, axis=1, keepdims=True))
        shrink = jnp.exp(top_old - top_new)
        weights = jnp.exp(scores - top_new)
        sum_ref[...] = shrink * sum_ref[...] + jnp.sum(weights, axis=1, keepdims=True)
        acc_ref[...] = shrink * acc_ref[...] + jnp.dot(
            weights.astype(jnp.bfloat16), values, preferred_element_type=jnp.float32
        )
        top_ref[...] = top_new


def prompt_attention(q_diag, cache, valid_count, score_scale):
    span = cache.shape[1]
    block_len = min(512, span)
    lanes = cache.shape[3]
    rows = q_diag.shape[0]

    def cache_block(number, valid):
        last = (valid[0] + block_len - 1) // block_len - 1
        return (0, jnp.maximum(jnp.minimum(number, last), 0), 0, 0)

    spec = pltpu.PrefetchScalarGridSpec(
        num_scalar_prefetch=1,
        grid=(span // block_len,),
        in_specs=[
            pl.BlockSpec((rows, lanes), lambda number, valid: (0, 0)),
            pl.BlockSpec((None, block_len, 2, lanes), cache_block),
        ],
        out_specs=[
            pl.BlockSpec((rows, lanes), lambda number, valid: (0, 0)),
            pl.BlockSpec((rows, 1), lambda number, valid: (0, 0)),
            pl.BlockSpec((rows, 1), lambda number, valid: (0, 0)),
        ],
    )
    return pl.pallas_call(
        functools.partial(prompt_kernel, block_len, score_scale),
        grid_spec=spec,
        cost_estimate=pl.CostEstimate(
            flops=4 * rows * lanes * span,
            transcendentals=rows * span,
            bytes_accessed=cache.size * 2 + rows * lanes * 6,
        ),
        out_shape=[
            jax.ShapeDtypeStruct((rows, lanes), jnp.float32),
            jax.ShapeDtypeStruct((rows, 1), jnp.float32),
            jax.ShapeDtypeStruct((rows, 1), jnp.float32),
        ],
    )(valid_count.reshape(1), q_diag, cache)


def tail_kernel(score_scale, lens_ref, q_ref, cache_ref, acc_ref, top_ref, sum_ref):
    number = pl.program_id(0)
    keys = cache_ref[:, 0, :]
    values = cache_ref[:, 1, :]
    scores = (
        lax.dot_general(q_ref[...], keys, (((1,), (1,)), ((), ())), preferred_element_type=jnp.float32)
        * score_scale
    )
    places = lax.broadcasted_iota(jnp.int32, scores.shape, 1)
    scores = jnp.where(places < lens_ref[number], scores, masked_value)
    top = jnp.max(scores, axis=1, keepdims=True)
    weights = jnp.exp(scores - top)
    top_ref[...] = top
    sum_ref[...] = jnp.sum(weights, axis=1, keepdims=True)
    acc_ref[...] = jnp.dot(weights.astype(jnp.bfloat16), values, preferred_element_type=jnp.float32)


def tail_attention(q_diag, cache, lens, score_scale):
    conts, rows, lanes = q_diag.shape
    cap = cache.shape[1]
    spec = pltpu.PrefetchScalarGridSpec(
        num_scalar_prefetch=1,
        grid=(conts,),
        in_specs=[
            pl.BlockSpec((None, rows, lanes), lambda number, lens: (number, 0, 0)),
            pl.BlockSpec((None, cap, 2, lanes), lambda number, lens: (number, 0, 0, 0)),
        ],
        out_specs=[
            pl.BlockSpec((None, rows, lanes), lambda number, lens: (number, 0, 0)),
            pl.BlockSpec((None, rows, 1), lambda number, lens: (number, 0, 0)),
            pl.BlockSpec((None, rows, 1), lambda number, lens: (number, 0, 0)),
        ],
    )
    return pl.pallas_call(
        functools.partial(tail_kernel, score_scale),
        grid_spec=spec,
        cost_estimate=pl.CostEstimate(
            flops=4 * conts * rows * lanes * cap,
            transcendentals=conts * rows * cap,
            bytes_accessed=cache.size * 2 + conts * rows * lanes * 6,
        ),
        out_shape=[
            jax.ShapeDtypeStruct((conts, rows, lanes), jnp.float32),
            jax.ShapeDtypeStruct((conts, rows, 1), jnp.float32),
            jax.ShapeDtypeStruct((conts, rows, 1), jnp.float32),
        ],
    )(lens, q_diag, cache)


def per_device(
    new_qkv,
    prompt_cache,
    tail_cache,
    residual,
    w_out,
    mlp_gain,
    w_gate,
    w_up,
    w_down,
    final_gain,
    score_weight,
    slot_part,
    prompt_len,
    tail_len,
):
    req_count = lax.axis_size("req")
    req_index = lax.axis_index("req")
    mlp_index = lax.axis_index("mlp")
    rows_here = new_qkv.shape[0]
    width_here = new_qkv.shape[2]
    heads_here = width_here // HD
    conts_here = rows_here // 2
    width = w_out.shape[1]
    score_scale = 1.0 / math.sqrt(HD)
    own_prompt = req_index // 2
    tail_here = lax.dynamic_slice_in_dim(tail_len, req_index * conts_here, conts_here)
    plen_here = lax.dynamic_index_in_dim(prompt_len, own_prompt, 0, keepdims=False)
    position = plen_here + tail_here[:, None] + jnp.arange(2, dtype=jnp.int32)[None, :]
    block = new_qkv.reshape(conts_here, 2, 3, heads_here, HD)
    query = rotary(block[:, :, 0].astype(jnp.float32), position).astype(jnp.bfloat16)
    key_new = rotary(block[:, :, 1].astype(jnp.float32), position).astype(jnp.bfloat16)
    value_new = block[:, :, 2]
    gathered = lax.all_gather(query.reshape(rows_here, width_here), "req", axis=0, tiled=True)
    mlp_count = lax.axis_size("mlp")
    weights_cat = jnp.concatenate([w_gate, w_up, jnp.transpose(w_down)], axis=1)
    weights_all = jnp.stack(
        [weights_cat]
        + [
            lax.ppermute(
                weights_cat, "mlp", [(m, (m + shift) % mlp_count) for m in range(mlp_count)]
            )
            for shift in range(1, mlp_count)
        ]
    )
    slot_ids = jnp.arange(req_count, dtype=jnp.int32)
    slot_of = jnp.sum(
        jnp.where(slot_part[None, :] == slot_ids[:, None], slot_ids[None, :], 0), axis=1
    )
    held_part = lax.dynamic_index_in_dim(slot_part, req_index, 0, keepdims=False)
    owned_prompt = held_part // 2
    held_half = held_part % 2
    span = prompt_cache.shape[1]
    owned_rows = 2 * rows_here
    q_owned = lax.dynamic_slice_in_dim(gathered, owned_prompt * owned_rows, owned_rows, 0).reshape(
        owned_rows, heads_here, HD
    )
    owned_len = lax.dynamic_index_in_dim(prompt_len, owned_prompt, 0, keepdims=False)
    valid_count = jnp.clip(owned_len - held_half * span, 0, span)
    eye = jnp.eye(heads_here, dtype=jnp.bfloat16)
    q_diag = jnp.einsum("rhd,hg->hrgd", q_owned, eye).reshape(heads_here * owned_rows, width_here)
    prompt_acc, prompt_top, prompt_sum = prompt_attention(q_diag, prompt_cache, valid_count, score_scale)
    prompt_acc = prompt_acc.reshape(heads_here, owned_rows, heads_here, HD)
    owner_numer = jnp.stack([prompt_acc[h, :, h, :] for h in range(heads_here)], axis=1)
    owner_total = prompt_sum.reshape(heads_here, owned_rows)
    prefix_max = prompt_top.reshape(heads_here, owned_rows)
    packed = jnp.concatenate(
        [
            owner_numer.reshape(owned_rows, width_here),
            jnp.transpose(owner_total),
            jnp.transpose(prefix_max),
        ],
        axis=1,
    )
    packed_all = lax.all_gather(packed[None], "req", axis=0, tiled=True)
    row_offset = req_index % 2 * rows_here
    slot_first = lax.dynamic_index_in_dim(slot_of, 2 * own_prompt, 0, keepdims=False)
    slot_second = lax.dynamic_index_in_dim(slot_of, 2 * own_prompt + 1, 0, keepdims=False)

    def part_of(slot):
        piece = lax.dynamic_slice_in_dim(
            lax.dynamic_index_in_dim(packed_all, slot, 0, keepdims=False), row_offset, rows_here, 0
        )
        numer = piece[:, :width_here].reshape(rows_here, heads_here, HD)
        total = piece[:, width_here : width_here + heads_here]
        top = piece[:, width_here + heads_here :]
        return numer, total, top

    numer_first, total_first, max_first = part_of(slot_first)
    numer_second, total_second, max_second = part_of(slot_second)

    tail_diag = jnp.einsum("cthd,hg->chtgd", query, eye).reshape(
        conts_here, heads_here * 2, width_here
    )
    tail_acc, tail_top, tail_sum = tail_attention(tail_diag, tail_cache, tail_here, score_scale)
    tail_acc = tail_acc.reshape(conts_here, heads_here, 2, heads_here, HD)
    cache_numer = jnp.stack([tail_acc[:, h, :, h, :] for h in range(heads_here)], axis=2)
    cache_top = tail_top.reshape(conts_here, heads_here, 2)
    cache_sum = tail_sum.reshape(conts_here, heads_here, 2)
    s_new = (
        jnp.einsum("cthd,cuhd->chtu", query, key_new, preferred_element_type=jnp.float32)
        * score_scale
    )
    causal = jnp.arange(2)[None, :] <= jnp.arange(2)[:, None]
    s_new = jnp.where(causal[None, None, :, :], s_new, masked_value)
    tail_max = jnp.maximum(cache_top, jnp.max(s_new, -1))
    cache_scale = jnp.exp(cache_top - tail_max)
    w_new = jnp.exp(s_new - tail_max[..., None])
    numer_tail = cache_numer * jnp.transpose(cache_scale, (0, 2, 1))[..., None]
    numer_tail = numer_tail + jnp.einsum(
        "chtu,cuhd->cthd", w_new.astype(jnp.bfloat16), value_new, preferred_element_type=jnp.float32
    )
    numer_tail = numer_tail.reshape(rows_here, heads_here, HD)
    total_tail = jnp.transpose(cache_sum * cache_scale + jnp.sum(w_new, -1), (0, 2, 1)).reshape(
        rows_here, heads_here
    )
    max_tail = jnp.transpose(tail_max, (0, 2, 1)).reshape(rows_here, heads_here)
    row_max = jnp.maximum(jnp.maximum(max_first, max_second), max_tail)
    scale_first = jnp.exp(max_first - row_max)
    scale_second = jnp.exp(max_second - row_max)
    scale_tail = jnp.exp(max_tail - row_max)
    row_total = total_first * scale_first + total_second * scale_second + total_tail * scale_tail
    row_numer = (
        numer_first * scale_first[..., None]
        + numer_second * scale_second[..., None]
        + numer_tail * scale_tail[..., None]
    )
    attn = (row_numer / row_total[:, :, None]).astype(jnp.bfloat16).reshape(rows_here, width_here)
    attn, weights_all = lax.optimization_barrier((attn, weights_all))
    partial = jnp.dot(attn, w_out, preferred_element_type=jnp.float32)
    col_start = mlp_index * width_here
    own_cols = lax.dynamic_slice_in_dim(partial, col_start, width_here, 1)
    partial = lax.dynamic_update_slice_in_dim(
        partial, own_cols + residual.astype(jnp.float32), col_start, 1
    )
    share = rows_here // mlp_count
    state_share = lax.dynamic_slice_in_dim(partial, mlp_index * share, share, 0)
    for shift in range(1, mlp_count):
        target = (mlp_index + shift) % mlp_count
        state_share = state_share + lax.ppermute(
            lax.dynamic_slice_in_dim(partial, target * share, share, 0),
            "mlp",
            [(m, (m + shift) % mlp_count) for m in range(mlp_count)],
        )
    mean_square = jnp.mean(state_share * state_share, axis=1, keepdims=True)
    normed_share = (state_share * lax.rsqrt(mean_square + norm_eps) * mlp_gain).astype(jnp.bfloat16)
    piece = lax.all_to_all(
        jnp.broadcast_to(normed_share[None], (req_count,) + normed_share.shape),
        "req",
        split_axis=0,
        concat_axis=0,
        tiled=True,
    ).reshape(req_count * share, width)
    hidden_here = w_gate.shape[1]
    gate_w = weights_all[:, :, :hidden_here]
    up_w = weights_all[:, :, hidden_here : 2 * hidden_here]
    down_w = weights_all[:, :, 2 * hidden_here :]
    gate = jnp.einsum("rk,mkj->rmj", piece, gate_w, preferred_element_type=jnp.float32)
    upper = jnp.einsum("rk,mkj->rmj", piece, up_w, preferred_element_type=jnp.float32)
    hidden_all = (jax.nn.silu(gate) * upper).astype(jnp.bfloat16)
    down_sum = jnp.einsum("rmj,mfj->rf", hidden_all, down_w, preferred_element_type=jnp.float32)
    row_sums = jnp.sum(
        lax.all_to_all(
            down_sum.reshape(req_count, share, width), "req", split_axis=0, concat_axis=0, tiled=True
        ),
        axis=0,
    )
    final_share = state_share + row_sums
    final_square = jnp.mean(final_share * final_share, axis=1)
    final_dot = jnp.sum(final_share * final_gain * score_weight, axis=1)
    score_share = final_dot * lax.rsqrt(final_square + norm_eps)
    payload = jnp.concatenate(
        [
            final_share.reshape(share, mlp_count, width_here),
            jnp.broadcast_to(score_share[:, None, None], (share, mlp_count, 1)),
        ],
        axis=2,
    )
    arrived = lax.all_to_all(payload, "mlp", split_axis=1, concat_axis=0, tiled=True)
    out_rows = arrived[:, 0, :width_here].astype(jnp.bfloat16)
    scores = arrived[:, 0, width_here]
    return (out_rows, scores)


def solution(mesh):
    in_specs = (
        P("req", None, "mlp"),
        P("req", None, None, "mlp"),
        P("req", None, None, "mlp"),
        P("req", "mlp"),
        P("mlp", None),
        P(),
        P(None, ("req", "mlp")),
        P(None, ("req", "mlp")),
        P(("req", "mlp"), None),
        P(),
        P(),
        P(),
        P(),
        P(),
    )
    out_specs = (P("req", "mlp"), P("req"))
    return jax.shard_map(
        per_device, mesh=mesh, in_specs=in_specs, out_specs=out_specs, check_vma=False
    )
```

```python
import functools
import math

import jax
import jax.numpy as jnp
from jax import lax
from jax.experimental import pallas as pl
from jax.experimental.pallas import tpu as pltpu
from jax.sharding import PartitionSpec as P

HD = 96


norm_eps = 1e-05
masked_value = -1e30


def rotary(values, position):
    half_dim = HD // 2
    freqs = 10000.0 ** (-(jnp.arange(half_dim, dtype=jnp.float32) * 2.0) / HD)
    angles = position.astype(jnp.float32)[..., None] * freqs
    cosine = jnp.cos(angles)[..., None, :]
    sine = jnp.sin(angles)[..., None, :]
    first = values[..., :half_dim]
    second = values[..., half_dim:]
    return jnp.concatenate(
        [first * cosine - second * sine, second * cosine + first * sine], axis=-1
    )


def prompt_kernel(block_len, score_scale, valid_ref, q_ref, cache_ref, acc_ref, top_ref, sum_ref):
    number = pl.program_id(0)

    @pl.when(number == 0)
    def _():
        acc_ref[...] = jnp.zeros_like(acc_ref)
        top_ref[...] = jnp.full_like(top_ref, masked_value)
        sum_ref[...] = jnp.zeros_like(sum_ref)

    @pl.when(number * block_len < valid_ref[0])
    def _():
        keys = cache_ref[:, 0, :]
        values = cache_ref[:, 1, :]
        scores = (
            lax.dot_general(
                q_ref[...], keys, (((1,), (1,)), ((), ())), preferred_element_type=jnp.float32
            )
            * score_scale
        )
        places = number * block_len + lax.broadcasted_iota(jnp.int32, scores.shape, 1)
        scores = jnp.where(places < valid_ref[0], scores, masked_value)
        top_old = top_ref[...]
        top_new = jnp.maximum(top_old, jnp.max(scores, axis=1, keepdims=True))
        shrink = jnp.exp(top_old - top_new)
        weights = jnp.exp(scores - top_new)
        sum_ref[...] = shrink * sum_ref[...] + jnp.sum(weights, axis=1, keepdims=True)
        acc_ref[...] = shrink * acc_ref[...] + jnp.dot(
            weights.astype(jnp.bfloat16), values, preferred_element_type=jnp.float32
        )
        top_ref[...] = top_new


def prompt_attention(q_diag, cache, valid_count, score_scale):
    span = cache.shape[1]
    block_len = min(512, span)
    lanes = cache.shape[3]
    rows = q_diag.shape[0]

    def cache_block(number, valid):
        last = (valid[0] + block_len - 1) // block_len - 1
        return (0, jnp.maximum(jnp.minimum(number, last), 0), 0, 0)

    spec = pltpu.PrefetchScalarGridSpec(
        num_scalar_prefetch=1,
        grid=(span // block_len,),
        in_specs=[
            pl.BlockSpec((rows, lanes), lambda number, valid: (0, 0)),
            pl.BlockSpec((None, block_len, 2, lanes), cache_block),
        ],
        out_specs=[
            pl.BlockSpec((rows, lanes), lambda number, valid: (0, 0)),
            pl.BlockSpec((rows, 1), lambda number, valid: (0, 0)),
            pl.BlockSpec((rows, 1), lambda number, valid: (0, 0)),
        ],
    )
    return pl.pallas_call(
        functools.partial(prompt_kernel, block_len, score_scale),
        grid_spec=spec,
        cost_estimate=pl.CostEstimate(
            flops=4 * rows * lanes * span,
            transcendentals=rows * span,
            bytes_accessed=cache.size * 2 + rows * lanes * 6,
        ),
        out_shape=[
            jax.ShapeDtypeStruct((rows, lanes), jnp.float32),
            jax.ShapeDtypeStruct((rows, 1), jnp.float32),
            jax.ShapeDtypeStruct((rows, 1), jnp.float32),
        ],
    )(valid_count.reshape(1), q_diag, cache)


def tail_kernel(score_scale, lens_ref, q_ref, cache_ref, acc_ref, top_ref, sum_ref):
    number = pl.program_id(0)
    keys = cache_ref[:, 0, :]
    values = cache_ref[:, 1, :]
    scores = (
        lax.dot_general(q_ref[...], keys, (((1,), (1,)), ((), ())), preferred_element_type=jnp.float32)
        * score_scale
    )
    places = lax.broadcasted_iota(jnp.int32, scores.shape, 1)
    scores = jnp.where(places < lens_ref[number], scores, masked_value)
    top = jnp.max(scores, axis=1, keepdims=True)
    weights = jnp.exp(scores - top)
    top_ref[...] = top
    sum_ref[...] = jnp.sum(weights, axis=1, keepdims=True)
    acc_ref[...] = jnp.dot(weights.astype(jnp.bfloat16), values, preferred_element_type=jnp.float32)


def tail_attention(q_diag, cache, lens, score_scale):
    conts, rows, lanes = q_diag.shape
    cap = cache.shape[1]
    spec = pltpu.PrefetchScalarGridSpec(
        num_scalar_prefetch=1,
        grid=(conts,),
        in_specs=[
            pl.BlockSpec((None, rows, lanes), lambda number, lens: (number, 0, 0)),
            pl.BlockSpec((None, cap, 2, lanes), lambda number, lens: (number, 0, 0, 0)),
        ],
        out_specs=[
            pl.BlockSpec((None, rows, lanes), lambda number, lens: (number, 0, 0)),
            pl.BlockSpec((None, rows, 1), lambda number, lens: (number, 0, 0)),
            pl.BlockSpec((None, rows, 1), lambda number, lens: (number, 0, 0)),
        ],
    )
    return pl.pallas_call(
        functools.partial(tail_kernel, score_scale),
        grid_spec=spec,
        cost_estimate=pl.CostEstimate(
            flops=4 * conts * rows * lanes * cap,
            transcendentals=conts * rows * cap,
            bytes_accessed=cache.size * 2 + conts * rows * lanes * 6,
        ),
        out_shape=[
            jax.ShapeDtypeStruct((conts, rows, lanes), jnp.float32),
            jax.ShapeDtypeStruct((conts, rows, 1), jnp.float32),
            jax.ShapeDtypeStruct((conts, rows, 1), jnp.float32),
        ],
    )(lens, q_diag, cache)


def per_device(
    new_qkv,
    prompt_cache,
    tail_cache,
    residual,
    w_out,
    mlp_gain,
    w_gate,
    w_up,
    w_down,
    final_gain,
    score_weight,
    slot_part,
    prompt_len,
    tail_len,
):
    req_count = lax.axis_size("req")
    req_index = lax.axis_index("req")
    mlp_index = lax.axis_index("mlp")
    rows_here = new_qkv.shape[0]
    width_here = new_qkv.shape[2]
    heads_here = width_here // HD
    conts_here = rows_here // 2
    width = w_out.shape[1]
    score_scale = 1.0 / math.sqrt(HD)
    own_prompt = req_index // 2
    tail_here = lax.dynamic_slice_in_dim(tail_len, req_index * conts_here, conts_here)
    plen_here = lax.dynamic_index_in_dim(prompt_len, own_prompt, 0, keepdims=False)
    position = plen_here + tail_here[:, None] + jnp.arange(2, dtype=jnp.int32)[None, :]
    block = new_qkv.reshape(conts_here, 2, 3, heads_here, HD)
    query = rotary(block[:, :, 0].astype(jnp.float32), position).astype(jnp.bfloat16)
    key_new = rotary(block[:, :, 1].astype(jnp.float32), position).astype(jnp.bfloat16)
    value_new = block[:, :, 2]
    gathered = lax.all_gather(query.reshape(rows_here, width_here), "req", axis=0, tiled=True)
    eye = jnp.eye(heads_here, dtype=jnp.bfloat16)
    tail_diag = jnp.einsum("cthd,hg->chtgd", query, eye).reshape(
        conts_here, heads_here * 2, width_here
    )
    tail_acc, tail_top, tail_sum = tail_attention(tail_diag, tail_cache, tail_here, score_scale)
    gathered, tail_acc, tail_top, tail_sum = lax.optimization_barrier(
        (gathered, tail_acc, tail_top, tail_sum)
    )
    mlp_count = lax.axis_size("mlp")
    weights_cat = jnp.concatenate([w_gate, w_up, jnp.transpose(w_down)], axis=1)
    weights_all = jnp.stack(
        [weights_cat]
        + [
            lax.ppermute(
                weights_cat, "mlp", [(m, (m + shift) % mlp_count) for m in range(mlp_count)]
            )
            for shift in range(1, mlp_count)
        ]
    )
    slot_ids = jnp.arange(req_count, dtype=jnp.int32)
    slot_of = jnp.sum(
        jnp.where(slot_part[None, :] == slot_ids[:, None], slot_ids[None, :], 0), axis=1
    )
    held_part = lax.dynamic_index_in_dim(slot_part, req_index, 0, keepdims=False)
    owned_prompt = held_part // 2
    held_half = held_part % 2
    span = prompt_cache.shape[1]
    owned_rows = 2 * rows_here
    q_owned = lax.dynamic_slice_in_dim(gathered, owned_prompt * owned_rows, owned_rows, 0).reshape(
        owned_rows, heads_here, HD
    )
    owned_len = lax.dynamic_index_in_dim(prompt_len, owned_prompt, 0, keepdims=False)
    valid_count = jnp.clip(owned_len - held_half * span, 0, span)
    q_diag = jnp.einsum("rhd,hg->hrgd", q_owned, eye).reshape(heads_here * owned_rows, width_here)
    prompt_acc, prompt_top, prompt_sum = prompt_attention(q_diag, prompt_cache, valid_count, score_scale)
    prompt_acc = prompt_acc.reshape(heads_here, owned_rows, heads_here, HD)
    owner_numer = jnp.stack([prompt_acc[h, :, h, :] for h in range(heads_here)], axis=1)
    owner_total = prompt_sum.reshape(heads_here, owned_rows)
    prefix_max = prompt_top.reshape(heads_here, owned_rows)
    packed = jnp.concatenate(
        [
            owner_numer.reshape(owned_rows, width_here),
            jnp.transpose(owner_total),
            jnp.transpose(prefix_max),
        ],
        axis=1,
    )
    packed_all = lax.all_gather(packed[None], "req", axis=0, tiled=True)
    row_offset = req_index % 2 * rows_here
    slot_first = lax.dynamic_index_in_dim(slot_of, 2 * own_prompt, 0, keepdims=False)
    slot_second = lax.dynamic_index_in_dim(slot_of, 2 * own_prompt + 1, 0, keepdims=False)

    def part_of(slot):
        piece = lax.dynamic_slice_in_dim(
            lax.dynamic_index_in_dim(packed_all, slot, 0, keepdims=False), row_offset, rows_here, 0
        )
        numer = piece[:, :width_here].reshape(rows_here, heads_here, HD)
        total = piece[:, width_here : width_here + heads_here]
        top = piece[:, width_here + heads_here :]
        return numer, total, top

    numer_first, total_first, max_first = part_of(slot_first)
    numer_second, total_second, max_second = part_of(slot_second)

    tail_acc = tail_acc.reshape(conts_here, heads_here, 2, heads_here, HD)
    cache_numer = jnp.stack([tail_acc[:, h, :, h, :] for h in range(heads_here)], axis=2)
    cache_top = tail_top.reshape(conts_here, heads_here, 2)
    cache_sum = tail_sum.reshape(conts_here, heads_here, 2)
    s_new = (
        jnp.einsum("cthd,cuhd->chtu", query, key_new, preferred_element_type=jnp.float32)
        * score_scale
    )
    causal = jnp.arange(2)[None, :] <= jnp.arange(2)[:, None]
    s_new = jnp.where(causal[None, None, :, :], s_new, masked_value)
    tail_max = jnp.maximum(cache_top, jnp.max(s_new, -1))
    cache_scale = jnp.exp(cache_top - tail_max)
    w_new = jnp.exp(s_new - tail_max[..., None])
    numer_tail = cache_numer * jnp.transpose(cache_scale, (0, 2, 1))[..., None]
    numer_tail = numer_tail + jnp.einsum(
        "chtu,cuhd->cthd", w_new.astype(jnp.bfloat16), value_new, preferred_element_type=jnp.float32
    )
    numer_tail = numer_tail.reshape(rows_here, heads_here, HD)
    total_tail = jnp.transpose(cache_sum * cache_scale + jnp.sum(w_new, -1), (0, 2, 1)).reshape(
        rows_here, heads_here
    )
    max_tail = jnp.transpose(tail_max, (0, 2, 1)).reshape(rows_here, heads_here)
    row_max = jnp.maximum(jnp.maximum(max_first, max_second), max_tail)
    scale_first = jnp.exp(max_first - row_max)
    scale_second = jnp.exp(max_second - row_max)
    scale_tail = jnp.exp(max_tail - row_max)
    row_total = total_first * scale_first + total_second * scale_second + total_tail * scale_tail
    row_numer = (
        numer_first * scale_first[..., None]
        + numer_second * scale_second[..., None]
        + numer_tail * scale_tail[..., None]
    )
    attn = (row_numer / row_total[:, :, None]).astype(jnp.bfloat16).reshape(rows_here, width_here)
    attn, weights_all = lax.optimization_barrier((attn, weights_all))
    partial = jnp.dot(attn, w_out, preferred_element_type=jnp.float32)
    col_start = mlp_index * width_here
    own_cols = lax.dynamic_slice_in_dim(partial, col_start, width_here, 1)
    partial = lax.dynamic_update_slice_in_dim(
        partial, own_cols + residual.astype(jnp.float32), col_start, 1
    )
    share = rows_here // mlp_count
    state_share = lax.dynamic_slice_in_dim(partial, mlp_index * share, share, 0)
    for shift in range(1, mlp_count):
        target = (mlp_index + shift) % mlp_count
        state_share = state_share + lax.ppermute(
            lax.dynamic_slice_in_dim(partial, target * share, share, 0),
            "mlp",
            [(m, (m + shift) % mlp_count) for m in range(mlp_count)],
        )
    mean_square = jnp.mean(state_share * state_share, axis=1, keepdims=True)
    normed_share = (state_share * lax.rsqrt(mean_square + norm_eps) * mlp_gain).astype(jnp.bfloat16)
    piece = lax.all_to_all(
        jnp.broadcast_to(normed_share[None], (req_count,) + normed_share.shape),
        "req",
        split_axis=0,
        concat_axis=0,
        tiled=True,
    ).reshape(req_count * share, width)
    hidden_here = w_gate.shape[1]
    gate_w = weights_all[:, :, :hidden_here]
    up_w = weights_all[:, :, hidden_here : 2 * hidden_here]
    down_w = weights_all[:, :, 2 * hidden_here :]
    gate = jnp.einsum("rk,mkj->rmj", piece, gate_w, preferred_element_type=jnp.float32)
    upper = jnp.einsum("rk,mkj->rmj", piece, up_w, preferred_element_type=jnp.float32)
    hidden_all = (jax.nn.silu(gate) * upper).astype(jnp.bfloat16)
    down_sum = jnp.einsum("rmj,mfj->rf", hidden_all, down_w, preferred_element_type=jnp.float32)
    row_sums = jnp.sum(
        lax.all_to_all(
            down_sum.astype(jnp.bfloat16).reshape(req_count, share, width),
            "req",
            split_axis=0,
            concat_axis=0,
            tiled=True,
        ).astype(jnp.float32),
        axis=0,
    )
    final_share = state_share + row_sums
    final_square = jnp.mean(final_share * final_share, axis=1)
    final_dot = jnp.sum(final_share * final_gain * score_weight, axis=1)
    score_share = final_dot * lax.rsqrt(final_square + norm_eps)
    payload = jnp.concatenate(
        [
            final_share.reshape(share, mlp_count, width_here),
            jnp.broadcast_to(score_share[:, None, None], (share, mlp_count, 1)),
        ],
        axis=2,
    )
    arrived = lax.dynamic_update_slice_in_dim(
        jnp.zeros((rows_here, width_here + 1), jnp.float32),
        lax.dynamic_index_in_dim(payload, mlp_index, 1, keepdims=False),
        mlp_index * share,
        0,
    )
    for shift in range(1, mlp_count):
        target = (mlp_index + shift) % mlp_count
        source = (mlp_index + mlp_count - shift) % mlp_count
        got = lax.ppermute(
            lax.dynamic_index_in_dim(payload, target, 1, keepdims=False),
            "mlp",
            [(m, (m + shift) % mlp_count) for m in range(mlp_count)],
        )
        arrived = lax.dynamic_update_slice_in_dim(arrived, got, source * share, 0)
    out_rows = arrived[:, :width_here].astype(jnp.bfloat16)
    scores = arrived[:, width_here]
    return (out_rows, scores)


def solution(mesh):
    in_specs = (
        P("req", None, "mlp"),
        P("req", None, None, "mlp"),
        P("req", None, None, "mlp"),
        P("req", "mlp"),
        P("mlp", None),
        P(),
        P(None, ("req", "mlp")),
        P(None, ("req", "mlp")),
        P(("req", "mlp"), None),
        P(),
        P(),
        P(),
        P(),
        P(),
    )
    out_specs = (P("req", "mlp"), P("req"))
    return jax.shard_map(
        per_device, mesh=mesh, in_specs=in_specs, out_specs=out_specs, check_vma=False
    )
```

```python
import functools
import math

import jax
import jax.numpy as jnp
from jax import lax
from jax.experimental import pallas as pl
from jax.experimental.pallas import tpu as pltpu
from jax.sharding import PartitionSpec as P

HD = 96


norm_eps = 1e-05
masked_value = -1e30


def rotary(values, position):
    half_dim = HD // 2
    freqs = 10000.0 ** (-(jnp.arange(half_dim, dtype=jnp.float32) * 2.0) / HD)
    angles = position.astype(jnp.float32)[..., None] * freqs
    cosine = jnp.cos(angles)[..., None, :]
    sine = jnp.sin(angles)[..., None, :]
    first = values[..., :half_dim]
    second = values[..., half_dim:]
    return jnp.concatenate(
        [first * cosine - second * sine, second * cosine + first * sine], axis=-1
    )


def prompt_kernel(block_len, score_scale, valid_ref, q_ref, cache_ref, acc_ref, top_ref, sum_ref):
    number = pl.program_id(0)

    @pl.when(number == 0)
    def _():
        acc_ref[...] = jnp.zeros_like(acc_ref)
        top_ref[...] = jnp.full_like(top_ref, masked_value)
        sum_ref[...] = jnp.zeros_like(sum_ref)

    @pl.when(number * block_len < valid_ref[0])
    def _():
        keys = cache_ref[:, 0, :]
        values = cache_ref[:, 1, :]
        scores = (
            lax.dot_general(
                q_ref[...], keys, (((1,), (1,)), ((), ())), preferred_element_type=jnp.float32
            )
            * score_scale
        )
        places = number * block_len + lax.broadcasted_iota(jnp.int32, scores.shape, 1)
        scores = jnp.where(places < valid_ref[0], scores, masked_value)
        top_old = top_ref[...]
        top_new = jnp.maximum(top_old, jnp.max(scores, axis=1, keepdims=True))
        shrink = jnp.exp(top_old - top_new)
        weights = jnp.exp(scores - top_new)
        sum_ref[...] = shrink * sum_ref[...] + jnp.sum(weights, axis=1, keepdims=True)
        acc_ref[...] = shrink * acc_ref[...] + jnp.dot(
            weights.astype(jnp.bfloat16), values, preferred_element_type=jnp.float32
        )
        top_ref[...] = top_new


def prompt_attention(q_diag, cache, valid_count, score_scale):
    span = cache.shape[1]
    block_len = min(512, span)
    lanes = cache.shape[3]
    rows = q_diag.shape[0]

    def cache_block(number, valid):
        last = (valid[0] + block_len - 1) // block_len - 1
        return (0, jnp.maximum(jnp.minimum(number, last), 0), 0, 0)

    spec = pltpu.PrefetchScalarGridSpec(
        num_scalar_prefetch=1,
        grid=(span // block_len,),
        in_specs=[
            pl.BlockSpec((rows, lanes), lambda number, valid: (0, 0)),
            pl.BlockSpec((None, block_len, 2, lanes), cache_block),
        ],
        out_specs=[
            pl.BlockSpec((rows, lanes), lambda number, valid: (0, 0)),
            pl.BlockSpec((rows, 1), lambda number, valid: (0, 0)),
            pl.BlockSpec((rows, 1), lambda number, valid: (0, 0)),
        ],
    )
    return pl.pallas_call(
        functools.partial(prompt_kernel, block_len, score_scale),
        grid_spec=spec,
        cost_estimate=pl.CostEstimate(
            flops=4 * rows * lanes * span,
            transcendentals=rows * span,
            bytes_accessed=cache.size * 2 + rows * lanes * 6,
        ),
        out_shape=[
            jax.ShapeDtypeStruct((rows, lanes), jnp.float32),
            jax.ShapeDtypeStruct((rows, 1), jnp.float32),
            jax.ShapeDtypeStruct((rows, 1), jnp.float32),
        ],
    )(valid_count.reshape(1), q_diag, cache)


def tail_kernel(score_scale, lens_ref, q_ref, cache_ref, acc_ref, top_ref, sum_ref):
    number = pl.program_id(0)
    keys = cache_ref[:, 0, :]
    values = cache_ref[:, 1, :]
    scores = (
        lax.dot_general(q_ref[...], keys, (((1,), (1,)), ((), ())), preferred_element_type=jnp.float32)
        * score_scale
    )
    places = lax.broadcasted_iota(jnp.int32, scores.shape, 1)
    scores = jnp.where(places < lens_ref[number], scores, masked_value)
    top = jnp.max(scores, axis=1, keepdims=True)
    weights = jnp.exp(scores - top)
    top_ref[...] = top
    sum_ref[...] = jnp.sum(weights, axis=1, keepdims=True)
    acc_ref[...] = jnp.dot(weights.astype(jnp.bfloat16), values, preferred_element_type=jnp.float32)


def tail_attention(q_diag, cache, lens, score_scale):
    conts, rows, lanes = q_diag.shape
    cap = cache.shape[1]
    spec = pltpu.PrefetchScalarGridSpec(
        num_scalar_prefetch=1,
        grid=(conts,),
        in_specs=[
            pl.BlockSpec((None, rows, lanes), lambda number, lens: (number, 0, 0)),
            pl.BlockSpec((None, cap, 2, lanes), lambda number, lens: (number, 0, 0, 0)),
        ],
        out_specs=[
            pl.BlockSpec((None, rows, lanes), lambda number, lens: (number, 0, 0)),
            pl.BlockSpec((None, rows, 1), lambda number, lens: (number, 0, 0)),
            pl.BlockSpec((None, rows, 1), lambda number, lens: (number, 0, 0)),
        ],
    )
    return pl.pallas_call(
        functools.partial(tail_kernel, score_scale),
        grid_spec=spec,
        cost_estimate=pl.CostEstimate(
            flops=4 * conts * rows * lanes * cap,
            transcendentals=conts * rows * cap,
            bytes_accessed=cache.size * 2 + conts * rows * lanes * 6,
        ),
        out_shape=[
            jax.ShapeDtypeStruct((conts, rows, lanes), jnp.float32),
            jax.ShapeDtypeStruct((conts, rows, 1), jnp.float32),
            jax.ShapeDtypeStruct((conts, rows, 1), jnp.float32),
        ],
    )(lens, q_diag, cache)


def per_device(
    new_qkv,
    prompt_cache,
    tail_cache,
    residual,
    w_out,
    mlp_gain,
    w_gate,
    w_up,
    w_down,
    final_gain,
    score_weight,
    slot_part,
    prompt_len,
    tail_len,
):
    req_count = lax.axis_size("req")
    req_index = lax.axis_index("req")
    mlp_index = lax.axis_index("mlp")
    rows_here = new_qkv.shape[0]
    width_here = new_qkv.shape[2]
    heads_here = width_here // HD
    conts_here = rows_here // 2
    width = w_out.shape[1]
    score_scale = 1.0 / math.sqrt(HD)
    own_prompt = req_index // 2
    tail_here = lax.dynamic_slice_in_dim(tail_len, req_index * conts_here, conts_here)
    plen_here = lax.dynamic_index_in_dim(prompt_len, own_prompt, 0, keepdims=False)
    position = plen_here + tail_here[:, None] + jnp.arange(2, dtype=jnp.int32)[None, :]
    block = new_qkv.reshape(conts_here, 2, 3, heads_here, HD)
    query = rotary(block[:, :, 0].astype(jnp.float32), position).astype(jnp.bfloat16)
    key_new = rotary(block[:, :, 1].astype(jnp.float32), position).astype(jnp.bfloat16)
    value_new = block[:, :, 2]
    mlp_count = lax.axis_size("mlp")
    weights_cat = jnp.concatenate([w_gate, w_up, jnp.transpose(w_down)], axis=1)
    weights_all = jnp.stack(
        [weights_cat]
        + [
            lax.ppermute(
                weights_cat, "mlp", [(m, (m + shift) % mlp_count) for m in range(mlp_count)]
            )
            for shift in range(1, mlp_count)
        ]
    )
    gathered = lax.all_gather(query.reshape(rows_here, width_here), "req", axis=0, tiled=True)
    eye = jnp.eye(heads_here, dtype=jnp.bfloat16)
    tail_diag = jnp.einsum("cthd,hg->chtgd", query, eye).reshape(
        conts_here, heads_here * 2, width_here
    )
    tail_acc, tail_top, tail_sum = tail_attention(tail_diag, tail_cache, tail_here, score_scale)
    gathered, tail_acc, tail_top, tail_sum, weights_all = lax.optimization_barrier(
        (gathered, tail_acc, tail_top, tail_sum, weights_all)
    )
    slot_ids = jnp.arange(req_count, dtype=jnp.int32)
    slot_of = jnp.sum(
        jnp.where(slot_part[None, :] == slot_ids[:, None], slot_ids[None, :], 0), axis=1
    )
    held_part = lax.dynamic_index_in_dim(slot_part, req_index, 0, keepdims=False)
    owned_prompt = held_part // 2
    held_half = held_part % 2
    span = prompt_cache.shape[1]
    owned_rows = 2 * rows_here
    q_owned = lax.dynamic_slice_in_dim(gathered, owned_prompt * owned_rows, owned_rows, 0).reshape(
        owned_rows, heads_here, HD
    )
    owned_len = lax.dynamic_index_in_dim(prompt_len, owned_prompt, 0, keepdims=False)
    valid_count = jnp.clip(owned_len - held_half * span, 0, span)
    q_diag = jnp.einsum("rhd,hg->hrgd", q_owned, eye).reshape(heads_here * owned_rows, width_here)
    prompt_acc, prompt_top, prompt_sum = prompt_attention(q_diag, prompt_cache, valid_count, score_scale)
    prompt_acc = prompt_acc.reshape(heads_here, owned_rows, heads_here, HD)
    owner_numer = jnp.stack([prompt_acc[h, :, h, :] for h in range(heads_here)], axis=1)
    owner_total = prompt_sum.reshape(heads_here, owned_rows)
    prefix_max = prompt_top.reshape(heads_here, owned_rows)
    packed = jnp.concatenate(
        [
            owner_numer.reshape(owned_rows, width_here),
            jnp.transpose(owner_total),
            jnp.transpose(prefix_max),
        ],
        axis=1,
    )
    packed_all = lax.all_gather(packed[None], "req", axis=0, tiled=True)
    row_offset = req_index % 2 * rows_here
    slot_first = lax.dynamic_index_in_dim(slot_of, 2 * own_prompt, 0, keepdims=False)
    slot_second = lax.dynamic_index_in_dim(slot_of, 2 * own_prompt + 1, 0, keepdims=False)

    def part_of(slot):
        piece = lax.dynamic_slice_in_dim(
            lax.dynamic_index_in_dim(packed_all, slot, 0, keepdims=False), row_offset, rows_here, 0
        )
        numer = piece[:, :width_here].reshape(rows_here, heads_here, HD)
        total = piece[:, width_here : width_here + heads_here]
        top = piece[:, width_here + heads_here :]
        return numer, total, top

    numer_first, total_first, max_first = part_of(slot_first)
    numer_second, total_second, max_second = part_of(slot_second)

    tail_acc = tail_acc.reshape(conts_here, heads_here, 2, heads_here, HD)
    cache_numer = jnp.stack([tail_acc[:, h, :, h, :] for h in range(heads_here)], axis=2)
    cache_top = tail_top.reshape(conts_here, heads_here, 2)
    cache_sum = tail_sum.reshape(conts_here, heads_here, 2)
    s_new = (
        jnp.einsum("cthd,cuhd->chtu", query, key_new, preferred_element_type=jnp.float32)
        * score_scale
    )
    causal = jnp.arange(2)[None, :] <= jnp.arange(2)[:, None]
    s_new = jnp.where(causal[None, None, :, :], s_new, masked_value)
    tail_max = jnp.maximum(cache_top, jnp.max(s_new, -1))
    cache_scale = jnp.exp(cache_top - tail_max)
    w_new = jnp.exp(s_new - tail_max[..., None])
    numer_tail = cache_numer * jnp.transpose(cache_scale, (0, 2, 1))[..., None]
    numer_tail = numer_tail + jnp.einsum(
        "chtu,cuhd->cthd", w_new.astype(jnp.bfloat16), value_new, preferred_element_type=jnp.float32
    )
    numer_tail = numer_tail.reshape(rows_here, heads_here, HD)
    total_tail = jnp.transpose(cache_sum * cache_scale + jnp.sum(w_new, -1), (0, 2, 1)).reshape(
        rows_here, heads_here
    )
    max_tail = jnp.transpose(tail_max, (0, 2, 1)).reshape(rows_here, heads_here)
    row_max = jnp.maximum(jnp.maximum(max_first, max_second), max_tail)
    scale_first = jnp.exp(max_first - row_max)
    scale_second = jnp.exp(max_second - row_max)
    scale_tail = jnp.exp(max_tail - row_max)
    row_total = total_first * scale_first + total_second * scale_second + total_tail * scale_tail
    row_numer = (
        numer_first * scale_first[..., None]
        + numer_second * scale_second[..., None]
        + numer_tail * scale_tail[..., None]
    )
    attn = (row_numer / row_total[:, :, None]).astype(jnp.bfloat16).reshape(rows_here, width_here)
    partial = jnp.dot(attn, w_out, preferred_element_type=jnp.float32)
    col_start = mlp_index * width_here
    own_cols = lax.dynamic_slice_in_dim(partial, col_start, width_here, 1)
    partial = lax.dynamic_update_slice_in_dim(
        partial, own_cols + residual.astype(jnp.float32), col_start, 1
    )
    share = rows_here // mlp_count
    state_share = lax.dynamic_slice_in_dim(partial, mlp_index * share, share, 0)
    for shift in range(1, mlp_count):
        target = (mlp_index + shift) % mlp_count
        state_share = state_share + lax.ppermute(
            lax.dynamic_slice_in_dim(partial, target * share, share, 0),
            "mlp",
            [(m, (m + shift) % mlp_count) for m in range(mlp_count)],
        )
    mean_square = jnp.mean(state_share * state_share, axis=1, keepdims=True)
    normed_share = (state_share * lax.rsqrt(mean_square + norm_eps) * mlp_gain).astype(jnp.bfloat16)
    piece = lax.all_to_all(
        jnp.broadcast_to(normed_share[None], (req_count,) + normed_share.shape),
        "req",
        split_axis=0,
        concat_axis=0,
        tiled=True,
    ).reshape(req_count * share, width)
    hidden_here = w_gate.shape[1]
    gate_w = weights_all[:, :, :hidden_here]
    up_w = weights_all[:, :, hidden_here : 2 * hidden_here]
    down_w = weights_all[:, :, 2 * hidden_here :]
    gate = jnp.einsum("rk,mkj->rmj", piece, gate_w, preferred_element_type=jnp.float32)
    upper = jnp.einsum("rk,mkj->rmj", piece, up_w, preferred_element_type=jnp.float32)
    hidden_all = (jax.nn.silu(gate) * upper).astype(jnp.bfloat16)
    down_sum = jnp.einsum("rmj,mfj->rf", hidden_all, down_w, preferred_element_type=jnp.float32)
    row_sums = jnp.sum(
        lax.all_to_all(
            down_sum.astype(jnp.bfloat16).reshape(req_count, share, width),
            "req",
            split_axis=0,
            concat_axis=0,
            tiled=True,
        ).astype(jnp.float32),
        axis=0,
    )
    final_share = state_share + row_sums
    final_square = jnp.mean(final_share * final_share, axis=1)
    final_dot = jnp.sum(final_share * final_gain * score_weight, axis=1)
    score_share = final_dot * lax.rsqrt(final_square + norm_eps)
    payload = jnp.concatenate(
        [
            final_share.reshape(share, mlp_count, width_here),
            jnp.broadcast_to(score_share[:, None, None], (share, mlp_count, 1)),
        ],
        axis=2,
    )
    arrived = lax.dynamic_update_slice_in_dim(
        jnp.zeros((rows_here, width_here + 1), jnp.float32),
        lax.dynamic_index_in_dim(payload, mlp_index, 1, keepdims=False),
        mlp_index * share,
        0,
    )
    for shift in range(1, mlp_count):
        target = (mlp_index + shift) % mlp_count
        source = (mlp_index + mlp_count - shift) % mlp_count
        got = lax.ppermute(
            lax.dynamic_index_in_dim(payload, target, 1, keepdims=False),
            "mlp",
            [(m, (m + shift) % mlp_count) for m in range(mlp_count)],
        )
        arrived = lax.dynamic_update_slice_in_dim(arrived, got, source * share, 0)
    out_rows = arrived[:, :width_here].astype(jnp.bfloat16)
    scores = arrived[:, width_here]
    return (out_rows, scores)


def solution(mesh):
    in_specs = (
        P("req", None, "mlp"),
        P("req", None, None, "mlp"),
        P("req", None, None, "mlp"),
        P("req", "mlp"),
        P("mlp", None),
        P(),
        P(None, ("req", "mlp")),
        P(None, ("req", "mlp")),
        P(("req", "mlp"), None),
        P(),
        P(),
        P(),
        P(),
        P(),
    )
    out_specs = (P("req", "mlp"), P("req"))
    return jax.shard_map(
        per_device, mesh=mesh, in_specs=in_specs, out_specs=out_specs, check_vma=False
    )
```

```python
import functools
import math

import jax
import jax.numpy as jnp
from jax import lax
from jax.experimental import pallas as pl
from jax.experimental.pallas import tpu as pltpu
from jax.sharding import PartitionSpec as P

HD = 96


norm_eps = 1e-05
masked_value = -1e30


def rotary(values, position):
    half_dim = HD // 2
    freqs = 10000.0 ** (-(jnp.arange(half_dim, dtype=jnp.float32) * 2.0) / HD)
    angles = position.astype(jnp.float32)[..., None] * freqs
    cosine = jnp.cos(angles)[..., None, :]
    sine = jnp.sin(angles)[..., None, :]
    first = values[..., :half_dim]
    second = values[..., half_dim:]
    return jnp.concatenate(
        [first * cosine - second * sine, second * cosine + first * sine], axis=-1
    )


def prompt_kernel(block_len, score_scale, valid_ref, q_ref, cache_ref, acc_ref, top_ref, sum_ref):
    number = pl.program_id(0)

    @pl.when(number == 0)
    def _():
        acc_ref[...] = jnp.zeros_like(acc_ref)
        top_ref[...] = jnp.full_like(top_ref, masked_value)
        sum_ref[...] = jnp.zeros_like(sum_ref)

    @pl.when(number * block_len < valid_ref[0])
    def _():
        keys = cache_ref[:, 0, :]
        values = cache_ref[:, 1, :]
        scores = (
            lax.dot_general(
                q_ref[...], keys, (((1,), (1,)), ((), ())), preferred_element_type=jnp.float32
            )
            * score_scale
        )
        places = number * block_len + lax.broadcasted_iota(jnp.int32, scores.shape, 1)
        scores = jnp.where(places < valid_ref[0], scores, masked_value)
        top_old = top_ref[...]
        top_new = jnp.maximum(top_old, jnp.max(scores, axis=1, keepdims=True))
        shrink = jnp.exp(top_old - top_new)
        weights = jnp.exp(scores - top_new)
        sum_ref[...] = shrink * sum_ref[...] + jnp.sum(weights, axis=1, keepdims=True)
        acc_ref[...] = shrink * acc_ref[...] + jnp.dot(
            weights.astype(jnp.bfloat16), values, preferred_element_type=jnp.float32
        )
        top_ref[...] = top_new


def prompt_attention(q_diag, cache, valid_count, score_scale):
    span = cache.shape[1]
    block_len = min(512, span)
    lanes = cache.shape[3]
    rows = q_diag.shape[0]

    def cache_block(number, valid):
        last = (valid[0] + block_len - 1) // block_len - 1
        return (0, jnp.maximum(jnp.minimum(number, last), 0), 0, 0)

    spec = pltpu.PrefetchScalarGridSpec(
        num_scalar_prefetch=1,
        grid=(span // block_len,),
        in_specs=[
            pl.BlockSpec((rows, lanes), lambda number, valid: (0, 0)),
            pl.BlockSpec((None, block_len, 2, lanes), cache_block),
        ],
        out_specs=[
            pl.BlockSpec((rows, lanes), lambda number, valid: (0, 0)),
            pl.BlockSpec((rows, 1), lambda number, valid: (0, 0)),
            pl.BlockSpec((rows, 1), lambda number, valid: (0, 0)),
        ],
    )
    return pl.pallas_call(
        functools.partial(prompt_kernel, block_len, score_scale),
        grid_spec=spec,
        cost_estimate=pl.CostEstimate(
            flops=4 * rows * lanes * span,
            transcendentals=rows * span,
            bytes_accessed=cache.size * 2 + rows * lanes * 6,
        ),
        out_shape=[
            jax.ShapeDtypeStruct((rows, lanes), jnp.float32),
            jax.ShapeDtypeStruct((rows, 1), jnp.float32),
            jax.ShapeDtypeStruct((rows, 1), jnp.float32),
        ],
    )(valid_count.reshape(1), q_diag, cache)


def tail_kernel(score_scale, lens_ref, q_ref, cache_ref, acc_ref, top_ref, sum_ref):
    number = pl.program_id(0)
    keys = cache_ref[:, 0, :]
    values = cache_ref[:, 1, :]
    scores = (
        lax.dot_general(q_ref[...], keys, (((1,), (1,)), ((), ())), preferred_element_type=jnp.float32)
        * score_scale
    )
    places = lax.broadcasted_iota(jnp.int32, scores.shape, 1)
    scores = jnp.where(places < lens_ref[number], scores, masked_value)
    top = jnp.max(scores, axis=1, keepdims=True)
    weights = jnp.exp(scores - top)
    top_ref[...] = top
    sum_ref[...] = jnp.sum(weights, axis=1, keepdims=True)
    acc_ref[...] = jnp.dot(weights.astype(jnp.bfloat16), values, preferred_element_type=jnp.float32)


def tail_attention(q_diag, cache, lens, score_scale):
    conts, rows, lanes = q_diag.shape
    cap = cache.shape[1]
    spec = pltpu.PrefetchScalarGridSpec(
        num_scalar_prefetch=1,
        grid=(conts,),
        in_specs=[
            pl.BlockSpec((None, rows, lanes), lambda number, lens: (number, 0, 0)),
            pl.BlockSpec((None, cap, 2, lanes), lambda number, lens: (number, 0, 0, 0)),
        ],
        out_specs=[
            pl.BlockSpec((None, rows, lanes), lambda number, lens: (number, 0, 0)),
            pl.BlockSpec((None, rows, 1), lambda number, lens: (number, 0, 0)),
            pl.BlockSpec((None, rows, 1), lambda number, lens: (number, 0, 0)),
        ],
    )
    return pl.pallas_call(
        functools.partial(tail_kernel, score_scale),
        grid_spec=spec,
        cost_estimate=pl.CostEstimate(
            flops=4 * conts * rows * lanes * cap,
            transcendentals=conts * rows * cap,
            bytes_accessed=cache.size * 2 + conts * rows * lanes * 6,
        ),
        out_shape=[
            jax.ShapeDtypeStruct((conts, rows, lanes), jnp.float32),
            jax.ShapeDtypeStruct((conts, rows, 1), jnp.float32),
            jax.ShapeDtypeStruct((conts, rows, 1), jnp.float32),
        ],
    )(lens, q_diag, cache)


def per_device(
    new_qkv,
    prompt_cache,
    tail_cache,
    residual,
    w_out,
    mlp_gain,
    w_gate,
    w_up,
    w_down,
    final_gain,
    score_weight,
    slot_part,
    prompt_len,
    tail_len,
):
    req_count = lax.axis_size("req")
    req_index = lax.axis_index("req")
    mlp_index = lax.axis_index("mlp")
    rows_here = new_qkv.shape[0]
    width_here = new_qkv.shape[2]
    heads_here = width_here // HD
    conts_here = rows_here // 2
    width = w_out.shape[1]
    score_scale = 1.0 / math.sqrt(HD)
    own_prompt = req_index // 2
    tail_here = lax.dynamic_slice_in_dim(tail_len, req_index * conts_here, conts_here)
    plen_here = lax.dynamic_index_in_dim(prompt_len, own_prompt, 0, keepdims=False)
    position = plen_here + tail_here[:, None] + jnp.arange(2, dtype=jnp.int32)[None, :]
    block = new_qkv.reshape(conts_here, 2, 3, heads_here, HD)
    query = rotary(block[:, :, 0].astype(jnp.float32), position).astype(jnp.bfloat16)
    key_new = rotary(block[:, :, 1].astype(jnp.float32), position).astype(jnp.bfloat16)
    value_new = block[:, :, 2]
    mlp_count = lax.axis_size("mlp")
    weights_cat = jnp.concatenate([w_gate, w_up, jnp.transpose(w_down)], axis=1)
    weights_all = jnp.stack(
        [weights_cat]
        + [
            lax.ppermute(
                weights_cat, "mlp", [(m, (m + shift) % mlp_count) for m in range(mlp_count)]
            )
            for shift in range(1, mlp_count)
        ]
    )
    gathered = lax.all_gather(query.reshape(rows_here, width_here), "req", axis=0, tiled=True)
    eye = jnp.eye(heads_here, dtype=jnp.bfloat16)
    tail_diag = jnp.einsum("cthd,hg->chtgd", query, eye).reshape(
        conts_here, heads_here * 2, width_here
    )
    tail_acc, tail_top, tail_sum = tail_attention(tail_diag, tail_cache, tail_here, score_scale)
    gathered, tail_acc, tail_top, tail_sum, weights_all = lax.optimization_barrier(
        (gathered, tail_acc, tail_top, tail_sum, weights_all)
    )
    slot_ids = jnp.arange(req_count, dtype=jnp.int32)
    slot_of = jnp.sum(
        jnp.where(slot_part[None, :] == slot_ids[:, None], slot_ids[None, :], 0), axis=1
    )
    held_part = lax.dynamic_index_in_dim(slot_part, req_index, 0, keepdims=False)
    owned_prompt = held_part // 2
    held_half = held_part % 2
    span = prompt_cache.shape[1]
    owned_rows = 2 * rows_here
    q_owned = lax.dynamic_slice_in_dim(gathered, owned_prompt * owned_rows, owned_rows, 0).reshape(
        owned_rows, heads_here, HD
    )
    owned_len = lax.dynamic_index_in_dim(prompt_len, owned_prompt, 0, keepdims=False)
    valid_count = jnp.clip(owned_len - held_half * span, 0, span)
    q_diag = jnp.einsum("rhd,hg->hrgd", q_owned, eye).reshape(heads_here * owned_rows, width_here)
    prompt_acc, prompt_top, prompt_sum = prompt_attention(q_diag, prompt_cache, valid_count, score_scale)
    prompt_acc = prompt_acc.reshape(heads_here, owned_rows, heads_here, HD)
    owner_numer = jnp.stack([prompt_acc[h, :, h, :] for h in range(heads_here)], axis=1)
    top_f = jnp.transpose(prompt_top.reshape(heads_here, owned_rows))
    top_b = top_f.astype(jnp.bfloat16).astype(jnp.float32)
    rebase = jnp.where(top_f > 0.5 * masked_value, jnp.exp(top_f - top_b), 0.0)
    owner_total = jnp.transpose(prompt_sum.reshape(heads_here, owned_rows)) * rebase
    owner_numer = owner_numer * rebase[:, :, None]
    packed = jnp.concatenate(
        [owner_numer.reshape(owned_rows, width_here), owner_total, top_b], axis=1
    ).astype(jnp.bfloat16)
    outgoing = lax.dynamic_update_slice_in_dim(
        jnp.zeros((req_count, rows_here, packed.shape[1]), jnp.bfloat16),
        packed.reshape(2, rows_here, packed.shape[1]),
        2 * owned_prompt,
        0,
    )
    incoming = lax.all_to_all(outgoing, "req", split_axis=0, concat_axis=0, tiled=True)
    slot_first = lax.dynamic_index_in_dim(slot_of, 2 * own_prompt, 0, keepdims=False)
    slot_second = lax.dynamic_index_in_dim(slot_of, 2 * own_prompt + 1, 0, keepdims=False)

    def part_of(slot):
        piece = lax.dynamic_index_in_dim(incoming, slot, 0, keepdims=False).astype(jnp.float32)
        numer = piece[:, :width_here].reshape(rows_here, heads_here, HD)
        total = piece[:, width_here : width_here + heads_here]
        top = piece[:, width_here + heads_here :]
        return numer, total, top

    numer_first, total_first, max_first = part_of(slot_first)
    numer_second, total_second, max_second = part_of(slot_second)

    tail_acc = tail_acc.reshape(conts_here, heads_here, 2, heads_here, HD)
    cache_numer = jnp.stack([tail_acc[:, h, :, h, :] for h in range(heads_here)], axis=2)
    cache_top = tail_top.reshape(conts_here, heads_here, 2)
    cache_sum = tail_sum.reshape(conts_here, heads_here, 2)
    s_new = (
        jnp.einsum("cthd,cuhd->chtu", query, key_new, preferred_element_type=jnp.float32)
        * score_scale
    )
    causal = jnp.arange(2)[None, :] <= jnp.arange(2)[:, None]
    s_new = jnp.where(causal[None, None, :, :], s_new, masked_value)
    tail_max = jnp.maximum(cache_top, jnp.max(s_new, -1))
    cache_scale = jnp.exp(cache_top - tail_max)
    w_new = jnp.exp(s_new - tail_max[..., None])
    numer_tail = cache_numer * jnp.transpose(cache_scale, (0, 2, 1))[..., None]
    numer_tail = numer_tail + jnp.einsum(
        "chtu,cuhd->cthd", w_new.astype(jnp.bfloat16), value_new, preferred_element_type=jnp.float32
    )
    numer_tail = numer_tail.reshape(rows_here, heads_here, HD)
    total_tail = jnp.transpose(cache_sum * cache_scale + jnp.sum(w_new, -1), (0, 2, 1)).reshape(
        rows_here, heads_here
    )
    max_tail = jnp.transpose(tail_max, (0, 2, 1)).reshape(rows_here, heads_here)
    row_max = jnp.maximum(jnp.maximum(max_first, max_second), max_tail)
    scale_first = jnp.exp(max_first - row_max)
    scale_second = jnp.exp(max_second - row_max)
    scale_tail = jnp.exp(max_tail - row_max)
    row_total = total_first * scale_first + total_second * scale_second + total_tail * scale_tail
    row_numer = (
        numer_first * scale_first[..., None]
        + numer_second * scale_second[..., None]
        + numer_tail * scale_tail[..., None]
    )
    attn = (row_numer / row_total[:, :, None]).astype(jnp.bfloat16).reshape(rows_here, width_here)
    partial = jnp.dot(attn, w_out, preferred_element_type=jnp.float32)
    col_start = mlp_index * width_here
    own_cols = lax.dynamic_slice_in_dim(partial, col_start, width_here, 1)
    partial = lax.dynamic_update_slice_in_dim(
        partial, own_cols + residual.astype(jnp.float32), col_start, 1
    )
    share = rows_here // mlp_count
    state_share = lax.dynamic_slice_in_dim(partial, mlp_index * share, share, 0)
    for shift in range(1, mlp_count):
        target = (mlp_index + shift) % mlp_count
        state_share = state_share + lax.ppermute(
            lax.dynamic_slice_in_dim(partial, target * share, share, 0),
            "mlp",
            [(m, (m + shift) % mlp_count) for m in range(mlp_count)],
        )
    mean_square = jnp.mean(state_share * state_share, axis=1, keepdims=True)
    normed_share = (state_share * lax.rsqrt(mean_square + norm_eps) * mlp_gain).astype(jnp.bfloat16)
    piece = lax.all_to_all(
        jnp.broadcast_to(normed_share[None], (req_count,) + normed_share.shape),
        "req",
        split_axis=0,
        concat_axis=0,
        tiled=True,
    ).reshape(req_count * share, width)
    hidden_here = w_gate.shape[1]
    gate_w = weights_all[:, :, :hidden_here]
    up_w = weights_all[:, :, hidden_here : 2 * hidden_here]
    down_w = weights_all[:, :, 2 * hidden_here :]
    gate = jnp.einsum("rk,mkj->rmj", piece, gate_w, preferred_element_type=jnp.float32)
    upper = jnp.einsum("rk,mkj->rmj", piece, up_w, preferred_element_type=jnp.float32)
    hidden_all = (jax.nn.silu(gate) * upper).astype(jnp.bfloat16)
    down_sum = jnp.einsum("rmj,mfj->rf", hidden_all, down_w, preferred_element_type=jnp.float32)
    row_sums = jnp.sum(
        lax.all_to_all(
            down_sum.astype(jnp.bfloat16).reshape(req_count, share, width),
            "req",
            split_axis=0,
            concat_axis=0,
            tiled=True,
        ).astype(jnp.float32),
        axis=0,
    )
    final_share = state_share + row_sums
    final_square = jnp.mean(final_share * final_share, axis=1)
    final_dot = jnp.sum(final_share * final_gain * score_weight, axis=1)
    score_share = final_dot * lax.rsqrt(final_square + norm_eps)
    payload = jnp.concatenate(
        [
            final_share.reshape(share, mlp_count, width_here),
            jnp.broadcast_to(score_share[:, None, None], (share, mlp_count, 1)),
        ],
        axis=2,
    )
    arrived = lax.dynamic_update_slice_in_dim(
        jnp.zeros((rows_here, width_here + 1), jnp.float32),
        lax.dynamic_index_in_dim(payload, mlp_index, 1, keepdims=False),
        mlp_index * share,
        0,
    )
    for shift in range(1, mlp_count):
        target = (mlp_index + shift) % mlp_count
        source = (mlp_index + mlp_count - shift) % mlp_count
        got = lax.ppermute(
            lax.dynamic_index_in_dim(payload, target, 1, keepdims=False),
            "mlp",
            [(m, (m + shift) % mlp_count) for m in range(mlp_count)],
        )
        arrived = lax.dynamic_update_slice_in_dim(arrived, got, source * share, 0)
    out_rows = arrived[:, :width_here].astype(jnp.bfloat16)
    scores = arrived[:, width_here]
    return (out_rows, scores)


def solution(mesh):
    in_specs = (
        P("req", None, "mlp"),
        P("req", None, None, "mlp"),
        P("req", None, None, "mlp"),
        P("req", "mlp"),
        P("mlp", None),
        P(),
        P(None, ("req", "mlp")),
        P(None, ("req", "mlp")),
        P(("req", "mlp"), None),
        P(),
        P(),
        P(),
        P(),
        P(),
    )
    out_specs = (P("req", "mlp"), P("req"))
    return jax.shard_map(
        per_device, mesh=mesh, in_specs=in_specs, out_specs=out_specs, check_vma=False
    )
```

```python
import functools
import math

import jax
import jax.numpy as jnp
from jax import lax
from jax.experimental import pallas as pl
from jax.experimental.pallas import tpu as pltpu
from jax.sharding import PartitionSpec as P

HD = 96


norm_eps = 1e-05
masked_value = -1e30


def rotary(values, position):
    half_dim = HD // 2
    freqs = 10000.0 ** (-(jnp.arange(half_dim, dtype=jnp.float32) * 2.0) / HD)
    angles = position.astype(jnp.float32)[..., None] * freqs
    cosine = jnp.cos(angles)[..., None, :]
    sine = jnp.sin(angles)[..., None, :]
    first = values[..., :half_dim]
    second = values[..., half_dim:]
    return jnp.concatenate(
        [first * cosine - second * sine, second * cosine + first * sine], axis=-1
    )


def prompt_kernel(block_len, score_scale, valid_ref, q_ref, cache_ref, acc_ref, top_ref, sum_ref):
    number = pl.program_id(0)

    @pl.when(number == 0)
    def _():
        acc_ref[...] = jnp.zeros_like(acc_ref)
        top_ref[...] = jnp.full_like(top_ref, masked_value)
        sum_ref[...] = jnp.zeros_like(sum_ref)

    @pl.when(number * block_len < valid_ref[0])
    def _():
        keys = cache_ref[:, 0, :]
        values = cache_ref[:, 1, :]
        scores = (
            lax.dot_general(
                q_ref[...], keys, (((1,), (1,)), ((), ())), preferred_element_type=jnp.float32
            )
            * score_scale
        )
        places = number * block_len + lax.broadcasted_iota(jnp.int32, scores.shape, 1)
        scores = jnp.where(places < valid_ref[0], scores, masked_value)
        top_old = top_ref[...]
        top_new = jnp.maximum(top_old, jnp.max(scores, axis=1, keepdims=True))
        shrink = jnp.exp(top_old - top_new)
        weights = jnp.exp(scores - top_new)
        sum_ref[...] = shrink * sum_ref[...] + jnp.sum(weights, axis=1, keepdims=True)
        acc_ref[...] = shrink * acc_ref[...] + jnp.dot(
            weights.astype(jnp.bfloat16), values, preferred_element_type=jnp.float32
        )
        top_ref[...] = top_new


def prompt_attention(q_diag, cache, valid_count, score_scale):
    span = cache.shape[1]
    block_len = min(1024, span)
    lanes = cache.shape[3]
    rows = q_diag.shape[0]

    def cache_block(number, valid):
        last = (valid[0] + block_len - 1) // block_len - 1
        return (0, jnp.maximum(jnp.minimum(number, last), 0), 0, 0)

    spec = pltpu.PrefetchScalarGridSpec(
        num_scalar_prefetch=1,
        grid=(span // block_len,),
        in_specs=[
            pl.BlockSpec((rows, lanes), lambda number, valid: (0, 0)),
            pl.BlockSpec((None, block_len, 2, lanes), cache_block),
        ],
        out_specs=[
            pl.BlockSpec((rows, lanes), lambda number, valid: (0, 0)),
            pl.BlockSpec((rows, 1), lambda number, valid: (0, 0)),
            pl.BlockSpec((rows, 1), lambda number, valid: (0, 0)),
        ],
    )
    return pl.pallas_call(
        functools.partial(prompt_kernel, block_len, score_scale),
        grid_spec=spec,
        cost_estimate=pl.CostEstimate(
            flops=4 * rows * lanes * span,
            transcendentals=rows * span,
            bytes_accessed=cache.size * 2 + rows * lanes * 6,
        ),
        out_shape=[
            jax.ShapeDtypeStruct((rows, lanes), jnp.float32),
            jax.ShapeDtypeStruct((rows, 1), jnp.float32),
            jax.ShapeDtypeStruct((rows, 1), jnp.float32),
        ],
    )(valid_count.reshape(1), q_diag, cache)


def tail_kernel(score_scale, lens_ref, q_ref, cache_ref, acc_ref, top_ref, sum_ref):
    number = pl.program_id(0)
    keys = cache_ref[:, 0, :]
    values = cache_ref[:, 1, :]
    scores = (
        lax.dot_general(q_ref[...], keys, (((1,), (1,)), ((), ())), preferred_element_type=jnp.float32)
        * score_scale
    )
    places = lax.broadcasted_iota(jnp.int32, scores.shape, 1)
    scores = jnp.where(places < lens_ref[number], scores, masked_value)
    top = jnp.max(scores, axis=1, keepdims=True)
    weights = jnp.exp(scores - top)
    top_ref[...] = top
    sum_ref[...] = jnp.sum(weights, axis=1, keepdims=True)
    acc_ref[...] = jnp.dot(weights.astype(jnp.bfloat16), values, preferred_element_type=jnp.float32)


def tail_attention(q_diag, cache, lens, score_scale):
    conts, rows, lanes = q_diag.shape
    cap = cache.shape[1]
    spec = pltpu.PrefetchScalarGridSpec(
        num_scalar_prefetch=1,
        grid=(conts,),
        in_specs=[
            pl.BlockSpec((None, rows, lanes), lambda number, lens: (number, 0, 0)),
            pl.BlockSpec((None, cap, 2, lanes), lambda number, lens: (number, 0, 0, 0)),
        ],
        out_specs=[
            pl.BlockSpec((None, rows, lanes), lambda number, lens: (number, 0, 0)),
            pl.BlockSpec((None, rows, 1), lambda number, lens: (number, 0, 0)),
            pl.BlockSpec((None, rows, 1), lambda number, lens: (number, 0, 0)),
        ],
    )
    return pl.pallas_call(
        functools.partial(tail_kernel, score_scale),
        grid_spec=spec,
        cost_estimate=pl.CostEstimate(
            flops=4 * conts * rows * lanes * cap,
            transcendentals=conts * rows * cap,
            bytes_accessed=cache.size * 2 + conts * rows * lanes * 6,
        ),
        out_shape=[
            jax.ShapeDtypeStruct((conts, rows, lanes), jnp.float32),
            jax.ShapeDtypeStruct((conts, rows, 1), jnp.float32),
            jax.ShapeDtypeStruct((conts, rows, 1), jnp.float32),
        ],
    )(lens, q_diag, cache)


def per_device(
    new_qkv,
    prompt_cache,
    tail_cache,
    residual,
    w_out,
    mlp_gain,
    w_gate,
    w_up,
    w_down,
    final_gain,
    score_weight,
    slot_part,
    prompt_len,
    tail_len,
):
    req_count = lax.axis_size("req")
    req_index = lax.axis_index("req")
    mlp_index = lax.axis_index("mlp")
    rows_here = new_qkv.shape[0]
    width_here = new_qkv.shape[2]
    heads_here = width_here // HD
    conts_here = rows_here // 2
    width = w_out.shape[1]
    score_scale = 1.0 / math.sqrt(HD)
    own_prompt = req_index // 2
    tail_here = lax.dynamic_slice_in_dim(tail_len, req_index * conts_here, conts_here)
    plen_here = lax.dynamic_index_in_dim(prompt_len, own_prompt, 0, keepdims=False)
    position = plen_here + tail_here[:, None] + jnp.arange(2, dtype=jnp.int32)[None, :]
    block = new_qkv.reshape(conts_here, 2, 3, heads_here, HD)
    query = rotary(block[:, :, 0].astype(jnp.float32), position).astype(jnp.bfloat16)
    key_new = rotary(block[:, :, 1].astype(jnp.float32), position).astype(jnp.bfloat16)
    value_new = block[:, :, 2]
    mlp_count = lax.axis_size("mlp")
    weights_cat = jnp.concatenate([w_gate, w_up, jnp.transpose(w_down)], axis=1)
    weights_all = jnp.stack(
        [weights_cat]
        + [
            lax.ppermute(
                weights_cat, "mlp", [(m, (m + shift) % mlp_count) for m in range(mlp_count)]
            )
            for shift in range(1, mlp_count)
        ]
    )
    gathered = lax.all_gather(query.reshape(rows_here, width_here), "req", axis=0, tiled=True)
    eye = jnp.eye(heads_here, dtype=jnp.bfloat16)
    tail_diag = jnp.einsum("cthd,hg->chtgd", query, eye).reshape(
        conts_here, heads_here * 2, width_here
    )
    tail_acc, tail_top, tail_sum = tail_attention(tail_diag, tail_cache, tail_here, score_scale)
    gathered, tail_acc, tail_top, tail_sum, weights_all = lax.optimization_barrier(
        (gathered, tail_acc, tail_top, tail_sum, weights_all)
    )
    slot_ids = jnp.arange(req_count, dtype=jnp.int32)
    slot_of = jnp.sum(
        jnp.where(slot_part[None, :] == slot_ids[:, None], slot_ids[None, :], 0), axis=1
    )
    held_part = lax.dynamic_index_in_dim(slot_part, req_index, 0, keepdims=False)
    owned_prompt = held_part // 2
    held_half = held_part % 2
    span = prompt_cache.shape[1]
    owned_rows = 2 * rows_here
    q_owned = lax.dynamic_slice_in_dim(gathered, owned_prompt * owned_rows, owned_rows, 0).reshape(
        owned_rows, heads_here, HD
    )
    owned_len = lax.dynamic_index_in_dim(prompt_len, owned_prompt, 0, keepdims=False)
    valid_count = jnp.clip(owned_len - held_half * span, 0, span)
    q_diag = jnp.einsum("rhd,hg->hrgd", q_owned, eye).reshape(heads_here * owned_rows, width_here)
    prompt_acc, prompt_top, prompt_sum = prompt_attention(q_diag, prompt_cache, valid_count, score_scale)
    prompt_acc = prompt_acc.reshape(heads_here, owned_rows, heads_here, HD)
    owner_numer = jnp.stack([prompt_acc[h, :, h, :] for h in range(heads_here)], axis=1)
    top_f = jnp.transpose(prompt_top.reshape(heads_here, owned_rows))
    top_b = top_f.astype(jnp.bfloat16).astype(jnp.float32)
    rebase = jnp.where(top_f > 0.5 * masked_value, jnp.exp(top_f - top_b), 0.0)
    owner_total = jnp.transpose(prompt_sum.reshape(heads_here, owned_rows)) * rebase
    owner_numer = owner_numer * rebase[:, :, None]
    packed = jnp.concatenate(
        [owner_numer.reshape(owned_rows, width_here), owner_total, top_b], axis=1
    ).astype(jnp.bfloat16)
    outgoing = lax.dynamic_update_slice_in_dim(
        jnp.zeros((req_count, rows_here, packed.shape[1]), jnp.bfloat16),
        packed.reshape(2, rows_here, packed.shape[1]),
        2 * owned_prompt,
        0,
    )
    incoming = lax.all_to_all(outgoing, "req", split_axis=0, concat_axis=0, tiled=True)
    slot_first = lax.dynamic_index_in_dim(slot_of, 2 * own_prompt, 0, keepdims=False)
    slot_second = lax.dynamic_index_in_dim(slot_of, 2 * own_prompt + 1, 0, keepdims=False)

    def part_of(slot):
        piece = lax.dynamic_index_in_dim(incoming, slot, 0, keepdims=False).astype(jnp.float32)
        numer = piece[:, :width_here].reshape(rows_here, heads_here, HD)
        total = piece[:, width_here : width_here + heads_here]
        top = piece[:, width_here + heads_here :]
        return numer, total, top

    numer_first, total_first, max_first = part_of(slot_first)
    numer_second, total_second, max_second = part_of(slot_second)

    tail_acc = tail_acc.reshape(conts_here, heads_here, 2, heads_here, HD)
    cache_numer = jnp.stack([tail_acc[:, h, :, h, :] for h in range(heads_here)], axis=2)
    cache_top = tail_top.reshape(conts_here, heads_here, 2)
    cache_sum = tail_sum.reshape(conts_here, heads_here, 2)
    s_new = (
        jnp.einsum("cthd,cuhd->chtu", query, key_new, preferred_element_type=jnp.float32)
        * score_scale
    )
    causal = jnp.arange(2)[None, :] <= jnp.arange(2)[:, None]
    s_new = jnp.where(causal[None, None, :, :], s_new, masked_value)
    tail_max = jnp.maximum(cache_top, jnp.max(s_new, -1))
    cache_scale = jnp.exp(cache_top - tail_max)
    w_new = jnp.exp(s_new - tail_max[..., None])
    numer_tail = cache_numer * jnp.transpose(cache_scale, (0, 2, 1))[..., None]
    numer_tail = numer_tail + jnp.einsum(
        "chtu,cuhd->cthd", w_new.astype(jnp.bfloat16), value_new, preferred_element_type=jnp.float32
    )
    numer_tail = numer_tail.reshape(rows_here, heads_here, HD)
    total_tail = jnp.transpose(cache_sum * cache_scale + jnp.sum(w_new, -1), (0, 2, 1)).reshape(
        rows_here, heads_here
    )
    max_tail = jnp.transpose(tail_max, (0, 2, 1)).reshape(rows_here, heads_here)
    row_max = jnp.maximum(jnp.maximum(max_first, max_second), max_tail)
    scale_first = jnp.exp(max_first - row_max)
    scale_second = jnp.exp(max_second - row_max)
    scale_tail = jnp.exp(max_tail - row_max)
    row_total = total_first * scale_first + total_second * scale_second + total_tail * scale_tail
    row_numer = (
        numer_first * scale_first[..., None]
        + numer_second * scale_second[..., None]
        + numer_tail * scale_tail[..., None]
    )
    attn = (row_numer / row_total[:, :, None]).astype(jnp.bfloat16).reshape(rows_here, width_here)
    partial = jnp.dot(attn, w_out, preferred_element_type=jnp.float32)
    col_start = mlp_index * width_here
    own_cols = lax.dynamic_slice_in_dim(partial, col_start, width_here, 1)
    partial = lax.dynamic_update_slice_in_dim(
        partial, own_cols + residual.astype(jnp.float32), col_start, 1
    )
    share = rows_here // mlp_count
    state_share = lax.dynamic_slice_in_dim(partial, mlp_index * share, share, 0)
    for shift in range(1, mlp_count):
        target = (mlp_index + shift) % mlp_count
        state_share = state_share + lax.ppermute(
            lax.dynamic_slice_in_dim(partial, target * share, share, 0),
            "mlp",
            [(m, (m + shift) % mlp_count) for m in range(mlp_count)],
        )
    mean_square = jnp.mean(state_share * state_share, axis=1, keepdims=True)
    normed_share = (state_share * lax.rsqrt(mean_square + norm_eps) * mlp_gain).astype(jnp.bfloat16)
    piece = lax.all_to_all(
        jnp.broadcast_to(normed_share[None], (req_count,) + normed_share.shape),
        "req",
        split_axis=0,
        concat_axis=0,
        tiled=True,
    ).reshape(req_count * share, width)
    hidden_here = w_gate.shape[1]
    gate_w = weights_all[:, :, :hidden_here]
    up_w = weights_all[:, :, hidden_here : 2 * hidden_here]
    down_w = weights_all[:, :, 2 * hidden_here :]
    gate = jnp.einsum("rk,mkj->rmj", piece, gate_w, preferred_element_type=jnp.float32)
    upper = jnp.einsum("rk,mkj->rmj", piece, up_w, preferred_element_type=jnp.float32)
    hidden_all = (jax.nn.silu(gate) * upper).astype(jnp.bfloat16)
    down_sum = jnp.einsum("rmj,mfj->rf", hidden_all, down_w, preferred_element_type=jnp.float32)
    row_sums = jnp.sum(
        lax.all_to_all(
            down_sum.astype(jnp.bfloat16).reshape(req_count, share, width),
            "req",
            split_axis=0,
            concat_axis=0,
            tiled=True,
        ).astype(jnp.float32),
        axis=0,
    )
    final_share = state_share + row_sums
    final_square = jnp.mean(final_share * final_share, axis=1)
    final_dot = jnp.sum(final_share * final_gain * score_weight, axis=1)
    score_share = final_dot * lax.rsqrt(final_square + norm_eps)
    payload = jnp.concatenate(
        [
            final_share.reshape(share, mlp_count, width_here),
            jnp.broadcast_to(score_share[:, None, None], (share, mlp_count, 1)),
        ],
        axis=2,
    )
    arrived = lax.dynamic_update_slice_in_dim(
        jnp.zeros((rows_here, width_here + 1), jnp.float32),
        lax.dynamic_index_in_dim(payload, mlp_index, 1, keepdims=False),
        mlp_index * share,
        0,
    )
    for shift in range(1, mlp_count):
        target = (mlp_index + shift) % mlp_count
        source = (mlp_index + mlp_count - shift) % mlp_count
        got = lax.ppermute(
            lax.dynamic_index_in_dim(payload, target, 1, keepdims=False),
            "mlp",
            [(m, (m + shift) % mlp_count) for m in range(mlp_count)],
        )
        arrived = lax.dynamic_update_slice_in_dim(arrived, got, source * share, 0)
    out_rows = arrived[:, :width_here].astype(jnp.bfloat16)
    scores = arrived[:, width_here]
    return (out_rows, scores)


def solution(mesh):
    in_specs = (
        P("req", None, "mlp"),
        P("req", None, None, "mlp"),
        P("req", None, None, "mlp"),
        P("req", "mlp"),
        P("mlp", None),
        P(),
        P(None, ("req", "mlp")),
        P(None, ("req", "mlp")),
        P(("req", "mlp"), None),
        P(),
        P(),
        P(),
        P(),
        P(),
    )
    out_specs = (P("req", "mlp"), P("req"))
    return jax.shard_map(
        per_device, mesh=mesh, in_specs=in_specs, out_specs=out_specs, check_vma=False
    )
```

```python
import functools
import math

import jax
import jax.numpy as jnp
from jax import lax
from jax.experimental import pallas as pl
from jax.experimental.pallas import tpu as pltpu
from jax.sharding import PartitionSpec as P

HD = 96


norm_eps = 1e-05
masked_value = -1e30


def rotary(values, position):
    half_dim = HD // 2
    freqs = 10000.0 ** (-(jnp.arange(half_dim, dtype=jnp.float32) * 2.0) / HD)
    angles = position.astype(jnp.float32)[..., None] * freqs
    cosine = jnp.cos(angles)[..., None, :]
    sine = jnp.sin(angles)[..., None, :]
    first = values[..., :half_dim]
    second = values[..., half_dim:]
    return jnp.concatenate(
        [first * cosine - second * sine, second * cosine + first * sine], axis=-1
    )


def prompt_kernel(block_len, score_scale, valid_ref, q_ref, cache_ref, acc_ref, top_ref, sum_ref):
    number = pl.program_id(0)
    start = number * block_len

    @pl.when(number == 0)
    def _():
        acc_ref[...] = jnp.zeros_like(acc_ref)
        top_ref[...] = jnp.full_like(top_ref, masked_value)
        sum_ref[...] = jnp.zeros_like(sum_ref)

    def step(masked):
        keys = cache_ref[:, 0, :]
        values = cache_ref[:, 1, :]
        scores = (
            lax.dot_general(
                q_ref[...], keys, (((1,), (1,)), ((), ())), preferred_element_type=jnp.float32
            )
            * score_scale
        )
        if masked:
            places = start + lax.broadcasted_iota(jnp.int32, scores.shape, 1)
            scores = jnp.where(places < valid_ref[0], scores, masked_value)
        top_old = top_ref[...]
        top_new = jnp.maximum(top_old, jnp.max(scores, axis=1, keepdims=True))
        shrink = jnp.exp(top_old - top_new)
        weights = jnp.exp(scores - top_new)
        sum_ref[...] = shrink * sum_ref[...] + jnp.sum(weights, axis=1, keepdims=True)
        acc_ref[...] = shrink * acc_ref[...] + jnp.dot(
            weights.astype(jnp.bfloat16), values, preferred_element_type=jnp.float32
        )
        top_ref[...] = top_new

    @pl.when(start + block_len <= valid_ref[0])
    def _():
        step(False)

    @pl.when(jnp.logical_and(start < valid_ref[0], start + block_len > valid_ref[0]))
    def _():
        step(True)


def prompt_attention(q_diag, cache, valid_count, score_scale):
    span = cache.shape[1]
    block_len = min(1024, span)
    lanes = cache.shape[3]
    rows = q_diag.shape[0]

    def cache_block(number, valid):
        last = (valid[0] + block_len - 1) // block_len - 1
        return (0, jnp.maximum(jnp.minimum(number, last), 0), 0, 0)

    spec = pltpu.PrefetchScalarGridSpec(
        num_scalar_prefetch=1,
        grid=(span // block_len,),
        in_specs=[
            pl.BlockSpec((rows, lanes), lambda number, valid: (0, 0)),
            pl.BlockSpec((None, block_len, 2, lanes), cache_block),
        ],
        out_specs=[
            pl.BlockSpec((rows, lanes), lambda number, valid: (0, 0)),
            pl.BlockSpec((rows, 1), lambda number, valid: (0, 0)),
            pl.BlockSpec((rows, 1), lambda number, valid: (0, 0)),
        ],
    )
    return pl.pallas_call(
        functools.partial(prompt_kernel, block_len, score_scale),
        grid_spec=spec,
        cost_estimate=pl.CostEstimate(
            flops=4 * rows * lanes * span,
            transcendentals=rows * span,
            bytes_accessed=cache.size * 2 + rows * lanes * 6,
        ),
        out_shape=[
            jax.ShapeDtypeStruct((rows, lanes), jnp.float32),
            jax.ShapeDtypeStruct((rows, 1), jnp.float32),
            jax.ShapeDtypeStruct((rows, 1), jnp.float32),
        ],
    )(valid_count.reshape(1), q_diag, cache)


def tail_kernel(score_scale, lens_ref, q_ref, cache_ref, acc_ref, top_ref, sum_ref):
    number = pl.program_id(0)
    keys = cache_ref[:, 0, :]
    values = cache_ref[:, 1, :]
    scores = (
        lax.dot_general(q_ref[...], keys, (((1,), (1,)), ((), ())), preferred_element_type=jnp.float32)
        * score_scale
    )
    places = lax.broadcasted_iota(jnp.int32, scores.shape, 1)
    scores = jnp.where(places < lens_ref[number], scores, masked_value)
    top = jnp.max(scores, axis=1, keepdims=True)
    weights = jnp.exp(scores - top)
    top_ref[...] = top
    sum_ref[...] = jnp.sum(weights, axis=1, keepdims=True)
    acc_ref[...] = jnp.dot(weights.astype(jnp.bfloat16), values, preferred_element_type=jnp.float32)


def tail_attention(q_diag, cache, lens, score_scale):
    conts, rows, lanes = q_diag.shape
    cap = cache.shape[1]
    spec = pltpu.PrefetchScalarGridSpec(
        num_scalar_prefetch=1,
        grid=(conts,),
        in_specs=[
            pl.BlockSpec((None, rows, lanes), lambda number, lens: (number, 0, 0)),
            pl.BlockSpec((None, cap, 2, lanes), lambda number, lens: (number, 0, 0, 0)),
        ],
        out_specs=[
            pl.BlockSpec((None, rows, lanes), lambda number, lens: (number, 0, 0)),
            pl.BlockSpec((None, rows, 1), lambda number, lens: (number, 0, 0)),
            pl.BlockSpec((None, rows, 1), lambda number, lens: (number, 0, 0)),
        ],
    )
    return pl.pallas_call(
        functools.partial(tail_kernel, score_scale),
        grid_spec=spec,
        cost_estimate=pl.CostEstimate(
            flops=4 * conts * rows * lanes * cap,
            transcendentals=conts * rows * cap,
            bytes_accessed=cache.size * 2 + conts * rows * lanes * 6,
        ),
        out_shape=[
            jax.ShapeDtypeStruct((conts, rows, lanes), jnp.float32),
            jax.ShapeDtypeStruct((conts, rows, 1), jnp.float32),
            jax.ShapeDtypeStruct((conts, rows, 1), jnp.float32),
        ],
    )(lens, q_diag, cache)


def per_device(
    new_qkv,
    prompt_cache,
    tail_cache,
    residual,
    w_out,
    mlp_gain,
    w_gate,
    w_up,
    w_down,
    final_gain,
    score_weight,
    slot_part,
    prompt_len,
    tail_len,
):
    req_count = lax.axis_size("req")
    req_index = lax.axis_index("req")
    mlp_index = lax.axis_index("mlp")
    rows_here = new_qkv.shape[0]
    width_here = new_qkv.shape[2]
    heads_here = width_here // HD
    conts_here = rows_here // 2
    width = w_out.shape[1]
    score_scale = 1.0 / math.sqrt(HD)
    own_prompt = req_index // 2
    tail_here = lax.dynamic_slice_in_dim(tail_len, req_index * conts_here, conts_here)
    plen_here = lax.dynamic_index_in_dim(prompt_len, own_prompt, 0, keepdims=False)
    position = plen_here + tail_here[:, None] + jnp.arange(2, dtype=jnp.int32)[None, :]
    block = new_qkv.reshape(conts_here, 2, 3, heads_here, HD)
    query = rotary(block[:, :, 0].astype(jnp.float32), position).astype(jnp.bfloat16)
    key_new = rotary(block[:, :, 1].astype(jnp.float32), position).astype(jnp.bfloat16)
    value_new = block[:, :, 2]
    mlp_count = lax.axis_size("mlp")
    weights_cat = jnp.concatenate([w_gate, w_up, jnp.transpose(w_down)], axis=1)
    weights_all = jnp.stack(
        [weights_cat]
        + [
            lax.ppermute(
                weights_cat, "mlp", [(m, (m + shift) % mlp_count) for m in range(mlp_count)]
            )
            for shift in range(1, mlp_count)
        ]
    )
    gathered = lax.all_gather(query.reshape(rows_here, width_here), "req", axis=0, tiled=True)
    eye = jnp.eye(heads_here, dtype=jnp.bfloat16)
    tail_diag = jnp.einsum("cthd,hg->chtgd", query, eye).reshape(
        conts_here, heads_here * 2, width_here
    )
    tail_acc, tail_top, tail_sum = tail_attention(tail_diag, tail_cache, tail_here, score_scale)
    gathered, tail_acc, tail_top, tail_sum, weights_all = lax.optimization_barrier(
        (gathered, tail_acc, tail_top, tail_sum, weights_all)
    )
    slot_ids = jnp.arange(req_count, dtype=jnp.int32)
    slot_of = jnp.sum(
        jnp.where(slot_part[None, :] == slot_ids[:, None], slot_ids[None, :], 0), axis=1
    )
    held_part = lax.dynamic_index_in_dim(slot_part, req_index, 0, keepdims=False)
    owned_prompt = held_part // 2
    held_half = held_part % 2
    span = prompt_cache.shape[1]
    owned_rows = 2 * rows_here
    q_owned = lax.dynamic_slice_in_dim(gathered, owned_prompt * owned_rows, owned_rows, 0).reshape(
        owned_rows, heads_here, HD
    )
    owned_len = lax.dynamic_index_in_dim(prompt_len, owned_prompt, 0, keepdims=False)
    valid_count = jnp.clip(owned_len - held_half * span, 0, span)
    q_diag = jnp.einsum("rhd,hg->hrgd", q_owned, eye).reshape(heads_here * owned_rows, width_here)
    prompt_acc, prompt_top, prompt_sum = prompt_attention(q_diag, prompt_cache, valid_count, score_scale)
    prompt_acc = prompt_acc.reshape(heads_here, owned_rows, heads_here, HD)
    owner_numer = jnp.stack([prompt_acc[h, :, h, :] for h in range(heads_here)], axis=1)
    top_f = jnp.transpose(prompt_top.reshape(heads_here, owned_rows))
    top_b = top_f.astype(jnp.bfloat16).astype(jnp.float32)
    rebase = jnp.where(top_f > 0.5 * masked_value, jnp.exp(top_f - top_b), 0.0)
    owner_total = jnp.transpose(prompt_sum.reshape(heads_here, owned_rows)) * rebase
    owner_numer = owner_numer * rebase[:, :, None]
    packed = jnp.concatenate(
        [owner_numer.reshape(owned_rows, width_here), owner_total, top_b], axis=1
    ).astype(jnp.bfloat16)
    outgoing = lax.dynamic_update_slice_in_dim(
        jnp.zeros((req_count, rows_here, packed.shape[1]), jnp.bfloat16),
        packed.reshape(2, rows_here, packed.shape[1]),
        2 * owned_prompt,
        0,
    )
    incoming = lax.all_to_all(outgoing, "req", split_axis=0, concat_axis=0, tiled=True)
    slot_first = lax.dynamic_index_in_dim(slot_of, 2 * own_prompt, 0, keepdims=False)
    slot_second = lax.dynamic_index_in_dim(slot_of, 2 * own_prompt + 1, 0, keepdims=False)

    def part_of(slot):
        piece = lax.dynamic_index_in_dim(incoming, slot, 0, keepdims=False).astype(jnp.float32)
        numer = piece[:, :width_here].reshape(rows_here, heads_here, HD)
        total = piece[:, width_here : width_here + heads_here]
        top = piece[:, width_here + heads_here :]
        return numer, total, top

    numer_first, total_first, max_first = part_of(slot_first)
    numer_second, total_second, max_second = part_of(slot_second)

    tail_acc = tail_acc.reshape(conts_here, heads_here, 2, heads_here, HD)
    cache_numer = jnp.stack([tail_acc[:, h, :, h, :] for h in range(heads_here)], axis=2)
    cache_top = tail_top.reshape(conts_here, heads_here, 2)
    cache_sum = tail_sum.reshape(conts_here, heads_here, 2)
    s_new = (
        jnp.einsum("cthd,cuhd->chtu", query, key_new, preferred_element_type=jnp.float32)
        * score_scale
    )
    causal = jnp.arange(2)[None, :] <= jnp.arange(2)[:, None]
    s_new = jnp.where(causal[None, None, :, :], s_new, masked_value)
    tail_max = jnp.maximum(cache_top, jnp.max(s_new, -1))
    cache_scale = jnp.exp(cache_top - tail_max)
    w_new = jnp.exp(s_new - tail_max[..., None])
    numer_tail = cache_numer * jnp.transpose(cache_scale, (0, 2, 1))[..., None]
    numer_tail = numer_tail + jnp.einsum(
        "chtu,cuhd->cthd", w_new.astype(jnp.bfloat16), value_new, preferred_element_type=jnp.float32
    )
    numer_tail = numer_tail.reshape(rows_here, heads_here, HD)
    total_tail = jnp.transpose(cache_sum * cache_scale + jnp.sum(w_new, -1), (0, 2, 1)).reshape(
        rows_here, heads_here
    )
    max_tail = jnp.transpose(tail_max, (0, 2, 1)).reshape(rows_here, heads_here)
    row_max = jnp.maximum(jnp.maximum(max_first, max_second), max_tail)
    scale_first = jnp.exp(max_first - row_max)
    scale_second = jnp.exp(max_second - row_max)
    scale_tail = jnp.exp(max_tail - row_max)
    row_total = total_first * scale_first + total_second * scale_second + total_tail * scale_tail
    row_numer = (
        numer_first * scale_first[..., None]
        + numer_second * scale_second[..., None]
        + numer_tail * scale_tail[..., None]
    )
    attn = (row_numer / row_total[:, :, None]).astype(jnp.bfloat16).reshape(rows_here, width_here)
    partial = jnp.dot(attn, w_out, preferred_element_type=jnp.float32)
    col_start = mlp_index * width_here
    own_cols = lax.dynamic_slice_in_dim(partial, col_start, width_here, 1)
    partial = lax.dynamic_update_slice_in_dim(
        partial, own_cols + residual.astype(jnp.float32), col_start, 1
    )
    share = rows_here // mlp_count
    state_share = lax.dynamic_slice_in_dim(partial, mlp_index * share, share, 0)
    for shift in range(1, mlp_count):
        target = (mlp_index + shift) % mlp_count
        state_share = state_share + lax.ppermute(
            lax.dynamic_slice_in_dim(partial, target * share, share, 0),
            "mlp",
            [(m, (m + shift) % mlp_count) for m in range(mlp_count)],
        )
    mean_square = jnp.mean(state_share * state_share, axis=1, keepdims=True)
    normed_share = (state_share * lax.rsqrt(mean_square + norm_eps) * mlp_gain).astype(jnp.bfloat16)
    piece = lax.all_to_all(
        jnp.broadcast_to(normed_share[None], (req_count,) + normed_share.shape),
        "req",
        split_axis=0,
        concat_axis=0,
        tiled=True,
    ).reshape(req_count * share, width)
    hidden_here = w_gate.shape[1]
    gate_w = weights_all[:, :, :hidden_here]
    up_w = weights_all[:, :, hidden_here : 2 * hidden_here]
    down_w = weights_all[:, :, 2 * hidden_here :]
    gate = jnp.einsum("rk,mkj->rmj", piece, gate_w, preferred_element_type=jnp.float32)
    upper = jnp.einsum("rk,mkj->rmj", piece, up_w, preferred_element_type=jnp.float32)
    hidden_all = (jax.nn.silu(gate) * upper).astype(jnp.bfloat16)
    down_sum = jnp.einsum("rmj,mfj->rf", hidden_all, down_w, preferred_element_type=jnp.float32)
    row_sums = jnp.sum(
        lax.all_to_all(
            down_sum.astype(jnp.bfloat16).reshape(req_count, share, width),
            "req",
            split_axis=0,
            concat_axis=0,
            tiled=True,
        ).astype(jnp.float32),
        axis=0,
    )
    final_share = state_share + row_sums
    final_square = jnp.mean(final_share * final_share, axis=1)
    final_dot = jnp.sum(final_share * final_gain * score_weight, axis=1)
    score_share = final_dot * lax.rsqrt(final_square + norm_eps)
    payload = jnp.concatenate(
        [
            final_share.reshape(share, mlp_count, width_here),
            jnp.broadcast_to(score_share[:, None, None], (share, mlp_count, 1)),
        ],
        axis=2,
    )
    arrived = lax.dynamic_update_slice_in_dim(
        jnp.zeros((rows_here, width_here + 1), jnp.float32),
        lax.dynamic_index_in_dim(payload, mlp_index, 1, keepdims=False),
        mlp_index * share,
        0,
    )
    for shift in range(1, mlp_count):
        target = (mlp_index + shift) % mlp_count
        source = (mlp_index + mlp_count - shift) % mlp_count
        got = lax.ppermute(
            lax.dynamic_index_in_dim(payload, target, 1, keepdims=False),
            "mlp",
            [(m, (m + shift) % mlp_count) for m in range(mlp_count)],
        )
        arrived = lax.dynamic_update_slice_in_dim(arrived, got, source * share, 0)
    out_rows = arrived[:, :width_here].astype(jnp.bfloat16)
    scores = arrived[:, width_here]
    return (out_rows, scores)


def solution(mesh):
    in_specs = (
        P("req", None, "mlp"),
        P("req", None, None, "mlp"),
        P("req", None, None, "mlp"),
        P("req", "mlp"),
        P("mlp", None),
        P(),
        P(None, ("req", "mlp")),
        P(None, ("req", "mlp")),
        P(("req", "mlp"), None),
        P(),
        P(),
        P(),
        P(),
        P(),
    )
    out_specs = (P("req", "mlp"), P("req"))
    return jax.shard_map(
        per_device, mesh=mesh, in_specs=in_specs, out_specs=out_specs, check_vma=False
    )
```

```python
import functools
import math

import jax
import jax.numpy as jnp
from jax import lax
from jax.experimental import pallas as pl
from jax.experimental.pallas import tpu as pltpu
from jax.sharding import PartitionSpec as P

HD = 96


norm_eps = 1e-05
masked_value = -1e30


def rotary(values, position):
    half_dim = HD // 2
    freqs = 10000.0 ** (-(jnp.arange(half_dim, dtype=jnp.float32) * 2.0) / HD)
    angles = position.astype(jnp.float32)[..., None] * freqs
    cosine = jnp.cos(angles)[..., None, :]
    sine = jnp.sin(angles)[..., None, :]
    first = values[..., :half_dim]
    second = values[..., half_dim:]
    return jnp.concatenate(
        [first * cosine - second * sine, second * cosine + first * sine], axis=-1
    )


def prompt_kernel(block_len, score_scale, valid_ref, q_ref, cache_ref, acc_ref, top_ref, sum_ref):
    number = pl.program_id(0)
    start = number * block_len

    @pl.when(number == 0)
    def _():
        acc_ref[...] = jnp.zeros_like(acc_ref)
        top_ref[...] = jnp.full_like(top_ref, masked_value)
        sum_ref[...] = jnp.zeros_like(sum_ref)

    @pl.when(start < valid_ref[0])
    def _():
        keys = cache_ref[:, 0, :]
        values = cache_ref[:, 1, :]
        places = start + lax.broadcasted_iota(jnp.int32, (1, block_len), 1)
        bias = jnp.where(places < valid_ref[0], 0.0, masked_value)
        scores = (
            lax.dot_general(
                q_ref[...], keys, (((1,), (1,)), ((), ())), preferred_element_type=jnp.float32
            )
            * score_scale
            + bias
        )
        top_old = top_ref[...]
        top_new = jnp.maximum(top_old, jnp.max(scores, axis=1, keepdims=True))
        shrink = jnp.exp(top_old - top_new)
        weights = jnp.exp(scores - top_new)
        sum_ref[...] = shrink * sum_ref[...] + jnp.sum(weights, axis=1, keepdims=True)
        acc_ref[...] = shrink * acc_ref[...] + jnp.dot(
            weights.astype(jnp.bfloat16), values, preferred_element_type=jnp.float32
        )
        top_ref[...] = top_new


def prompt_attention(q_diag, cache, valid_count, score_scale):
    span = cache.shape[1]
    block_len = min(1024, span)
    lanes = cache.shape[3]
    rows = q_diag.shape[0]

    def cache_block(number, valid):
        last = (valid[0] + block_len - 1) // block_len - 1
        return (0, jnp.maximum(jnp.minimum(number, last), 0), 0, 0)

    spec = pltpu.PrefetchScalarGridSpec(
        num_scalar_prefetch=1,
        grid=(span // block_len,),
        in_specs=[
            pl.BlockSpec((rows, lanes), lambda number, valid: (0, 0)),
            pl.BlockSpec((None, block_len, 2, lanes), cache_block),
        ],
        out_specs=[
            pl.BlockSpec((rows, lanes), lambda number, valid: (0, 0)),
            pl.BlockSpec((rows, 1), lambda number, valid: (0, 0)),
            pl.BlockSpec((rows, 1), lambda number, valid: (0, 0)),
        ],
    )
    return pl.pallas_call(
        functools.partial(prompt_kernel, block_len, score_scale),
        grid_spec=spec,
        cost_estimate=pl.CostEstimate(
            flops=4 * rows * lanes * span,
            transcendentals=rows * span,
            bytes_accessed=cache.size * 2 + rows * lanes * 6,
        ),
        out_shape=[
            jax.ShapeDtypeStruct((rows, lanes), jnp.float32),
            jax.ShapeDtypeStruct((rows, 1), jnp.float32),
            jax.ShapeDtypeStruct((rows, 1), jnp.float32),
        ],
    )(valid_count.reshape(1), q_diag, cache)


def tail_kernel(score_scale, lens_ref, q_ref, cache_ref, acc_ref, top_ref, sum_ref):
    number = pl.program_id(0)
    keys = cache_ref[:, 0, :]
    values = cache_ref[:, 1, :]
    scores = (
        lax.dot_general(q_ref[...], keys, (((1,), (1,)), ((), ())), preferred_element_type=jnp.float32)
        * score_scale
    )
    places = lax.broadcasted_iota(jnp.int32, scores.shape, 1)
    scores = jnp.where(places < lens_ref[number], scores, masked_value)
    top = jnp.max(scores, axis=1, keepdims=True)
    weights = jnp.exp(scores - top)
    top_ref[...] = top
    sum_ref[...] = jnp.sum(weights, axis=1, keepdims=True)
    acc_ref[...] = jnp.dot(weights.astype(jnp.bfloat16), values, preferred_element_type=jnp.float32)


def tail_attention(q_diag, cache, lens, score_scale):
    conts, rows, lanes = q_diag.shape
    cap = cache.shape[1]
    spec = pltpu.PrefetchScalarGridSpec(
        num_scalar_prefetch=1,
        grid=(conts,),
        in_specs=[
            pl.BlockSpec((None, rows, lanes), lambda number, lens: (number, 0, 0)),
            pl.BlockSpec((None, cap, 2, lanes), lambda number, lens: (number, 0, 0, 0)),
        ],
        out_specs=[
            pl.BlockSpec((None, rows, lanes), lambda number, lens: (number, 0, 0)),
            pl.BlockSpec((None, rows, 1), lambda number, lens: (number, 0, 0)),
            pl.BlockSpec((None, rows, 1), lambda number, lens: (number, 0, 0)),
        ],
    )
    return pl.pallas_call(
        functools.partial(tail_kernel, score_scale),
        grid_spec=spec,
        cost_estimate=pl.CostEstimate(
            flops=4 * conts * rows * lanes * cap,
            transcendentals=conts * rows * cap,
            bytes_accessed=cache.size * 2 + conts * rows * lanes * 6,
        ),
        out_shape=[
            jax.ShapeDtypeStruct((conts, rows, lanes), jnp.float32),
            jax.ShapeDtypeStruct((conts, rows, 1), jnp.float32),
            jax.ShapeDtypeStruct((conts, rows, 1), jnp.float32),
        ],
    )(lens, q_diag, cache)


def per_device(
    new_qkv,
    prompt_cache,
    tail_cache,
    residual,
    w_out,
    mlp_gain,
    w_gate,
    w_up,
    w_down,
    final_gain,
    score_weight,
    slot_part,
    prompt_len,
    tail_len,
):
    req_count = lax.axis_size("req")
    req_index = lax.axis_index("req")
    mlp_index = lax.axis_index("mlp")
    rows_here = new_qkv.shape[0]
    width_here = new_qkv.shape[2]
    heads_here = width_here // HD
    conts_here = rows_here // 2
    width = w_out.shape[1]
    score_scale = 1.0 / math.sqrt(HD)
    own_prompt = req_index // 2
    tail_here = lax.dynamic_slice_in_dim(tail_len, req_index * conts_here, conts_here)
    plen_here = lax.dynamic_index_in_dim(prompt_len, own_prompt, 0, keepdims=False)
    position = plen_here + tail_here[:, None] + jnp.arange(2, dtype=jnp.int32)[None, :]
    block = new_qkv.reshape(conts_here, 2, 3, heads_here, HD)
    query = rotary(block[:, :, 0].astype(jnp.float32), position).astype(jnp.bfloat16)
    key_new = rotary(block[:, :, 1].astype(jnp.float32), position).astype(jnp.bfloat16)
    value_new = block[:, :, 2]
    mlp_count = lax.axis_size("mlp")
    weights_cat = jnp.concatenate([w_gate, w_up, jnp.transpose(w_down)], axis=1)
    weights_all = jnp.stack(
        [weights_cat]
        + [
            lax.ppermute(
                weights_cat, "mlp", [(m, (m + shift) % mlp_count) for m in range(mlp_count)]
            )
            for shift in range(1, mlp_count)
        ]
    )
    gathered = lax.all_gather(query.reshape(rows_here, width_here), "req", axis=0, tiled=True)
    eye = jnp.eye(heads_here, dtype=jnp.bfloat16)
    tail_diag = jnp.einsum("cthd,hg->chtgd", query, eye).reshape(
        conts_here, heads_here * 2, width_here
    )
    tail_acc, tail_top, tail_sum = tail_attention(tail_diag, tail_cache, tail_here, score_scale)
    gathered, tail_acc, tail_top, tail_sum, weights_all = lax.optimization_barrier(
        (gathered, tail_acc, tail_top, tail_sum, weights_all)
    )
    slot_ids = jnp.arange(req_count, dtype=jnp.int32)
    slot_of = jnp.sum(
        jnp.where(slot_part[None, :] == slot_ids[:, None], slot_ids[None, :], 0), axis=1
    )
    held_part = lax.dynamic_index_in_dim(slot_part, req_index, 0, keepdims=False)
    owned_prompt = held_part // 2
    held_half = held_part % 2
    span = prompt_cache.shape[1]
    owned_rows = 2 * rows_here
    q_owned = lax.dynamic_slice_in_dim(gathered, owned_prompt * owned_rows, owned_rows, 0).reshape(
        owned_rows, heads_here, HD
    )
    owned_len = lax.dynamic_index_in_dim(prompt_len, owned_prompt, 0, keepdims=False)
    valid_count = jnp.clip(owned_len - held_half * span, 0, span)
    q_diag = jnp.einsum("rhd,hg->hrgd", q_owned, eye).reshape(heads_here * owned_rows, width_here)
    prompt_acc, prompt_top, prompt_sum = prompt_attention(q_diag, prompt_cache, valid_count, score_scale)
    prompt_acc = prompt_acc.reshape(heads_here, owned_rows, heads_here, HD)
    owner_numer = jnp.stack([prompt_acc[h, :, h, :] for h in range(heads_here)], axis=1)
    top_f = jnp.transpose(prompt_top.reshape(heads_here, owned_rows))
    top_b = top_f.astype(jnp.bfloat16).astype(jnp.float32)
    rebase = jnp.where(top_f > 0.5 * masked_value, jnp.exp(top_f - top_b), 0.0)
    owner_total = jnp.transpose(prompt_sum.reshape(heads_here, owned_rows)) * rebase
    owner_numer = owner_numer * rebase[:, :, None]
    packed = jnp.concatenate(
        [owner_numer.reshape(owned_rows, width_here), owner_total, top_b], axis=1
    ).astype(jnp.bfloat16)
    outgoing = lax.dynamic_update_slice_in_dim(
        jnp.zeros((req_count, rows_here, packed.shape[1]), jnp.bfloat16),
        packed.reshape(2, rows_here, packed.shape[1]),
        2 * owned_prompt,
        0,
    )
    incoming = lax.all_to_all(outgoing, "req", split_axis=0, concat_axis=0, tiled=True)
    slot_first = lax.dynamic_index_in_dim(slot_of, 2 * own_prompt, 0, keepdims=False)
    slot_second = lax.dynamic_index_in_dim(slot_of, 2 * own_prompt + 1, 0, keepdims=False)

    def part_of(slot):
        piece = lax.dynamic_index_in_dim(incoming, slot, 0, keepdims=False).astype(jnp.float32)
        numer = piece[:, :width_here].reshape(rows_here, heads_here, HD)
        total = piece[:, width_here : width_here + heads_here]
        top = piece[:, width_here + heads_here :]
        return numer, total, top

    numer_first, total_first, max_first = part_of(slot_first)
    numer_second, total_second, max_second = part_of(slot_second)

    tail_acc = tail_acc.reshape(conts_here, heads_here, 2, heads_here, HD)
    cache_numer = jnp.stack([tail_acc[:, h, :, h, :] for h in range(heads_here)], axis=2)
    cache_top = tail_top.reshape(conts_here, heads_here, 2)
    cache_sum = tail_sum.reshape(conts_here, heads_here, 2)
    s_new = (
        jnp.einsum("cthd,cuhd->chtu", query, key_new, preferred_element_type=jnp.float32)
        * score_scale
    )
    causal = jnp.arange(2)[None, :] <= jnp.arange(2)[:, None]
    s_new = jnp.where(causal[None, None, :, :], s_new, masked_value)
    tail_max = jnp.maximum(cache_top, jnp.max(s_new, -1))
    cache_scale = jnp.exp(cache_top - tail_max)
    w_new = jnp.exp(s_new - tail_max[..., None])
    numer_tail = cache_numer * jnp.transpose(cache_scale, (0, 2, 1))[..., None]
    numer_tail = numer_tail + jnp.einsum(
        "chtu,cuhd->cthd", w_new.astype(jnp.bfloat16), value_new, preferred_element_type=jnp.float32
    )
    numer_tail = numer_tail.reshape(rows_here, heads_here, HD)
    total_tail = jnp.transpose(cache_sum * cache_scale + jnp.sum(w_new, -1), (0, 2, 1)).reshape(
        rows_here, heads_here
    )
    max_tail = jnp.transpose(tail_max, (0, 2, 1)).reshape(rows_here, heads_here)
    row_max = jnp.maximum(jnp.maximum(max_first, max_second), max_tail)
    scale_first = jnp.exp(max_first - row_max)
    scale_second = jnp.exp(max_second - row_max)
    scale_tail = jnp.exp(max_tail - row_max)
    row_total = total_first * scale_first + total_second * scale_second + total_tail * scale_tail
    row_numer = (
        numer_first * scale_first[..., None]
        + numer_second * scale_second[..., None]
        + numer_tail * scale_tail[..., None]
    )
    attn = (row_numer / row_total[:, :, None]).astype(jnp.bfloat16).reshape(rows_here, width_here)
    partial = jnp.dot(attn, w_out, preferred_element_type=jnp.float32)
    col_start = mlp_index * width_here
    own_cols = lax.dynamic_slice_in_dim(partial, col_start, width_here, 1)
    partial = lax.dynamic_update_slice_in_dim(
        partial, own_cols + residual.astype(jnp.float32), col_start, 1
    )
    share = rows_here // mlp_count
    state_share = lax.dynamic_slice_in_dim(partial, mlp_index * share, share, 0)
    for shift in range(1, mlp_count):
        target = (mlp_index + shift) % mlp_count
        state_share = state_share + lax.ppermute(
            lax.dynamic_slice_in_dim(partial, target * share, share, 0),
            "mlp",
            [(m, (m + shift) % mlp_count) for m in range(mlp_count)],
        )
    mean_square = jnp.mean(state_share * state_share, axis=1, keepdims=True)
    normed_share = (state_share * lax.rsqrt(mean_square + norm_eps) * mlp_gain).astype(jnp.bfloat16)
    piece = lax.all_to_all(
        jnp.broadcast_to(normed_share[None], (req_count,) + normed_share.shape),
        "req",
        split_axis=0,
        concat_axis=0,
        tiled=True,
    ).reshape(req_count * share, width)
    hidden_here = w_gate.shape[1]
    gate_w = weights_all[:, :, :hidden_here]
    up_w = weights_all[:, :, hidden_here : 2 * hidden_here]
    down_w = weights_all[:, :, 2 * hidden_here :]
    gate = jnp.einsum("rk,mkj->rmj", piece, gate_w, preferred_element_type=jnp.float32)
    upper = jnp.einsum("rk,mkj->rmj", piece, up_w, preferred_element_type=jnp.float32)
    hidden_all = (jax.nn.silu(gate) * upper).astype(jnp.bfloat16)
    down_sum = jnp.einsum("rmj,mfj->rf", hidden_all, down_w, preferred_element_type=jnp.float32)
    row_sums = jnp.sum(
        lax.all_to_all(
            down_sum.astype(jnp.bfloat16).reshape(req_count, share, width),
            "req",
            split_axis=0,
            concat_axis=0,
            tiled=True,
        ).astype(jnp.float32),
        axis=0,
    )
    final_share = state_share + row_sums
    final_square = jnp.mean(final_share * final_share, axis=1)
    final_dot = jnp.sum(final_share * final_gain * score_weight, axis=1)
    score_share = final_dot * lax.rsqrt(final_square + norm_eps)
    payload = jnp.concatenate(
        [
            final_share.reshape(share, mlp_count, width_here),
            jnp.broadcast_to(score_share[:, None, None], (share, mlp_count, 1)),
        ],
        axis=2,
    )
    arrived = lax.dynamic_update_slice_in_dim(
        jnp.zeros((rows_here, width_here + 1), jnp.float32),
        lax.dynamic_index_in_dim(payload, mlp_index, 1, keepdims=False),
        mlp_index * share,
        0,
    )
    for shift in range(1, mlp_count):
        target = (mlp_index + shift) % mlp_count
        source = (mlp_index + mlp_count - shift) % mlp_count
        got = lax.ppermute(
            lax.dynamic_index_in_dim(payload, target, 1, keepdims=False),
            "mlp",
            [(m, (m + shift) % mlp_count) for m in range(mlp_count)],
        )
        arrived = lax.dynamic_update_slice_in_dim(arrived, got, source * share, 0)
    out_rows = arrived[:, :width_here].astype(jnp.bfloat16)
    scores = arrived[:, width_here]
    return (out_rows, scores)


def solution(mesh):
    in_specs = (
        P("req", None, "mlp"),
        P("req", None, None, "mlp"),
        P("req", None, None, "mlp"),
        P("req", "mlp"),
        P("mlp", None),
        P(),
        P(None, ("req", "mlp")),
        P(None, ("req", "mlp")),
        P(("req", "mlp"), None),
        P(),
        P(),
        P(),
        P(),
        P(),
    )
    out_specs = (P("req", "mlp"), P("req"))
    return jax.shard_map(
        per_device, mesh=mesh, in_specs=in_specs, out_specs=out_specs, check_vma=False
    )
```

```python
import functools
import math

import jax
import jax.numpy as jnp
from jax import lax
from jax.experimental import pallas as pl
from jax.experimental.pallas import tpu as pltpu
from jax.sharding import PartitionSpec as P

HD = 96


norm_eps = 1e-05
masked_value = -1e30


def rotary(values, position):
    half_dim = HD // 2
    freqs = 10000.0 ** (-(jnp.arange(half_dim, dtype=jnp.float32) * 2.0) / HD)
    angles = position.astype(jnp.float32)[..., None] * freqs
    cosine = jnp.cos(angles)[..., None, :]
    sine = jnp.sin(angles)[..., None, :]
    first = values[..., :half_dim]
    second = values[..., half_dim:]
    return jnp.concatenate(
        [first * cosine - second * sine, second * cosine + first * sine], axis=-1
    )


def prompt_kernel(block_len, score_scale, valid_ref, q_ref, cache_ref, acc_ref, top_ref, sum_ref):
    number = pl.program_id(0)
    start = number * block_len

    @pl.when(number == 0)
    def _():
        acc_ref[...] = jnp.zeros_like(acc_ref)
        top_ref[...] = jnp.full_like(top_ref, masked_value)
        sum_ref[...] = jnp.zeros_like(sum_ref)

    def step(masked):
        keys = cache_ref[:, 0, :]
        values = cache_ref[:, 1, :]
        scores = (
            lax.dot_general(
                q_ref[...], keys, (((1,), (1,)), ((), ())), preferred_element_type=jnp.float32
            )
            * score_scale
        )
        if masked:
            places = start + lax.broadcasted_iota(jnp.int32, scores.shape, 1)
            scores = jnp.where(places < valid_ref[0], scores, masked_value)
        top_old = top_ref[...]
        top_new = jnp.maximum(top_old, jnp.max(scores, axis=1, keepdims=True))
        shrink = jnp.exp(top_old - top_new)
        weights = jnp.exp(scores - top_new)
        sum_ref[...] = shrink * sum_ref[...] + jnp.sum(weights, axis=1, keepdims=True)
        acc_ref[...] = shrink * acc_ref[...] + jnp.dot(
            weights.astype(jnp.bfloat16), values, preferred_element_type=jnp.float32
        )
        top_ref[...] = top_new

    @pl.when(start + block_len <= valid_ref[0])
    def _():
        step(False)

    @pl.when(jnp.logical_and(start < valid_ref[0], start + block_len > valid_ref[0]))
    def _():
        step(True)


def prompt_attention(q_diag, cache, valid_count, score_scale):
    span = cache.shape[1]
    block_len = min(1024, span)
    lanes = cache.shape[3]
    rows = q_diag.shape[0]

    def cache_block(number, valid):
        last = (valid[0] + block_len - 1) // block_len - 1
        return (0, jnp.maximum(jnp.minimum(number, last), 0), 0, 0)

    spec = pltpu.PrefetchScalarGridSpec(
        num_scalar_prefetch=1,
        grid=(span // block_len,),
        in_specs=[
            pl.BlockSpec((rows, lanes), lambda number, valid: (0, 0)),
            pl.BlockSpec((None, block_len, 2, lanes), cache_block),
        ],
        out_specs=[
            pl.BlockSpec((rows, lanes), lambda number, valid: (0, 0)),
            pl.BlockSpec((rows, 1), lambda number, valid: (0, 0)),
            pl.BlockSpec((rows, 1), lambda number, valid: (0, 0)),
        ],
    )
    return pl.pallas_call(
        functools.partial(prompt_kernel, block_len, score_scale),
        grid_spec=spec,
        cost_estimate=pl.CostEstimate(
            flops=4 * rows * lanes * span,
            transcendentals=rows * span,
            bytes_accessed=cache.size * 2 + rows * lanes * 6,
        ),
        out_shape=[
            jax.ShapeDtypeStruct((rows, lanes), jnp.float32),
            jax.ShapeDtypeStruct((rows, 1), jnp.float32),
            jax.ShapeDtypeStruct((rows, 1), jnp.float32),
        ],
    )(valid_count.reshape(1), q_diag, cache)


def tail_kernel(score_scale, lens_ref, q_ref, cache_ref, acc_ref, top_ref, sum_ref):
    number = pl.program_id(0)
    keys = cache_ref[:, 0, :]
    values = cache_ref[:, 1, :]
    scores = (
        lax.dot_general(q_ref[...], keys, (((1,), (1,)), ((), ())), preferred_element_type=jnp.float32)
        * score_scale
    )
    places = lax.broadcasted_iota(jnp.int32, scores.shape, 1)
    scores = jnp.where(places < lens_ref[number], scores, masked_value)
    top = jnp.max(scores, axis=1, keepdims=True)
    weights = jnp.exp(scores - top)
    top_ref[...] = top
    sum_ref[...] = jnp.sum(weights, axis=1, keepdims=True)
    acc_ref[...] = jnp.dot(weights.astype(jnp.bfloat16), values, preferred_element_type=jnp.float32)


def tail_attention(q_diag, cache, lens, score_scale):
    conts, rows, lanes = q_diag.shape
    cap = cache.shape[1]
    spec = pltpu.PrefetchScalarGridSpec(
        num_scalar_prefetch=1,
        grid=(conts,),
        in_specs=[
            pl.BlockSpec((None, rows, lanes), lambda number, lens: (number, 0, 0)),
            pl.BlockSpec((None, cap, 2, lanes), lambda number, lens: (number, 0, 0, 0)),
        ],
        out_specs=[
            pl.BlockSpec((None, rows, lanes), lambda number, lens: (number, 0, 0)),
            pl.BlockSpec((None, rows, 1), lambda number, lens: (number, 0, 0)),
            pl.BlockSpec((None, rows, 1), lambda number, lens: (number, 0, 0)),
        ],
    )
    return pl.pallas_call(
        functools.partial(tail_kernel, score_scale),
        grid_spec=spec,
        cost_estimate=pl.CostEstimate(
            flops=4 * conts * rows * lanes * cap,
            transcendentals=conts * rows * cap,
            bytes_accessed=cache.size * 2 + conts * rows * lanes * 6,
        ),
        out_shape=[
            jax.ShapeDtypeStruct((conts, rows, lanes), jnp.float32),
            jax.ShapeDtypeStruct((conts, rows, 1), jnp.float32),
            jax.ShapeDtypeStruct((conts, rows, 1), jnp.float32),
        ],
    )(lens, q_diag, cache)


def per_device(
    new_qkv,
    prompt_cache,
    tail_cache,
    residual,
    w_out,
    mlp_gain,
    w_gate,
    w_up,
    w_down,
    final_gain,
    score_weight,
    slot_part,
    prompt_len,
    tail_len,
):
    req_count = lax.axis_size("req")
    req_index = lax.axis_index("req")
    mlp_index = lax.axis_index("mlp")
    rows_here = new_qkv.shape[0]
    width_here = new_qkv.shape[2]
    heads_here = width_here // HD
    conts_here = rows_here // 2
    width = w_out.shape[1]
    score_scale = 1.0 / math.sqrt(HD)
    own_prompt = req_index // 2
    tail_here = lax.dynamic_slice_in_dim(tail_len, req_index * conts_here, conts_here)
    plen_here = lax.dynamic_index_in_dim(prompt_len, own_prompt, 0, keepdims=False)
    position = plen_here + tail_here[:, None] + jnp.arange(2, dtype=jnp.int32)[None, :]
    block = new_qkv.reshape(conts_here, 2, 3, heads_here, HD)
    query = rotary(block[:, :, 0].astype(jnp.float32), position).astype(jnp.bfloat16)
    key_new = rotary(block[:, :, 1].astype(jnp.float32), position).astype(jnp.bfloat16)
    value_new = block[:, :, 2]
    mlp_count = lax.axis_size("mlp")
    weights_cat = jnp.concatenate([w_gate, w_up, jnp.transpose(w_down)], axis=1)
    ahead = [(m, (m + 1) % mlp_count) for m in range(mlp_count)]
    behind = [(m, (m + mlp_count - 1) % mlp_count) for m in range(mlp_count)]
    from_behind = lax.ppermute(weights_cat, "mlp", ahead)
    from_ahead = lax.ppermute(weights_cat, "mlp", behind)
    half = weights_cat.shape[1] // 2
    far = jnp.concatenate(
        [
            lax.ppermute(from_behind[:, :half], "mlp", ahead),
            lax.ppermute(from_ahead[:, half:], "mlp", behind),
        ],
        axis=1,
    )
    weights_all = jnp.stack([weights_cat, from_behind, far, from_ahead])
    gathered = lax.all_gather(query.reshape(rows_here, width_here), "req", axis=0, tiled=True)
    eye = jnp.eye(heads_here, dtype=jnp.bfloat16)
    tail_diag = jnp.einsum("cthd,hg->chtgd", query, eye).reshape(
        conts_here, heads_here * 2, width_here
    )
    tail_acc, tail_top, tail_sum = tail_attention(tail_diag, tail_cache, tail_here, score_scale)
    gathered, tail_acc, tail_top, tail_sum, weights_all = lax.optimization_barrier(
        (gathered, tail_acc, tail_top, tail_sum, weights_all)
    )
    slot_ids = jnp.arange(req_count, dtype=jnp.int32)
    slot_of = jnp.sum(
        jnp.where(slot_part[None, :] == slot_ids[:, None], slot_ids[None, :], 0), axis=1
    )
    held_part = lax.dynamic_index_in_dim(slot_part, req_index, 0, keepdims=False)
    owned_prompt = held_part // 2
    held_half = held_part % 2
    span = prompt_cache.shape[1]
    owned_rows = 2 * rows_here
    q_owned = lax.dynamic_slice_in_dim(gathered, owned_prompt * owned_rows, owned_rows, 0).reshape(
        owned_rows, heads_here, HD
    )
    owned_len = lax.dynamic_index_in_dim(prompt_len, owned_prompt, 0, keepdims=False)
    valid_count = jnp.clip(owned_len - held_half * span, 0, span)
    q_diag = jnp.einsum("rhd,hg->hrgd", q_owned, eye).reshape(heads_here * owned_rows, width_here)
    prompt_acc, prompt_top, prompt_sum = prompt_attention(q_diag, prompt_cache, valid_count, score_scale)
    prompt_acc = prompt_acc.reshape(heads_here, owned_rows, heads_here, HD)
    owner_numer = jnp.stack([prompt_acc[h, :, h, :] for h in range(heads_here)], axis=1)
    top_f = jnp.transpose(prompt_top.reshape(heads_here, owned_rows))
    top_b = top_f.astype(jnp.bfloat16).astype(jnp.float32)
    rebase = jnp.where(top_f > 0.5 * masked_value, jnp.exp(top_f - top_b), 0.0)
    owner_total = jnp.transpose(prompt_sum.reshape(heads_here, owned_rows)) * rebase
    owner_numer = owner_numer * rebase[:, :, None]
    packed = jnp.concatenate(
        [owner_numer.reshape(owned_rows, width_here), owner_total, top_b], axis=1
    ).astype(jnp.bfloat16)
    outgoing = lax.dynamic_update_slice_in_dim(
        jnp.zeros((req_count, rows_here, packed.shape[1]), jnp.bfloat16),
        packed.reshape(2, rows_here, packed.shape[1]),
        2 * owned_prompt,
        0,
    )
    incoming = lax.all_to_all(outgoing, "req", split_axis=0, concat_axis=0, tiled=True)
    slot_first = lax.dynamic_index_in_dim(slot_of, 2 * own_prompt, 0, keepdims=False)
    slot_second = lax.dynamic_index_in_dim(slot_of, 2 * own_prompt + 1, 0, keepdims=False)

    def part_of(slot):
        piece = lax.dynamic_index_in_dim(incoming, slot, 0, keepdims=False).astype(jnp.float32)
        numer = piece[:, :width_here].reshape(rows_here, heads_here, HD)
        total = piece[:, width_here : width_here + heads_here]
        top = piece[:, width_here + heads_here :]
        return numer, total, top

    numer_first, total_first, max_first = part_of(slot_first)
    numer_second, total_second, max_second = part_of(slot_second)

    tail_acc = tail_acc.reshape(conts_here, heads_here, 2, heads_here, HD)
    cache_numer = jnp.stack([tail_acc[:, h, :, h, :] for h in range(heads_here)], axis=2)
    cache_top = tail_top.reshape(conts_here, heads_here, 2)
    cache_sum = tail_sum.reshape(conts_here, heads_here, 2)
    s_new = (
        jnp.einsum("cthd,cuhd->chtu", query, key_new, preferred_element_type=jnp.float32)
        * score_scale
    )
    causal = jnp.arange(2)[None, :] <= jnp.arange(2)[:, None]
    s_new = jnp.where(causal[None, None, :, :], s_new, masked_value)
    tail_max = jnp.maximum(cache_top, jnp.max(s_new, -1))
    cache_scale = jnp.exp(cache_top - tail_max)
    w_new = jnp.exp(s_new - tail_max[..., None])
    numer_tail = cache_numer * jnp.transpose(cache_scale, (0, 2, 1))[..., None]
    numer_tail = numer_tail + jnp.einsum(
        "chtu,cuhd->cthd", w_new.astype(jnp.bfloat16), value_new, preferred_element_type=jnp.float32
    )
    numer_tail = numer_tail.reshape(rows_here, heads_here, HD)
    total_tail = jnp.transpose(cache_sum * cache_scale + jnp.sum(w_new, -1), (0, 2, 1)).reshape(
        rows_here, heads_here
    )
    max_tail = jnp.transpose(tail_max, (0, 2, 1)).reshape(rows_here, heads_here)
    row_max = jnp.maximum(jnp.maximum(max_first, max_second), max_tail)
    scale_first = jnp.exp(max_first - row_max)
    scale_second = jnp.exp(max_second - row_max)
    scale_tail = jnp.exp(max_tail - row_max)
    row_total = total_first * scale_first + total_second * scale_second + total_tail * scale_tail
    row_numer = (
        numer_first * scale_first[..., None]
        + numer_second * scale_second[..., None]
        + numer_tail * scale_tail[..., None]
    )
    attn = (row_numer / row_total[:, :, None]).astype(jnp.bfloat16).reshape(rows_here, width_here)
    partial = jnp.dot(attn, w_out, preferred_element_type=jnp.float32)
    col_start = mlp_index * width_here
    own_cols = lax.dynamic_slice_in_dim(partial, col_start, width_here, 1)
    partial = lax.dynamic_update_slice_in_dim(
        partial, own_cols + residual.astype(jnp.float32), col_start, 1
    )
    share = rows_here // mlp_count
    state_share = lax.dynamic_slice_in_dim(partial, mlp_index * share, share, 0)
    for shift in range(1, mlp_count):
        target = (mlp_index + shift) % mlp_count
        state_share = state_share + lax.ppermute(
            lax.dynamic_slice_in_dim(partial, target * share, share, 0),
            "mlp",
            [(m, (m + shift) % mlp_count) for m in range(mlp_count)],
        )
    mean_square = jnp.mean(state_share * state_share, axis=1, keepdims=True)
    normed_share = (state_share * lax.rsqrt(mean_square + norm_eps) * mlp_gain).astype(jnp.bfloat16)
    piece = lax.all_to_all(
        jnp.broadcast_to(normed_share[None], (req_count,) + normed_share.shape),
        "req",
        split_axis=0,
        concat_axis=0,
        tiled=True,
    ).reshape(req_count * share, width)
    hidden_here = w_gate.shape[1]
    gate_w = weights_all[:, :, :hidden_here]
    up_w = weights_all[:, :, hidden_here : 2 * hidden_here]
    down_w = weights_all[:, :, 2 * hidden_here :]
    gate = jnp.einsum("rk,mkj->rmj", piece, gate_w, preferred_element_type=jnp.float32)
    upper = jnp.einsum("rk,mkj->rmj", piece, up_w, preferred_element_type=jnp.float32)
    hidden_all = (jax.nn.silu(gate) * upper).astype(jnp.bfloat16)
    down_sum = jnp.einsum("rmj,mfj->rf", hidden_all, down_w, preferred_element_type=jnp.float32)
    row_sums = jnp.sum(
        lax.all_to_all(
            down_sum.astype(jnp.bfloat16).reshape(req_count, share, width),
            "req",
            split_axis=0,
            concat_axis=0,
            tiled=True,
        ).astype(jnp.float32),
        axis=0,
    )
    final_share = state_share + row_sums
    final_square = jnp.mean(final_share * final_share, axis=1)
    final_dot = jnp.sum(final_share * final_gain * score_weight, axis=1)
    score_share = final_dot * lax.rsqrt(final_square + norm_eps)
    payload = jnp.concatenate(
        [
            final_share.reshape(share, mlp_count, width_here),
            jnp.broadcast_to(score_share[:, None, None], (share, mlp_count, 1)),
        ],
        axis=2,
    )
    arrived = lax.dynamic_update_slice_in_dim(
        jnp.zeros((rows_here, width_here + 1), jnp.float32),
        lax.dynamic_index_in_dim(payload, mlp_index, 1, keepdims=False),
        mlp_index * share,
        0,
    )
    for shift in range(1, mlp_count):
        target = (mlp_index + shift) % mlp_count
        source = (mlp_index + mlp_count - shift) % mlp_count
        got = lax.ppermute(
            lax.dynamic_index_in_dim(payload, target, 1, keepdims=False),
            "mlp",
            [(m, (m + shift) % mlp_count) for m in range(mlp_count)],
        )
        arrived = lax.dynamic_update_slice_in_dim(arrived, got, source * share, 0)
    out_rows = arrived[:, :width_here].astype(jnp.bfloat16)
    scores = arrived[:, width_here]
    return (out_rows, scores)


def solution(mesh):
    in_specs = (
        P("req", None, "mlp"),
        P("req", None, None, "mlp"),
        P("req", None, None, "mlp"),
        P("req", "mlp"),
        P("mlp", None),
        P(),
        P(None, ("req", "mlp")),
        P(None, ("req", "mlp")),
        P(("req", "mlp"), None),
        P(),
        P(),
        P(),
        P(),
        P(),
    )
    out_specs = (P("req", "mlp"), P("req"))
    return jax.shard_map(
        per_device, mesh=mesh, in_specs=in_specs, out_specs=out_specs, check_vma=False
    )
```

```python
import functools
import math

import jax
import jax.numpy as jnp
from jax import lax
from jax.experimental import pallas as pl
from jax.experimental.pallas import tpu as pltpu
from jax.sharding import PartitionSpec as P

HD = 96


norm_eps = 1e-05
masked_value = -1e30


def rotary(values, position):
    half_dim = HD // 2
    freqs = 10000.0 ** (-(jnp.arange(half_dim, dtype=jnp.float32) * 2.0) / HD)
    angles = position.astype(jnp.float32)[..., None] * freqs
    cosine = jnp.cos(angles)[..., None, :]
    sine = jnp.sin(angles)[..., None, :]
    first = values[..., :half_dim]
    second = values[..., half_dim:]
    return jnp.concatenate(
        [first * cosine - second * sine, second * cosine + first * sine], axis=-1
    )


def prompt_kernel(block_len, score_scale, valid_ref, q_ref, cache_ref, acc_ref, top_ref, sum_ref):
    number = pl.program_id(0)
    start = number * block_len

    @pl.when(number == 0)
    def _():
        acc_ref[...] = jnp.zeros_like(acc_ref)
        top_ref[...] = jnp.full_like(top_ref, masked_value)
        sum_ref[...] = jnp.zeros_like(sum_ref)

    def step(masked):
        keys = cache_ref[:, 0, :]
        values = cache_ref[:, 1, :]
        scores = (
            lax.dot_general(
                q_ref[...], keys, (((1,), (1,)), ((), ())), preferred_element_type=jnp.float32
            )
            * score_scale
        )
        if masked:
            places = start + lax.broadcasted_iota(jnp.int32, scores.shape, 1)
            scores = jnp.where(places < valid_ref[0], scores, masked_value)
        top_old = top_ref[...]
        top_new = jnp.maximum(top_old, jnp.max(scores, axis=1, keepdims=True))
        shrink = jnp.exp(top_old - top_new)
        weights = jnp.exp(scores - top_new)
        sum_ref[...] = shrink * sum_ref[...] + jnp.sum(weights, axis=1, keepdims=True)
        acc_ref[...] = shrink * acc_ref[...] + jnp.dot(
            weights.astype(jnp.bfloat16), values, preferred_element_type=jnp.float32
        )
        top_ref[...] = top_new

    @pl.when(start + block_len <= valid_ref[0])
    def _():
        step(False)

    @pl.when(jnp.logical_and(start < valid_ref[0], start + block_len > valid_ref[0]))
    def _():
        step(True)


def prompt_attention(q_diag, cache, valid_count, score_scale):
    span = cache.shape[1]
    block_len = min(1024, span)
    lanes = cache.shape[3]
    rows = q_diag.shape[0]

    def cache_block(number, valid):
        last = (valid[0] + block_len - 1) // block_len - 1
        return (0, jnp.maximum(jnp.minimum(number, last), 0), 0, 0)

    spec = pltpu.PrefetchScalarGridSpec(
        num_scalar_prefetch=1,
        grid=(span // block_len,),
        in_specs=[
            pl.BlockSpec((rows, lanes), lambda number, valid: (0, 0)),
            pl.BlockSpec((None, block_len, 2, lanes), cache_block),
        ],
        out_specs=[
            pl.BlockSpec((rows, lanes), lambda number, valid: (0, 0)),
            pl.BlockSpec((rows, 1), lambda number, valid: (0, 0)),
            pl.BlockSpec((rows, 1), lambda number, valid: (0, 0)),
        ],
    )
    return pl.pallas_call(
        functools.partial(prompt_kernel, block_len, score_scale),
        grid_spec=spec,
        cost_estimate=pl.CostEstimate(
            flops=4 * rows * lanes * span,
            transcendentals=rows * span,
            bytes_accessed=cache.size * 2 + rows * lanes * 6,
        ),
        out_shape=[
            jax.ShapeDtypeStruct((rows, lanes), jnp.float32),
            jax.ShapeDtypeStruct((rows, 1), jnp.float32),
            jax.ShapeDtypeStruct((rows, 1), jnp.float32),
        ],
    )(valid_count.reshape(1), q_diag, cache)


def tail_kernel(score_scale, lens_ref, q_ref, cache_ref, acc_ref, top_ref, sum_ref):
    number = pl.program_id(0)
    keys = cache_ref[:, 0, :]
    values = cache_ref[:, 1, :]
    scores = (
        lax.dot_general(q_ref[...], keys, (((1,), (1,)), ((), ())), preferred_element_type=jnp.float32)
        * score_scale
    )
    places = lax.broadcasted_iota(jnp.int32, scores.shape, 1)
    scores = jnp.where(places < lens_ref[number], scores, masked_value)
    top = jnp.max(scores, axis=1, keepdims=True)
    weights = jnp.exp(scores - top)
    top_ref[...] = top
    sum_ref[...] = jnp.sum(weights, axis=1, keepdims=True)
    acc_ref[...] = jnp.dot(weights.astype(jnp.bfloat16), values, preferred_element_type=jnp.float32)


def tail_attention(q_diag, cache, lens, score_scale):
    conts, rows, lanes = q_diag.shape
    cap = cache.shape[1]
    spec = pltpu.PrefetchScalarGridSpec(
        num_scalar_prefetch=1,
        grid=(conts,),
        in_specs=[
            pl.BlockSpec((None, rows, lanes), lambda number, lens: (number, 0, 0)),
            pl.BlockSpec((None, cap, 2, lanes), lambda number, lens: (number, 0, 0, 0)),
        ],
        out_specs=[
            pl.BlockSpec((None, rows, lanes), lambda number, lens: (number, 0, 0)),
            pl.BlockSpec((None, rows, 1), lambda number, lens: (number, 0, 0)),
            pl.BlockSpec((None, rows, 1), lambda number, lens: (number, 0, 0)),
        ],
    )
    return pl.pallas_call(
        functools.partial(tail_kernel, score_scale),
        grid_spec=spec,
        cost_estimate=pl.CostEstimate(
            flops=4 * conts * rows * lanes * cap,
            transcendentals=conts * rows * cap,
            bytes_accessed=cache.size * 2 + conts * rows * lanes * 6,
        ),
        out_shape=[
            jax.ShapeDtypeStruct((conts, rows, lanes), jnp.float32),
            jax.ShapeDtypeStruct((conts, rows, 1), jnp.float32),
            jax.ShapeDtypeStruct((conts, rows, 1), jnp.float32),
        ],
    )(lens, q_diag, cache)


def per_device(
    new_qkv,
    prompt_cache,
    tail_cache,
    residual,
    w_out,
    mlp_gain,
    w_gate,
    w_up,
    w_down,
    final_gain,
    score_weight,
    slot_part,
    prompt_len,
    tail_len,
):
    req_count = lax.axis_size("req")
    req_index = lax.axis_index("req")
    mlp_index = lax.axis_index("mlp")
    rows_here = new_qkv.shape[0]
    width_here = new_qkv.shape[2]
    heads_here = width_here // HD
    conts_here = rows_here // 2
    width = w_out.shape[1]
    score_scale = 1.0 / math.sqrt(HD)
    own_prompt = req_index // 2
    tail_here = lax.dynamic_slice_in_dim(tail_len, req_index * conts_here, conts_here)
    plen_here = lax.dynamic_index_in_dim(prompt_len, own_prompt, 0, keepdims=False)
    position = plen_here + tail_here[:, None] + jnp.arange(2, dtype=jnp.int32)[None, :]
    block = new_qkv.reshape(conts_here, 2, 3, heads_here, HD)
    query = rotary(block[:, :, 0].astype(jnp.float32), position).astype(jnp.bfloat16)
    key_new = rotary(block[:, :, 1].astype(jnp.float32), position).astype(jnp.bfloat16)
    value_new = block[:, :, 2]
    mlp_count = lax.axis_size("mlp")
    weights_cat = jnp.concatenate([w_gate, w_up], axis=1)
    rings = [[(m, (m + shift) % mlp_count) for m in range(mlp_count)] for shift in range(1, mlp_count)]
    weights_all = jnp.stack([weights_cat] + [lax.ppermute(weights_cat, "mlp", ring) for ring in rings])
    down_w = jnp.stack([w_down] + [lax.ppermute(w_down, "mlp", ring) for ring in rings])
    gathered = lax.all_gather(query.reshape(rows_here, width_here), "req", axis=0, tiled=True)
    eye = jnp.eye(heads_here, dtype=jnp.bfloat16)
    tail_diag = jnp.einsum("cthd,hg->chtgd", query, eye).reshape(
        conts_here, heads_here * 2, width_here
    )
    tail_acc, tail_top, tail_sum = tail_attention(tail_diag, tail_cache, tail_here, score_scale)
    gathered, tail_acc, tail_top, tail_sum, weights_all = lax.optimization_barrier(
        (gathered, tail_acc, tail_top, tail_sum, weights_all)
    )
    slot_ids = jnp.arange(req_count, dtype=jnp.int32)
    slot_of = jnp.sum(
        jnp.where(slot_part[None, :] == slot_ids[:, None], slot_ids[None, :], 0), axis=1
    )
    held_part = lax.dynamic_index_in_dim(slot_part, req_index, 0, keepdims=False)
    owned_prompt = held_part // 2
    held_half = held_part % 2
    span = prompt_cache.shape[1]
    owned_rows = 2 * rows_here
    q_owned = lax.dynamic_slice_in_dim(gathered, owned_prompt * owned_rows, owned_rows, 0).reshape(
        owned_rows, heads_here, HD
    )
    owned_len = lax.dynamic_index_in_dim(prompt_len, owned_prompt, 0, keepdims=False)
    valid_count = jnp.clip(owned_len - held_half * span, 0, span)
    q_diag = jnp.einsum("rhd,hg->hrgd", q_owned, eye).reshape(heads_here * owned_rows, width_here)
    prompt_acc, prompt_top, prompt_sum = prompt_attention(q_diag, prompt_cache, valid_count, score_scale)
    prompt_acc = prompt_acc.reshape(heads_here, owned_rows, heads_here, HD)
    owner_numer = jnp.stack([prompt_acc[h, :, h, :] for h in range(heads_here)], axis=1)
    top_f = jnp.transpose(prompt_top.reshape(heads_here, owned_rows))
    top_b = top_f.astype(jnp.bfloat16).astype(jnp.float32)
    rebase = jnp.where(top_f > 0.5 * masked_value, jnp.exp(top_f - top_b), 0.0)
    owner_total = jnp.transpose(prompt_sum.reshape(heads_here, owned_rows)) * rebase
    owner_numer = owner_numer * rebase[:, :, None]
    packed = jnp.concatenate(
        [owner_numer.reshape(owned_rows, width_here), owner_total, top_b], axis=1
    ).astype(jnp.bfloat16)
    outgoing = lax.dynamic_update_slice_in_dim(
        jnp.zeros((req_count, rows_here, packed.shape[1]), jnp.bfloat16),
        packed.reshape(2, rows_here, packed.shape[1]),
        2 * owned_prompt,
        0,
    )
    incoming = lax.all_to_all(outgoing, "req", split_axis=0, concat_axis=0, tiled=True)
    slot_first = lax.dynamic_index_in_dim(slot_of, 2 * own_prompt, 0, keepdims=False)
    slot_second = lax.dynamic_index_in_dim(slot_of, 2 * own_prompt + 1, 0, keepdims=False)

    def part_of(slot):
        piece = lax.dynamic_index_in_dim(incoming, slot, 0, keepdims=False).astype(jnp.float32)
        numer = piece[:, :width_here].reshape(rows_here, heads_here, HD)
        total = piece[:, width_here : width_here + heads_here]
        top = piece[:, width_here + heads_here :]
        return numer, total, top

    numer_first, total_first, max_first = part_of(slot_first)
    numer_second, total_second, max_second = part_of(slot_second)

    tail_acc = tail_acc.reshape(conts_here, heads_here, 2, heads_here, HD)
    cache_numer = jnp.stack([tail_acc[:, h, :, h, :] for h in range(heads_here)], axis=2)
    cache_top = tail_top.reshape(conts_here, heads_here, 2)
    cache_sum = tail_sum.reshape(conts_here, heads_here, 2)
    s_new = (
        jnp.einsum("cthd,cuhd->chtu", query, key_new, preferred_element_type=jnp.float32)
        * score_scale
    )
    causal = jnp.arange(2)[None, :] <= jnp.arange(2)[:, None]
    s_new = jnp.where(causal[None, None, :, :], s_new, masked_value)
    tail_max = jnp.maximum(cache_top, jnp.max(s_new, -1))
    cache_scale = jnp.exp(cache_top - tail_max)
    w_new = jnp.exp(s_new - tail_max[..., None])
    numer_tail = cache_numer * jnp.transpose(cache_scale, (0, 2, 1))[..., None]
    numer_tail = numer_tail + jnp.einsum(
        "chtu,cuhd->cthd", w_new.astype(jnp.bfloat16), value_new, preferred_element_type=jnp.float32
    )
    numer_tail = numer_tail.reshape(rows_here, heads_here, HD)
    total_tail = jnp.transpose(cache_sum * cache_scale + jnp.sum(w_new, -1), (0, 2, 1)).reshape(
        rows_here, heads_here
    )
    max_tail = jnp.transpose(tail_max, (0, 2, 1)).reshape(rows_here, heads_here)
    row_max = jnp.maximum(jnp.maximum(max_first, max_second), max_tail)
    scale_first = jnp.exp(max_first - row_max)
    scale_second = jnp.exp(max_second - row_max)
    scale_tail = jnp.exp(max_tail - row_max)
    row_total = total_first * scale_first + total_second * scale_second + total_tail * scale_tail
    row_numer = (
        numer_first * scale_first[..., None]
        + numer_second * scale_second[..., None]
        + numer_tail * scale_tail[..., None]
    )
    attn = (row_numer / row_total[:, :, None]).astype(jnp.bfloat16).reshape(rows_here, width_here)
    partial = jnp.dot(attn, w_out, preferred_element_type=jnp.float32)
    col_start = mlp_index * width_here
    own_cols = lax.dynamic_slice_in_dim(partial, col_start, width_here, 1)
    partial = lax.dynamic_update_slice_in_dim(
        partial, own_cols + residual.astype(jnp.float32), col_start, 1
    )
    share = rows_here // mlp_count
    state_share = lax.dynamic_slice_in_dim(partial, mlp_index * share, share, 0)
    for shift in range(1, mlp_count):
        target = (mlp_index + shift) % mlp_count
        state_share = state_share + lax.ppermute(
            lax.dynamic_slice_in_dim(partial, target * share, share, 0),
            "mlp",
            [(m, (m + shift) % mlp_count) for m in range(mlp_count)],
        )
    mean_square = jnp.mean(state_share * state_share, axis=1, keepdims=True)
    normed_share = (state_share * lax.rsqrt(mean_square + norm_eps) * mlp_gain).astype(jnp.bfloat16)
    piece = lax.all_to_all(
        jnp.broadcast_to(normed_share[None], (req_count,) + normed_share.shape),
        "req",
        split_axis=0,
        concat_axis=0,
        tiled=True,
    ).reshape(req_count * share, width)
    hidden_here = w_gate.shape[1]
    gate_w = weights_all[:, :, :hidden_here]
    up_w = weights_all[:, :, hidden_here : 2 * hidden_here]
    gate = jnp.einsum("rk,mkj->rmj", piece, gate_w, preferred_element_type=jnp.float32)
    upper = jnp.einsum("rk,mkj->rmj", piece, up_w, preferred_element_type=jnp.float32)
    hidden_all = (jax.nn.silu(gate) * upper).astype(jnp.bfloat16)
    down_sum = jnp.einsum("rmj,mjf->rf", hidden_all, down_w, preferred_element_type=jnp.float32)
    row_sums = jnp.sum(
        lax.all_to_all(
            down_sum.astype(jnp.bfloat16).reshape(req_count, share, width),
            "req",
            split_axis=0,
            concat_axis=0,
            tiled=True,
        ).astype(jnp.float32),
        axis=0,
    )
    final_share = state_share + row_sums
    final_square = jnp.mean(final_share * final_share, axis=1)
    final_dot = jnp.sum(final_share * final_gain * score_weight, axis=1)
    score_share = final_dot * lax.rsqrt(final_square + norm_eps)
    payload = jnp.concatenate(
        [
            final_share.reshape(share, mlp_count, width_here),
            jnp.broadcast_to(score_share[:, None, None], (share, mlp_count, 1)),
        ],
        axis=2,
    )
    arrived = lax.dynamic_update_slice_in_dim(
        jnp.zeros((rows_here, width_here + 1), jnp.float32),
        lax.dynamic_index_in_dim(payload, mlp_index, 1, keepdims=False),
        mlp_index * share,
        0,
    )
    for shift in range(1, mlp_count):
        target = (mlp_index + shift) % mlp_count
        source = (mlp_index + mlp_count - shift) % mlp_count
        got = lax.ppermute(
            lax.dynamic_index_in_dim(payload, target, 1, keepdims=False),
            "mlp",
            [(m, (m + shift) % mlp_count) for m in range(mlp_count)],
        )
        arrived = lax.dynamic_update_slice_in_dim(arrived, got, source * share, 0)
    out_rows = arrived[:, :width_here].astype(jnp.bfloat16)
    scores = arrived[:, width_here]
    return (out_rows, scores)


def solution(mesh):
    in_specs = (
        P("req", None, "mlp"),
        P("req", None, None, "mlp"),
        P("req", None, None, "mlp"),
        P("req", "mlp"),
        P("mlp", None),
        P(),
        P(None, ("req", "mlp")),
        P(None, ("req", "mlp")),
        P(("req", "mlp"), None),
        P(),
        P(),
        P(),
        P(),
        P(),
    )
    out_specs = (P("req", "mlp"), P("req"))
    return jax.shard_map(
        per_device, mesh=mesh, in_specs=in_specs, out_specs=out_specs, check_vma=False
    )
```

```python
import functools
import math

import jax
import jax.numpy as jnp
from jax import lax
from jax.experimental import pallas as pl
from jax.experimental.pallas import tpu as pltpu
from jax.sharding import PartitionSpec as P

HD = 96


norm_eps = 1e-05
masked_value = -1e30


def rotary(values, position):
    half_dim = HD // 2
    freqs = 10000.0 ** (-(jnp.arange(half_dim, dtype=jnp.float32) * 2.0) / HD)
    angles = position.astype(jnp.float32)[..., None] * freqs
    cosine = jnp.cos(angles)[..., None, :]
    sine = jnp.sin(angles)[..., None, :]
    first = values[..., :half_dim]
    second = values[..., half_dim:]
    return jnp.concatenate(
        [first * cosine - second * sine, second * cosine + first * sine], axis=-1
    )


def prompt_kernel(block_len, score_scale, valid_ref, q_ref, cache_ref, acc_ref, top_ref, sum_ref):
    number = pl.program_id(0)
    start = number * block_len

    @pl.when(number == 0)
    def _():
        acc_ref[...] = jnp.zeros_like(acc_ref)
        top_ref[...] = jnp.full_like(top_ref, masked_value)
        sum_ref[...] = jnp.zeros_like(sum_ref)

    @pl.when(start < valid_ref[0])
    def _():
        keys = cache_ref[:, 0, :]
        values = cache_ref[:, 1, :]
        places = start + lax.broadcasted_iota(jnp.int32, (1, block_len), 1)
        bias = jnp.where(places < valid_ref[0], 0.0, masked_value)
        scores = (
            lax.dot_general(
                q_ref[...], keys, (((1,), (1,)), ((), ())), preferred_element_type=jnp.float32
            )
            * score_scale
            + bias
        )
        top_old = top_ref[...]
        top_new = jnp.maximum(top_old, jnp.max(scores, axis=1, keepdims=True))
        shrink = jnp.exp(top_old - top_new)
        weights = jnp.exp(scores - top_new)
        sum_ref[...] = shrink * sum_ref[...] + jnp.sum(weights, axis=1, keepdims=True)
        acc_ref[...] = shrink * acc_ref[...] + jnp.dot(
            weights.astype(jnp.bfloat16), values, preferred_element_type=jnp.float32
        )
        top_ref[...] = top_new


def prompt_attention(q_diag, cache, valid_count, score_scale):
    span = cache.shape[1]
    block_len = min(1024, span)
    lanes = cache.shape[3]
    rows = q_diag.shape[0]

    def cache_block(number, valid):
        last = (valid[0] + block_len - 1) // block_len - 1
        return (0, jnp.maximum(jnp.minimum(number, last), 0), 0, 0)

    spec = pltpu.PrefetchScalarGridSpec(
        num_scalar_prefetch=1,
        grid=(span // block_len,),
        in_specs=[
            pl.BlockSpec((rows, lanes), lambda number, valid: (0, 0)),
            pl.BlockSpec((None, block_len, 2, lanes), cache_block),
        ],
        out_specs=[
            pl.BlockSpec((rows, lanes), lambda number, valid: (0, 0)),
            pl.BlockSpec((rows, 1), lambda number, valid: (0, 0)),
            pl.BlockSpec((rows, 1), lambda number, valid: (0, 0)),
        ],
    )
    return pl.pallas_call(
        functools.partial(prompt_kernel, block_len, score_scale),
        grid_spec=spec,
        cost_estimate=pl.CostEstimate(
            flops=4 * rows * lanes * span,
            transcendentals=rows * span,
            bytes_accessed=cache.size * 2 + rows * lanes * 6,
        ),
        out_shape=[
            jax.ShapeDtypeStruct((rows, lanes), jnp.float32),
            jax.ShapeDtypeStruct((rows, 1), jnp.float32),
            jax.ShapeDtypeStruct((rows, 1), jnp.float32),
        ],
    )(valid_count.reshape(1), q_diag, cache)


def tail_kernel(score_scale, lens_ref, q_ref, cache_ref, acc_ref, top_ref, sum_ref):
    number = pl.program_id(0)
    keys = cache_ref[:, 0, :]
    values = cache_ref[:, 1, :]
    scores = (
        lax.dot_general(q_ref[...], keys, (((1,), (1,)), ((), ())), preferred_element_type=jnp.float32)
        * score_scale
    )
    places = lax.broadcasted_iota(jnp.int32, scores.shape, 1)
    scores = jnp.where(places < lens_ref[number], scores, masked_value)
    top = jnp.max(scores, axis=1, keepdims=True)
    weights = jnp.exp(scores - top)
    top_ref[...] = top
    sum_ref[...] = jnp.sum(weights, axis=1, keepdims=True)
    acc_ref[...] = jnp.dot(weights.astype(jnp.bfloat16), values, preferred_element_type=jnp.float32)


def tail_attention(q_diag, cache, lens, score_scale):
    conts, rows, lanes = q_diag.shape
    cap = cache.shape[1]
    spec = pltpu.PrefetchScalarGridSpec(
        num_scalar_prefetch=1,
        grid=(conts,),
        in_specs=[
            pl.BlockSpec((None, rows, lanes), lambda number, lens: (number, 0, 0)),
            pl.BlockSpec((None, cap, 2, lanes), lambda number, lens: (number, 0, 0, 0)),
        ],
        out_specs=[
            pl.BlockSpec((None, rows, lanes), lambda number, lens: (number, 0, 0)),
            pl.BlockSpec((None, rows, 1), lambda number, lens: (number, 0, 0)),
            pl.BlockSpec((None, rows, 1), lambda number, lens: (number, 0, 0)),
        ],
    )
    return pl.pallas_call(
        functools.partial(tail_kernel, score_scale),
        grid_spec=spec,
        cost_estimate=pl.CostEstimate(
            flops=4 * conts * rows * lanes * cap,
            transcendentals=conts * rows * cap,
            bytes_accessed=cache.size * 2 + conts * rows * lanes * 6,
        ),
        out_shape=[
            jax.ShapeDtypeStruct((conts, rows, lanes), jnp.float32),
            jax.ShapeDtypeStruct((conts, rows, 1), jnp.float32),
            jax.ShapeDtypeStruct((conts, rows, 1), jnp.float32),
        ],
    )(lens, q_diag, cache)


def per_device(
    new_qkv,
    prompt_cache,
    tail_cache,
    residual,
    w_out,
    mlp_gain,
    w_gate,
    w_up,
    w_down,
    final_gain,
    score_weight,
    slot_part,
    prompt_len,
    tail_len,
):
    req_count = lax.axis_size("req")
    req_index = lax.axis_index("req")
    mlp_index = lax.axis_index("mlp")
    rows_here = new_qkv.shape[0]
    width_here = new_qkv.shape[2]
    heads_here = width_here // HD
    conts_here = rows_here // 2
    width = w_out.shape[1]
    score_scale = 1.0 / math.sqrt(HD)
    own_prompt = req_index // 2
    tail_here = lax.dynamic_slice_in_dim(tail_len, req_index * conts_here, conts_here)
    plen_here = lax.dynamic_index_in_dim(prompt_len, own_prompt, 0, keepdims=False)
    position = plen_here + tail_here[:, None] + jnp.arange(2, dtype=jnp.int32)[None, :]
    block = new_qkv.reshape(conts_here, 2, 3, heads_here, HD)
    query = rotary(block[:, :, 0].astype(jnp.float32), position).astype(jnp.bfloat16)
    key_new = rotary(block[:, :, 1].astype(jnp.float32), position).astype(jnp.bfloat16)
    value_new = block[:, :, 2]
    mlp_count = lax.axis_size("mlp")
    weights_cat = jnp.concatenate([w_gate, w_up], axis=1)
    rings = [[(m, (m + shift) % mlp_count) for m in range(mlp_count)] for shift in range(1, mlp_count)]
    weights_all = jnp.stack([weights_cat] + [lax.ppermute(weights_cat, "mlp", ring) for ring in rings])
    down_w = jnp.stack([w_down] + [lax.ppermute(w_down, "mlp", ring) for ring in rings])
    gathered = lax.all_gather(query.reshape(rows_here, width_here), "req", axis=0, tiled=True)
    eye = jnp.eye(heads_here, dtype=jnp.bfloat16)
    tail_diag = jnp.einsum("cthd,hg->chtgd", query, eye).reshape(
        conts_here, heads_here * 2, width_here
    )
    tail_acc, tail_top, tail_sum = tail_attention(tail_diag, tail_cache, tail_here, score_scale)
    gathered, tail_acc, tail_top, tail_sum, weights_all = lax.optimization_barrier(
        (gathered, tail_acc, tail_top, tail_sum, weights_all)
    )
    slot_ids = jnp.arange(req_count, dtype=jnp.int32)
    slot_of = jnp.sum(
        jnp.where(slot_part[None, :] == slot_ids[:, None], slot_ids[None, :], 0), axis=1
    )
    held_part = lax.dynamic_index_in_dim(slot_part, req_index, 0, keepdims=False)
    owned_prompt = held_part // 2
    held_half = held_part % 2
    span = prompt_cache.shape[1]
    owned_rows = 2 * rows_here
    q_owned = lax.dynamic_slice_in_dim(gathered, owned_prompt * owned_rows, owned_rows, 0).reshape(
        owned_rows, heads_here, HD
    )
    owned_len = lax.dynamic_index_in_dim(prompt_len, owned_prompt, 0, keepdims=False)
    valid_count = jnp.clip(owned_len - held_half * span, 0, span)
    q_diag = jnp.einsum("rhd,hg->hrgd", q_owned, eye).reshape(heads_here * owned_rows, width_here)
    prompt_acc, prompt_top, prompt_sum = prompt_attention(q_diag, prompt_cache, valid_count, score_scale)
    prompt_acc = prompt_acc.reshape(heads_here, owned_rows, heads_here, HD)
    owner_numer = jnp.stack([prompt_acc[h, :, h, :] for h in range(heads_here)], axis=1)
    top_f = jnp.transpose(prompt_top.reshape(heads_here, owned_rows))
    top_b = top_f.astype(jnp.bfloat16).astype(jnp.float32)
    rebase = jnp.where(top_f > 0.5 * masked_value, jnp.exp(top_f - top_b), 0.0)
    owner_total = jnp.transpose(prompt_sum.reshape(heads_here, owned_rows)) * rebase
    owner_numer = owner_numer * rebase[:, :, None]
    packed = jnp.concatenate(
        [owner_numer.reshape(owned_rows, width_here), owner_total, top_b], axis=1
    ).astype(jnp.bfloat16)
    outgoing = lax.dynamic_update_slice_in_dim(
        jnp.zeros((req_count, rows_here, packed.shape[1]), jnp.bfloat16),
        packed.reshape(2, rows_here, packed.shape[1]),
        2 * owned_prompt,
        0,
    )
    incoming = lax.all_to_all(outgoing, "req", split_axis=0, concat_axis=0, tiled=True)
    slot_first = lax.dynamic_index_in_dim(slot_of, 2 * own_prompt, 0, keepdims=False)
    slot_second = lax.dynamic_index_in_dim(slot_of, 2 * own_prompt + 1, 0, keepdims=False)

    def part_of(slot):
        piece = lax.dynamic_index_in_dim(incoming, slot, 0, keepdims=False).astype(jnp.float32)
        numer = piece[:, :width_here].reshape(rows_here, heads_here, HD)
        total = piece[:, width_here : width_here + heads_here]
        top = piece[:, width_here + heads_here :]
        return numer, total, top

    numer_first, total_first, max_first = part_of(slot_first)
    numer_second, total_second, max_second = part_of(slot_second)

    tail_acc = tail_acc.reshape(conts_here, heads_here, 2, heads_here, HD)
    cache_numer = jnp.stack([tail_acc[:, h, :, h, :] for h in range(heads_here)], axis=2)
    cache_top = tail_top.reshape(conts_here, heads_here, 2)
    cache_sum = tail_sum.reshape(conts_here, heads_here, 2)
    s_new = (
        jnp.einsum("cthd,cuhd->chtu", query, key_new, preferred_element_type=jnp.float32)
        * score_scale
    )
    causal = jnp.arange(2)[None, :] <= jnp.arange(2)[:, None]
    s_new = jnp.where(causal[None, None, :, :], s_new, masked_value)
    tail_max = jnp.maximum(cache_top, jnp.max(s_new, -1))
    cache_scale = jnp.exp(cache_top - tail_max)
    w_new = jnp.exp(s_new - tail_max[..., None])
    numer_tail = cache_numer * jnp.transpose(cache_scale, (0, 2, 1))[..., None]
    numer_tail = numer_tail + jnp.einsum(
        "chtu,cuhd->cthd", w_new.astype(jnp.bfloat16), value_new, preferred_element_type=jnp.float32
    )
    numer_tail = numer_tail.reshape(rows_here, heads_here, HD)
    total_tail = jnp.transpose(cache_sum * cache_scale + jnp.sum(w_new, -1), (0, 2, 1)).reshape(
        rows_here, heads_here
    )
    max_tail = jnp.transpose(tail_max, (0, 2, 1)).reshape(rows_here, heads_here)
    row_max = jnp.maximum(jnp.maximum(max_first, max_second), max_tail)
    scale_first = jnp.exp(max_first - row_max)
    scale_second = jnp.exp(max_second - row_max)
    scale_tail = jnp.exp(max_tail - row_max)
    row_total = total_first * scale_first + total_second * scale_second + total_tail * scale_tail
    row_numer = (
        numer_first * scale_first[..., None]
        + numer_second * scale_second[..., None]
        + numer_tail * scale_tail[..., None]
    )
    attn = (row_numer / row_total[:, :, None]).astype(jnp.bfloat16).reshape(rows_here, width_here)
    partial = jnp.dot(attn, w_out, preferred_element_type=jnp.float32)
    col_start = mlp_index * width_here
    own_cols = lax.dynamic_slice_in_dim(partial, col_start, width_here, 1)
    partial = lax.dynamic_update_slice_in_dim(
        partial, own_cols + residual.astype(jnp.float32), col_start, 1
    )
    share = rows_here // mlp_count
    state_share = lax.dynamic_slice_in_dim(partial, mlp_index * share, share, 0)
    for shift in range(1, mlp_count):
        target = (mlp_index + shift) % mlp_count
        state_share = state_share + lax.ppermute(
            lax.dynamic_slice_in_dim(partial, target * share, share, 0),
            "mlp",
            [(m, (m + shift) % mlp_count) for m in range(mlp_count)],
        )
    mean_square = jnp.mean(state_share * state_share, axis=1, keepdims=True)
    normed_share = (state_share * lax.rsqrt(mean_square + norm_eps) * mlp_gain).astype(jnp.bfloat16)
    piece = lax.all_to_all(
        jnp.broadcast_to(normed_share[None], (req_count,) + normed_share.shape),
        "req",
        split_axis=0,
        concat_axis=0,
        tiled=True,
    ).reshape(req_count * share, width)
    hidden_here = w_gate.shape[1]
    gate_w = weights_all[:, :, :hidden_here]
    up_w = weights_all[:, :, hidden_here : 2 * hidden_here]
    gate = jnp.einsum("rk,mkj->rmj", piece, gate_w, preferred_element_type=jnp.float32)
    upper = jnp.einsum("rk,mkj->rmj", piece, up_w, preferred_element_type=jnp.float32)
    hidden_all = (jax.nn.silu(gate) * upper).astype(jnp.bfloat16)
    down_sum = jnp.einsum("rmj,mjf->rf", hidden_all, down_w, preferred_element_type=jnp.float32)
    row_sums = jnp.sum(
        lax.all_to_all(
            down_sum.astype(jnp.bfloat16).reshape(req_count, share, width),
            "req",
            split_axis=0,
            concat_axis=0,
            tiled=True,
        ).astype(jnp.float32),
        axis=0,
    )
    final_share = state_share + row_sums
    final_square = jnp.mean(final_share * final_share, axis=1)
    final_dot = jnp.sum(final_share * final_gain * score_weight, axis=1)
    score_share = final_dot * lax.rsqrt(final_square + norm_eps)
    payload = jnp.concatenate(
        [
            final_share.reshape(share, mlp_count, width_here),
            jnp.broadcast_to(score_share[:, None, None], (share, mlp_count, 1)),
        ],
        axis=2,
    )
    arrived = lax.dynamic_update_slice_in_dim(
        jnp.zeros((rows_here, width_here + 1), jnp.float32),
        lax.dynamic_index_in_dim(payload, mlp_index, 1, keepdims=False),
        mlp_index * share,
        0,
    )
    for shift in range(1, mlp_count):
        target = (mlp_index + shift) % mlp_count
        source = (mlp_index + mlp_count - shift) % mlp_count
        got = lax.ppermute(
            lax.dynamic_index_in_dim(payload, target, 1, keepdims=False),
            "mlp",
            [(m, (m + shift) % mlp_count) for m in range(mlp_count)],
        )
        arrived = lax.dynamic_update_slice_in_dim(arrived, got, source * share, 0)
    out_rows = arrived[:, :width_here].astype(jnp.bfloat16)
    scores = arrived[:, width_here]
    return (out_rows, scores)


def solution(mesh):
    in_specs = (
        P("req", None, "mlp"),
        P("req", None, None, "mlp"),
        P("req", None, None, "mlp"),
        P("req", "mlp"),
        P("mlp", None),
        P(),
        P(None, ("req", "mlp")),
        P(None, ("req", "mlp")),
        P(("req", "mlp"), None),
        P(),
        P(),
        P(),
        P(),
        P(),
    )
    out_specs = (P("req", "mlp"), P("req"))
    return jax.shard_map(
        per_device, mesh=mesh, in_specs=in_specs, out_specs=out_specs, check_vma=False
    )
```

```python
import functools
import math

import jax
import jax.numpy as jnp
from jax import lax
from jax.experimental import pallas as pl
from jax.experimental.pallas import tpu as pltpu
from jax.sharding import PartitionSpec as P

HD = 96


norm_eps = 1e-05
masked_value = -1e30


def rotary(values, position):
    half_dim = HD // 2
    freqs = 10000.0 ** (-(jnp.arange(half_dim, dtype=jnp.float32) * 2.0) / HD)
    angles = position.astype(jnp.float32)[..., None] * freqs
    cosine = jnp.cos(angles)[..., None, :]
    sine = jnp.sin(angles)[..., None, :]
    first = values[..., :half_dim]
    second = values[..., half_dim:]
    return jnp.concatenate(
        [first * cosine - second * sine, second * cosine + first * sine], axis=-1
    )


def prompt_kernel(block_len, score_scale, valid_ref, q_ref, cache_ref, acc_ref, top_ref, sum_ref):
    number = pl.program_id(0)
    start = number * block_len

    @pl.when(number == 0)
    def _():
        acc_ref[...] = jnp.zeros_like(acc_ref)
        top_ref[...] = jnp.full_like(top_ref, masked_value)
        sum_ref[...] = jnp.zeros_like(sum_ref)

    @pl.when(start < valid_ref[0])
    def _():
        keys = cache_ref[:, 0, :]
        values = cache_ref[:, 1, :]
        places = start + lax.broadcasted_iota(jnp.int32, (1, block_len), 1)
        bias = jnp.where(places < valid_ref[0], 0.0, masked_value)
        scores = (
            lax.dot_general(
                q_ref[...], keys, (((1,), (1,)), ((), ())), preferred_element_type=jnp.float32
            )
            * score_scale
            + bias
        )
        top_old = top_ref[...]
        top_new = jnp.maximum(top_old, jnp.max(scores, axis=1, keepdims=True))
        shrink = jnp.exp(top_old - top_new)
        weights = jnp.exp(scores - top_new)
        sum_ref[...] = shrink * sum_ref[...] + jnp.sum(weights, axis=1, keepdims=True)
        acc_ref[...] = shrink * acc_ref[...] + jnp.dot(
            weights.astype(jnp.bfloat16), values, preferred_element_type=jnp.float32
        )
        top_ref[...] = top_new


def prompt_attention(q_diag, cache, valid_count, score_scale):
    span = cache.shape[1]
    block_len = min(1024, span)
    lanes = cache.shape[3]
    rows = q_diag.shape[0]

    def cache_block(number, valid):
        last = (valid[0] + block_len - 1) // block_len - 1
        return (0, jnp.maximum(jnp.minimum(number, last), 0), 0, 0)

    spec = pltpu.PrefetchScalarGridSpec(
        num_scalar_prefetch=1,
        grid=(span // block_len,),
        in_specs=[
            pl.BlockSpec((rows, lanes), lambda number, valid: (0, 0)),
            pl.BlockSpec((None, block_len, 2, lanes), cache_block),
        ],
        out_specs=[
            pl.BlockSpec((rows, lanes), lambda number, valid: (0, 0)),
            pl.BlockSpec((rows, 1), lambda number, valid: (0, 0)),
            pl.BlockSpec((rows, 1), lambda number, valid: (0, 0)),
        ],
    )
    return pl.pallas_call(
        functools.partial(prompt_kernel, block_len, score_scale),
        grid_spec=spec,
        cost_estimate=pl.CostEstimate(
            flops=4 * rows * lanes * span,
            transcendentals=rows * span,
            bytes_accessed=cache.size * 2 + rows * lanes * 6,
        ),
        out_shape=[
            jax.ShapeDtypeStruct((rows, lanes), jnp.float32),
            jax.ShapeDtypeStruct((rows, 1), jnp.float32),
            jax.ShapeDtypeStruct((rows, 1), jnp.float32),
        ],
    )(valid_count.reshape(1), q_diag, cache)


def tail_kernel(score_scale, lens_ref, q_ref, cache_ref, acc_ref, top_ref, sum_ref):
    number = pl.program_id(0)
    keys = cache_ref[:, 0, :]
    values = cache_ref[:, 1, :]
    scores = (
        lax.dot_general(q_ref[...], keys, (((1,), (1,)), ((), ())), preferred_element_type=jnp.float32)
        * score_scale
    )
    places = lax.broadcasted_iota(jnp.int32, scores.shape, 1)
    scores = jnp.where(places < lens_ref[number], scores, masked_value)
    top = jnp.max(scores, axis=1, keepdims=True)
    weights = jnp.exp(scores - top)
    top_ref[...] = top
    sum_ref[...] = jnp.sum(weights, axis=1, keepdims=True)
    acc_ref[...] = jnp.dot(weights.astype(jnp.bfloat16), values, preferred_element_type=jnp.float32)


def tail_attention(q_diag, cache, lens, score_scale):
    conts, rows, lanes = q_diag.shape
    cap = cache.shape[1]
    spec = pltpu.PrefetchScalarGridSpec(
        num_scalar_prefetch=1,
        grid=(conts,),
        in_specs=[
            pl.BlockSpec((None, rows, lanes), lambda number, lens: (number, 0, 0)),
            pl.BlockSpec((None, cap, 2, lanes), lambda number, lens: (number, 0, 0, 0)),
        ],
        out_specs=[
            pl.BlockSpec((None, rows, lanes), lambda number, lens: (number, 0, 0)),
            pl.BlockSpec((None, rows, 1), lambda number, lens: (number, 0, 0)),
            pl.BlockSpec((None, rows, 1), lambda number, lens: (number, 0, 0)),
        ],
    )
    return pl.pallas_call(
        functools.partial(tail_kernel, score_scale),
        grid_spec=spec,
        cost_estimate=pl.CostEstimate(
            flops=4 * conts * rows * lanes * cap,
            transcendentals=conts * rows * cap,
            bytes_accessed=cache.size * 2 + conts * rows * lanes * 6,
        ),
        out_shape=[
            jax.ShapeDtypeStruct((conts, rows, lanes), jnp.float32),
            jax.ShapeDtypeStruct((conts, rows, 1), jnp.float32),
            jax.ShapeDtypeStruct((conts, rows, 1), jnp.float32),
        ],
    )(lens, q_diag, cache)


def per_device(
    new_qkv,
    prompt_cache,
    tail_cache,
    residual,
    w_out,
    mlp_gain,
    w_gate,
    w_up,
    w_down,
    final_gain,
    score_weight,
    slot_part,
    prompt_len,
    tail_len,
):
    req_count = lax.axis_size("req")
    req_index = lax.axis_index("req")
    mlp_index = lax.axis_index("mlp")
    rows_here = new_qkv.shape[0]
    width_here = new_qkv.shape[2]
    heads_here = width_here // HD
    conts_here = rows_here // 2
    width = w_out.shape[1]
    score_scale = 1.0 / math.sqrt(HD)
    own_prompt = req_index // 2
    tail_here = lax.dynamic_slice_in_dim(tail_len, req_index * conts_here, conts_here)
    plen_here = lax.dynamic_index_in_dim(prompt_len, own_prompt, 0, keepdims=False)
    position = plen_here + tail_here[:, None] + jnp.arange(2, dtype=jnp.int32)[None, :]
    block = new_qkv.reshape(conts_here, 2, 3, heads_here, HD)
    query = rotary(block[:, :, 0].astype(jnp.float32), position).astype(jnp.bfloat16)
    key_new = rotary(block[:, :, 1].astype(jnp.float32), position).astype(jnp.bfloat16)
    value_new = block[:, :, 2]
    mlp_count = lax.axis_size("mlp")
    weights_cat = w_gate
    rings = [[(m, (m + shift) % mlp_count) for m in range(mlp_count)] for shift in range(1, mlp_count)]
    weights_all = jnp.stack([weights_cat] + [lax.ppermute(weights_cat, "mlp", ring) for ring in rings])
    down_w = jnp.stack([w_down] + [lax.ppermute(w_down, "mlp", ring) for ring in rings])
    up_w = jnp.stack([w_up] + [lax.ppermute(w_up, "mlp", ring) for ring in rings])
    gathered = lax.all_gather(query.reshape(rows_here, width_here), "req", axis=0, tiled=True)
    eye = jnp.eye(heads_here, dtype=jnp.bfloat16)
    tail_diag = jnp.einsum("cthd,hg->chtgd", query, eye).reshape(
        conts_here, heads_here * 2, width_here
    )
    tail_acc, tail_top, tail_sum = tail_attention(tail_diag, tail_cache, tail_here, score_scale)
    gathered, tail_acc, tail_top, tail_sum, weights_all = lax.optimization_barrier(
        (gathered, tail_acc, tail_top, tail_sum, weights_all)
    )
    slot_ids = jnp.arange(req_count, dtype=jnp.int32)
    slot_of = jnp.sum(
        jnp.where(slot_part[None, :] == slot_ids[:, None], slot_ids[None, :], 0), axis=1
    )
    held_part = lax.dynamic_index_in_dim(slot_part, req_index, 0, keepdims=False)
    owned_prompt = held_part // 2
    held_half = held_part % 2
    span = prompt_cache.shape[1]
    owned_rows = 2 * rows_here
    q_owned = lax.dynamic_slice_in_dim(gathered, owned_prompt * owned_rows, owned_rows, 0).reshape(
        owned_rows, heads_here, HD
    )
    owned_len = lax.dynamic_index_in_dim(prompt_len, owned_prompt, 0, keepdims=False)
    valid_count = jnp.clip(owned_len - held_half * span, 0, span)
    q_diag = jnp.einsum("rhd,hg->hrgd", q_owned, eye).reshape(heads_here * owned_rows, width_here)
    prompt_acc, prompt_top, prompt_sum = prompt_attention(q_diag, prompt_cache, valid_count, score_scale)
    prompt_acc = prompt_acc.reshape(heads_here, owned_rows, heads_here, HD)
    owner_numer = jnp.stack([prompt_acc[h, :, h, :] for h in range(heads_here)], axis=1)
    top_f = jnp.transpose(prompt_top.reshape(heads_here, owned_rows))
    top_b = top_f.astype(jnp.bfloat16).astype(jnp.float32)
    rebase = jnp.where(top_f > 0.5 * masked_value, jnp.exp(top_f - top_b), 0.0)
    owner_total = jnp.transpose(prompt_sum.reshape(heads_here, owned_rows)) * rebase
    owner_numer = owner_numer * rebase[:, :, None]
    packed = jnp.concatenate(
        [owner_numer.reshape(owned_rows, width_here), owner_total, top_b], axis=1
    ).astype(jnp.bfloat16)
    outgoing = lax.dynamic_update_slice_in_dim(
        jnp.zeros((req_count, rows_here, packed.shape[1]), jnp.bfloat16),
        packed.reshape(2, rows_here, packed.shape[1]),
        2 * owned_prompt,
        0,
    )
    incoming = lax.all_to_all(outgoing, "req", split_axis=0, concat_axis=0, tiled=True)
    slot_first = lax.dynamic_index_in_dim(slot_of, 2 * own_prompt, 0, keepdims=False)
    slot_second = lax.dynamic_index_in_dim(slot_of, 2 * own_prompt + 1, 0, keepdims=False)

    def part_of(slot):
        piece = lax.dynamic_index_in_dim(incoming, slot, 0, keepdims=False).astype(jnp.float32)
        numer = piece[:, :width_here].reshape(rows_here, heads_here, HD)
        total = piece[:, width_here : width_here + heads_here]
        top = piece[:, width_here + heads_here :]
        return numer, total, top

    numer_first, total_first, max_first = part_of(slot_first)
    numer_second, total_second, max_second = part_of(slot_second)

    tail_acc = tail_acc.reshape(conts_here, heads_here, 2, heads_here, HD)
    cache_numer = jnp.stack([tail_acc[:, h, :, h, :] for h in range(heads_here)], axis=2)
    cache_top = tail_top.reshape(conts_here, heads_here, 2)
    cache_sum = tail_sum.reshape(conts_here, heads_here, 2)
    s_new = (
        jnp.einsum("cthd,cuhd->chtu", query, key_new, preferred_element_type=jnp.float32)
        * score_scale
    )
    causal = jnp.arange(2)[None, :] <= jnp.arange(2)[:, None]
    s_new = jnp.where(causal[None, None, :, :], s_new, masked_value)
    tail_max = jnp.maximum(cache_top, jnp.max(s_new, -1))
    cache_scale = jnp.exp(cache_top - tail_max)
    w_new = jnp.exp(s_new - tail_max[..., None])
    numer_tail = cache_numer * jnp.transpose(cache_scale, (0, 2, 1))[..., None]
    numer_tail = numer_tail + jnp.einsum(
        "chtu,cuhd->cthd", w_new.astype(jnp.bfloat16), value_new, preferred_element_type=jnp.float32
    )
    numer_tail = numer_tail.reshape(rows_here, heads_here, HD)
    total_tail = jnp.transpose(cache_sum * cache_scale + jnp.sum(w_new, -1), (0, 2, 1)).reshape(
        rows_here, heads_here
    )
    max_tail = jnp.transpose(tail_max, (0, 2, 1)).reshape(rows_here, heads_here)
    row_max = jnp.maximum(jnp.maximum(max_first, max_second), max_tail)
    scale_first = jnp.exp(max_first - row_max)
    scale_second = jnp.exp(max_second - row_max)
    scale_tail = jnp.exp(max_tail - row_max)
    row_total = total_first * scale_first + total_second * scale_second + total_tail * scale_tail
    row_numer = (
        numer_first * scale_first[..., None]
        + numer_second * scale_second[..., None]
        + numer_tail * scale_tail[..., None]
    )
    attn = (row_numer / row_total[:, :, None]).astype(jnp.bfloat16).reshape(rows_here, width_here)
    partial = jnp.dot(attn, w_out, preferred_element_type=jnp.float32)
    col_start = mlp_index * width_here
    own_cols = lax.dynamic_slice_in_dim(partial, col_start, width_here, 1)
    partial = lax.dynamic_update_slice_in_dim(
        partial, own_cols + residual.astype(jnp.float32), col_start, 1
    )
    share = rows_here // mlp_count
    state_share = lax.dynamic_slice_in_dim(partial, mlp_index * share, share, 0)
    for shift in range(1, mlp_count):
        target = (mlp_index + shift) % mlp_count
        state_share = state_share + lax.ppermute(
            lax.dynamic_slice_in_dim(partial, target * share, share, 0),
            "mlp",
            [(m, (m + shift) % mlp_count) for m in range(mlp_count)],
        )
    mean_square = jnp.mean(state_share * state_share, axis=1, keepdims=True)
    normed_share = (state_share * lax.rsqrt(mean_square + norm_eps) * mlp_gain).astype(jnp.bfloat16)
    piece = lax.all_to_all(
        jnp.broadcast_to(normed_share[None], (req_count,) + normed_share.shape),
        "req",
        split_axis=0,
        concat_axis=0,
        tiled=True,
    ).reshape(req_count * share, width)
    hidden_here = w_gate.shape[1]
    gate_w = weights_all[:, :, :hidden_here]
    gate = jnp.einsum("rk,mkj->rmj", piece, gate_w, preferred_element_type=jnp.float32)
    upper = jnp.einsum("rk,mkj->rmj", piece, up_w, preferred_element_type=jnp.float32)
    hidden_all = (jax.nn.silu(gate) * upper).astype(jnp.bfloat16)
    down_sum = jnp.einsum("rmj,mjf->rf", hidden_all, down_w, preferred_element_type=jnp.float32)
    row_sums = jnp.sum(
        lax.all_to_all(
            down_sum.astype(jnp.bfloat16).reshape(req_count, share, width),
            "req",
            split_axis=0,
            concat_axis=0,
            tiled=True,
        ).astype(jnp.float32),
        axis=0,
    )
    final_share = state_share + row_sums
    final_square = jnp.mean(final_share * final_share, axis=1)
    final_dot = jnp.sum(final_share * final_gain * score_weight, axis=1)
    score_share = final_dot * lax.rsqrt(final_square + norm_eps)
    payload = jnp.concatenate(
        [
            final_share.reshape(share, mlp_count, width_here),
            jnp.broadcast_to(score_share[:, None, None], (share, mlp_count, 1)),
        ],
        axis=2,
    )
    arrived = lax.dynamic_update_slice_in_dim(
        jnp.zeros((rows_here, width_here + 1), jnp.float32),
        lax.dynamic_index_in_dim(payload, mlp_index, 1, keepdims=False),
        mlp_index * share,
        0,
    )
    for shift in range(1, mlp_count):
        target = (mlp_index + shift) % mlp_count
        source = (mlp_index + mlp_count - shift) % mlp_count
        got = lax.ppermute(
            lax.dynamic_index_in_dim(payload, target, 1, keepdims=False),
            "mlp",
            [(m, (m + shift) % mlp_count) for m in range(mlp_count)],
        )
        arrived = lax.dynamic_update_slice_in_dim(arrived, got, source * share, 0)
    out_rows = arrived[:, :width_here].astype(jnp.bfloat16)
    scores = arrived[:, width_here]
    return (out_rows, scores)


def solution(mesh):
    in_specs = (
        P("req", None, "mlp"),
        P("req", None, None, "mlp"),
        P("req", None, None, "mlp"),
        P("req", "mlp"),
        P("mlp", None),
        P(),
        P(None, ("req", "mlp")),
        P(None, ("req", "mlp")),
        P(("req", "mlp"), None),
        P(),
        P(),
        P(),
        P(),
        P(),
    )
    out_specs = (P("req", "mlp"), P("req"))
    return jax.shard_map(
        per_device, mesh=mesh, in_specs=in_specs, out_specs=out_specs, check_vma=False
    )
```
